256 devices in a mesh: lat: 32 (over z, x), lon: 2 (over core), ens: 4 (over y).
Axes of the slice: x: 4, y: 4, z: 8, core: 2. Of those that a mesh axis runs over, the one named last changes fastest.
Arguments:
- fields: bfloat16 [1024, 256, 256], P(('ens', 'lat'), 'lon'), parts along dimension 0, may hold values from -6 to 6
- lon_taps: float32 [256, 4, 9], replicated, may hold values from -2 to 2
- lat_taps: bfloat16 [256, 4, 6], P('lat'), may hold values from -2.5 to 2.5
- cycle_taps: bfloat16 [4, 8, 256], replicated, may hold values from -0.375 to 0.375
- band_start: int32 [256], P('lat'), may hold values from -4 to 254, as said below
- band_width: int32 [256], P('lat'), may hold values from 4 to 6, as said below
- mixing: bfloat16 [4, 256, 256], replicated, may hold values from -0.1875 to 0.1875
Outputs:
- layer_out: bfloat16 [1024, 256, 256], P(('ens', 'lat'), 'lon'), parts along dimension 0
The draws below stay inside these ranges and needn't reach their ends.
There are 4 independent parts, one for each index of `ens`. The reference program is written for one: setup_inputs(seed, part) draws one part's arguments, and reference() takes and returns one part's arrays. A program takes and returns all parts, laid end to end along the dimension named above; an argument that names none is the same for every part. Nothing has to cross between parts.
Inputs may be any that keep to these rules, and one draw needn't show every extreme that they name: band_start[i] = i - 4 + s with s in 0 .. 3; s = 0 where i % 8 == 0 and s = 3 where i % 8 == 7. band_width[i] = 6 where i % 8 is 0 or 7.
All inputs are finite; a program needn't handle non-finite values.
Results may differ from the reference program's by a relative error of at most 0.0052.
Values may be sent and summed in bfloat16 or wider, within the bound.
A program may use at most 64 MiB of HBM per device.

```python
import jax
import jax.numpy as jnp
from jax import lax

CHAN = 256
BASIS = 4
REACH = 4
BAND = 6
HALO = 4
LAT_DEV = 8
POLAR = 4
NLAT = 256
NLON = 256


def draw_band_start(key, part):
    rows_all = jnp.arange(NLAT, dtype=jnp.int32)
    top_shift = 2 * HALO - BAND + 1
    shift = jax.random.randint(jax.random.fold_in(key, 11), (NLAT,), 0, top_shift + 1, dtype=jnp.int32)
    inside = rows_all % LAT_DEV
    shift = jnp.where(inside == 0, 0, jnp.where(inside == LAT_DEV - 1, top_shift, shift))
    return (rows_all - HALO + shift).astype(jnp.int32)


def draw_band_width(key, part):
    rows_all = jnp.arange(NLAT, dtype=jnp.int32)
    widths = jax.random.randint(jax.random.fold_in(key, 23), (NLAT,), BAND - 2, BAND + 1, dtype=jnp.int32)
    inside = rows_all % LAT_DEV
    edge = (inside == 0) | (inside == LAT_DEV - 1)
    return jnp.where(edge, BAND, widths).astype(jnp.int32)


def steps_of(stream_key, shape, pieces, smallest, high):
    factor_of, own = 1.0, jax.random.fold_in(stream_key, 6)
    for dim, blocks in pieces:
        steps = jnp.exp(jax.random.uniform(jax.random.fold_in(own, dim), (blocks,), jnp.float32, smallest / len(pieces), high / len(pieces)))
        factor_of = factor_of * jnp.repeat(steps, shape[dim] // blocks).reshape([-1 if axis == dim else 1 for axis in range(len(shape))])
    return factor_of


def gaussian(rng, shape, scale, bound, split=(), kind=jnp.bfloat16):
    values = jax.random.normal(rng, shape, jnp.float32) * scale
    if len(split) > 0:
        values = steps_of(rng, shape, split, -0.22, 0.18) * values
    return jnp.clip(values, min=-bound, max=bound).astype(kind)


def setup_inputs(seed: int = 0, part: int = 0) -> dict:
    splits = jax.random.split(jax.random.key(seed), 8)
    part_keys = jax.random.split(jax.random.fold_in(splits[7], part), 8)
    fields = gaussian(part_keys[0], (NLAT, NLON, CHAN), 1.0, 6.0, ((0, 32), (1, 2)))
    lon_taps = gaussian(splits[1], (NLAT, BASIS, 2 * REACH + 1), 0.35, 2.0, (), jnp.float32)
    lat_taps = gaussian(splits[2], (NLAT, BASIS, BAND), 0.45, 2.5, ((0, 32),))
    cycle_taps = gaussian(splits[3], (BASIS, 2 * POLAR, NLON), NLON ** -0.5, 0.375)
    band_start = draw_band_start(jax.random.fold_in(splits[7], 71), part)
    band_width = draw_band_width(jax.random.fold_in(splits[7], 71), part)
    mixing = gaussian(splits[6], (BASIS, CHAN, CHAN), (BASIS * CHAN) ** -0.5, 0.1875)
    return {"fields": fields, "lon_taps": lon_taps, "lat_taps": lat_taps, "cycle_taps": cycle_taps, "band_start": band_start, "band_width": band_width, "mixing": mixing}


def short_filter(fields, taps_now):
    total = jnp.zeros(fields.shape, jnp.float32)
    for offset in range(2 * REACH + 1):
        moved = jnp.roll(fields, REACH - offset, axis=1).astype(jnp.float32)
        total = total + taps_now[:, offset][:, None, None] * moved
    return total


def reference(fields, lon_taps, lat_taps, cycle_taps, band_start, band_width, mixing):
    columns = jnp.arange(NLON, dtype=jnp.int32)
    lag_table = (columns[:, None] - columns[None, :]) % NLON
    polar_ids = [p for p in range(POLAR)] + [NLAT - POLAR + p for p in range(POLAR)]

    def per_basis(mixed, inputs):
        lon_now, lat_now, cycle_now, mix_now = inputs
        filtered = short_filter(fields, lon_now).astype(jnp.bfloat16)
        for index in range(2 * POLAR):
            row_id = polar_ids[index]
            circ = cycle_now[index][lag_table]
            cycle_row = jnp.dot(circ, fields[row_id], preferred_element_type=jnp.float32)
            filtered = filtered.at[row_id].set(cycle_row.astype(jnp.bfloat16))
        hidden = jnp.zeros(fields.shape, jnp.float32)
        for step_t in range(BAND):
            source = band_start + step_t
            usable = (step_t < band_width) & (source >= 0) & (source < NLAT)
            picked = filtered[jnp.clip(source, 0, NLAT - 1).astype(jnp.int32)].astype(jnp.float32)
            weight = jnp.where(usable, lat_now[:, step_t].astype(jnp.float32), jnp.zeros((NLAT,), jnp.float32))
            hidden = hidden + weight[:, None, None] * picked
        hidden = hidden.astype(jnp.bfloat16)
        mixed = mixed + jnp.dot(hidden.reshape(NLAT * NLON, CHAN), mix_now, preferred_element_type=jnp.float32)
        return mixed, None

    start_sum = jnp.zeros((NLAT * NLON, CHAN), jnp.float32)
    inputs = (jnp.moveaxis(lon_taps, 1, 0), jnp.moveaxis(lat_taps, 1, 0), cycle_taps, mixing)
    mixed, unused = lax.scan(per_basis, start_sum, inputs)
    result = fields.astype(jnp.float32) + mixed.reshape(NLAT, NLON, CHAN)
    return result.astype(jnp.bfloat16)
```

```python
import jax
import jax.numpy as jnp
from jax import lax
from jax.sharding import PartitionSpec as P

HALO = 4


def extended_2(cells, sides, width, closed):
    for axis, dim in sides:
        count = lax.axis_size(axis)
        ends = count if closed else count - 1
        head = lax.slice_in_dim(cells, 0, width, axis=dim)
        tail = lax.slice_in_dim(cells, cells.shape[dim] - width, cells.shape[dim], axis=dim)
        cells = jnp.concatenate(
            [
                lax.ppermute(tail, axis, [(i, (i + 1) % count) for i in range(ends)]),
                cells,
                lax.ppermute(head, axis, [((i + 1) % count, i) for i in range(ends)]),
            ],
            axis=dim,
        )
    return cells


def toeplitz(coef, base, out_count, in_count, cycle_len):
    lead = coef.shape[:-1]
    window_len = out_count + in_count - 1
    tripled = jnp.concatenate([coef, coef, coef], axis=-1)
    begin = (base - in_count + 1) % cycle_len
    window = lax.dynamic_slice_in_dim(tripled, begin, window_len, len(lead))
    flipped = jnp.flip(window, axis=-1)
    rolled = jnp.roll(flipped, -(out_count - 1), axis=-1)
    tiled = jnp.tile(rolled, (1,) * len(lead) + (out_count,))
    cut = tiled[..., : out_count * (window_len - 1)]
    shaped = cut.reshape(lead + (out_count, window_len - 1))
    return shaped[..., :in_count]


def cycle_fold(coef, col_start, col_count, cycle_len, block_in):
    width_in = block_in.shape[1]
    circ = toeplitz(coef, col_start, col_count, width_in, cycle_len)
    return jnp.einsum("kpjm,pmc->kpjc", circ, block_in, preferred_element_type=jnp.float32)


def shards(fields, lon_taps, lat_taps, cycle_taps, band_start, band_width, mixing):
    row_count, col_count, chan_count = fields.shape
    basis_count = lon_taps.shape[1]
    reach_cells = (lon_taps.shape[2] - 1) // 2
    band_len = lat_taps.shape[2]
    polar_rows = row_count // 2
    lat_count = lax.axis_size("lat")
    lon_count = lax.axis_size("lon")
    cycle_len = lon_count * col_count
    lat_pos = lax.axis_index("lat")
    lon_pos = lax.axis_index("lon")
    ext_rows = row_count + 2 * HALO
    padded = extended_2(fields, (("lon", 1),), reach_cells, True)
    ext = extended_2(padded, (("lat", 0),), HALO, False)
    taps_padded = jnp.pad(lon_taps, ((HALO, HALO), (0, 0), (0, 0)))
    taps_here = lax.dynamic_slice_in_dim(taps_padded, lat_pos * row_count, ext_rows, 0)
    accum = jnp.zeros((basis_count, ext_rows, col_count, chan_count), jnp.float32)
    for offset in range(2 * reach_cells + 1):
        tap_now = jnp.transpose(taps_here[:, :, offset])
        accum = accum + tap_now[:, :, None, None] * ext[
            None, :, offset : offset + col_count, :
        ].astype(jnp.float32)
    filtered = accum.astype(jnp.bfloat16)
    at_top = lat_pos == 0
    at_bottom = lat_pos == lat_count - 1
    slot_start = jnp.where(at_top, 0, row_count - polar_rows).astype(jnp.int32)
    slot_rows = lax.dynamic_slice_in_dim(fields, slot_start, polar_rows, 0)
    col_start = lon_pos * col_count
    coef_start = jnp.where(at_top, 0, polar_rows).astype(jnp.int32)
    coef = lax.dynamic_slice_in_dim(cycle_taps, coef_start, polar_rows, 1)
    polar_sum = cycle_fold(
        coef, col_start, col_count, cycle_len, lax.all_gather(slot_rows, "lon", axis=1, tiled=True)
    )
    polar_z = polar_sum.astype(jnp.bfloat16)
    current = lax.dynamic_slice_in_dim(filtered, slot_start + HALO, polar_rows, 1)
    polar_here = jnp.where(at_top | at_bottom, polar_z, current)
    filtered = lax.dynamic_update_slice_in_dim(filtered, polar_here, slot_start + HALO, 1)
    base_row = lat_pos * row_count
    steps_band = jnp.arange(band_len, dtype=jnp.int32)
    target = band_start[:, None] - base_row + HALO + steps_band[None, :]
    usable = steps_band[None, :] < band_width[:, None]
    ext_ids = jnp.arange(ext_rows, dtype=jnp.int32)
    select = ((target[:, :, None] == ext_ids[None, None, :]) & usable[:, :, None]).astype(
        jnp.float32
    )
    band_matrix = jnp.einsum("lkt,lte->kle", lat_taps.astype(jnp.float32), select).astype(
        jnp.bfloat16
    )
    hidden = jnp.einsum(
        "kle,kejc->kljc", band_matrix, filtered, preferred_element_type=jnp.float32
    ).astype(jnp.bfloat16)
    mixed = jnp.einsum("kljc,kco->ljo", hidden, mixing, preferred_element_type=jnp.float32)
    return (fields.astype(jnp.float32) + mixed).astype(jnp.bfloat16)


def solution(mesh):
    in_specs = (
        P(("ens", "lat"), "lon", None),
        P(),
        P("lat", None, None),
        P(),
        P("lat"),
        P("lat"),
        P(),
    )
    out_specs = P(("ens", "lat"), "lon", None)
    return jax.shard_map(shards, mesh=mesh, in_specs=in_specs, out_specs=out_specs, check_vma=False)
```

```python
import jax
import jax.numpy as jnp
from jax import lax
from jax.sharding import PartitionSpec as P

HALO = 4


def extended_2(cells, sides, width, closed):
    for axis, dim in sides:
        count = lax.axis_size(axis)
        ends = count if closed else count - 1
        head = lax.slice_in_dim(cells, 0, width, axis=dim)
        tail = lax.slice_in_dim(cells, cells.shape[dim] - width, cells.shape[dim], axis=dim)
        cells = jnp.concatenate(
            [
                lax.ppermute(tail, axis, [(i, (i + 1) % count) for i in range(ends)]),
                cells,
                lax.ppermute(head, axis, [((i + 1) % count, i) for i in range(ends)]),
            ],
            axis=dim,
        )
    return cells


def toeplitz(coef, base, out_count, in_count, cycle_len):
    lead = coef.shape[:-1]
    window_len = out_count + in_count - 1
    tripled = jnp.concatenate([coef, coef, coef], axis=-1)
    begin = (base - in_count + 1) % cycle_len
    window = lax.dynamic_slice_in_dim(tripled, begin, window_len, len(lead))
    flipped = jnp.flip(window, axis=-1)
    rolled = jnp.roll(flipped, -(out_count - 1), axis=-1)
    tiled = jnp.tile(rolled, (1,) * len(lead) + (out_count,))
    cut = tiled[..., : out_count * (window_len - 1)]
    shaped = cut.reshape(lead + (out_count, window_len - 1))
    return shaped[..., :in_count]


def cycle_fold(coef, col_start, col_count, cycle_len, block_in):
    width_in = block_in.shape[1]
    circ = toeplitz(coef, col_start, col_count, width_in, cycle_len)
    return jnp.einsum("kpjm,pmc->kpjc", circ, block_in, preferred_element_type=jnp.float32)


def shards(fields, lon_taps, lat_taps, cycle_taps, band_start, band_width, mixing):
    row_count, col_count, chan_count = fields.shape
    basis_count = lon_taps.shape[1]
    reach_cells = (lon_taps.shape[2] - 1) // 2
    band_len = lat_taps.shape[2]
    polar_rows = row_count // 2
    lat_count = lax.axis_size("lat")
    lon_count = lax.axis_size("lon")
    cycle_len = lon_count * col_count
    lat_pos = lax.axis_index("lat")
    lon_pos = lax.axis_index("lon")
    ext_rows = row_count + 2 * HALO
    padded = extended_2(fields, (("lon", 1),), reach_cells, True)
    ext = extended_2(padded, (("lat", 0),), HALO, False)
    taps_padded = jnp.pad(lon_taps, ((HALO, HALO), (0, 0), (0, 0)))
    taps_here = lax.dynamic_slice_in_dim(taps_padded, lat_pos * row_count, ext_rows, 0)
    accum = jnp.zeros((basis_count, ext_rows, col_count, chan_count), jnp.float32)
    for offset in range(2 * reach_cells + 1):
        tap_now = jnp.transpose(taps_here[:, :, offset])
        accum = accum + tap_now[:, :, None, None] * ext[
            None, :, offset : offset + col_count, :
        ].astype(jnp.float32)
    filtered = accum.astype(jnp.bfloat16)
    at_top = lat_pos == 0
    at_bottom = lat_pos == lat_count - 1
    slot_start = jnp.where(at_top, 0, row_count - polar_rows).astype(jnp.int32)
    slot_rows = lax.dynamic_slice_in_dim(fields, slot_start, polar_rows, 0)
    col_start = lon_pos * col_count
    coef_start = jnp.where(at_top, 0, polar_rows).astype(jnp.int32)
    coef = lax.dynamic_slice_in_dim(cycle_taps, coef_start, polar_rows, 1)
    other_rows = lax.ppermute(slot_rows, "lon", [(i, (i + 1) % lon_count) for i in range(lon_count)])
    pair = [slot_rows, other_rows] if lon_count == 2 else None
    gathered = jnp.where(lon_pos == 0, jnp.concatenate(pair, axis=1), jnp.concatenate(pair[::-1], axis=1))
    polar_sum = cycle_fold(coef, col_start, col_count, cycle_len, gathered)
    polar_z = polar_sum.astype(jnp.bfloat16)
    current = lax.dynamic_slice_in_dim(filtered, slot_start + HALO, polar_rows, 1)
    polar_here = jnp.where(at_top | at_bottom, polar_z, current)
    filtered = lax.dynamic_update_slice_in_dim(filtered, polar_here, slot_start + HALO, 1)
    base_row = lat_pos * row_count
    steps_band = jnp.arange(band_len, dtype=jnp.int32)
    target = band_start[:, None] - base_row + HALO + steps_band[None, :]
    usable = steps_band[None, :] < band_width[:, None]
    ext_ids = jnp.arange(ext_rows, dtype=jnp.int32)
    select = ((target[:, :, None] == ext_ids[None, None, :]) & usable[:, :, None]).astype(
        jnp.float32
    )
    band_matrix = jnp.einsum("lkt,lte->kle", lat_taps.astype(jnp.float32), select).astype(
        jnp.bfloat16
    )
    hidden = jnp.einsum(
        "kle,kejc->kljc", band_matrix, filtered, preferred_element_type=jnp.float32
    ).astype(jnp.bfloat16)
    mixed = jnp.einsum("kljc,kco->ljo", hidden, mixing, preferred_element_type=jnp.float32)
    return (fields.astype(jnp.float32) + mixed).astype(jnp.bfloat16)


def solution(mesh):
    in_specs = (
        P(("ens", "lat"), "lon", None),
        P(),
        P("lat", None, None),
        P(),
        P("lat"),
        P("lat"),
        P(),
    )
    out_specs = P(("ens", "lat"), "lon", None)
    return jax.shard_map(shards, mesh=mesh, in_specs=in_specs, out_specs=out_specs, check_vma=False)
```

```python
import functools

import jax
import jax.numpy as jnp
from jax import lax
from jax.experimental import pallas as pl
from jax.experimental.pallas import tpu as pltpu
from jax.sharding import PartitionSpec as P

HALO = 4
LANES = 128


def extended_2(cells, sides, width, closed):
    for axis, dim in sides:
        count = lax.axis_size(axis)
        ends = count if closed else count - 1
        head = lax.slice_in_dim(cells, 0, width, axis=dim)
        tail = lax.slice_in_dim(cells, cells.shape[dim] - width, cells.shape[dim], axis=dim)
        cells = jnp.concatenate(
            [
                lax.ppermute(tail, axis, [(i, (i + 1) % count) for i in range(ends)]),
                cells,
                lax.ppermute(head, axis, [((i + 1) % count, i) for i in range(ends)]),
            ],
            axis=dim,
        )
    return cells


def banded(vec, rows, upper):
    rolled = pltpu.roll(jnp.broadcast_to(vec, (rows, LANES)), 0, 1, stride=1, stride_axis=0)
    row = lax.broadcasted_iota(jnp.int32, (rows, LANES), 0)
    col = lax.broadcasted_iota(jnp.int32, (rows, LANES), 1)
    keep = col >= row if upper else col < row
    return jnp.where(keep, rolled, 0.0)


def conv_kernel(basis, ext_rows, out_rows, band_len,
                ctl_ref, idx_ref, wgt_ref, ext_ref, tap_ref, fields_ref, mix_ref,
                polar_ref, crev_ref, out_ref, f_ref, h_ref):
    cols = out_ref.shape[1]
    chans = out_ref.shape[2]
    polar_count = polar_ref.shape[0]

    def filter_row(r, carry):
        x = ext_ref[r]
        parts = []
        for k in range(basis):
            for half in range(2):
                u = tap_ref[k, half, pl.ds(r, 1), :]
                left = banded(u, cols, True)
                right = banded(u, cols, False)
                parts.append(jnp.concatenate([left, right], axis=1).astype(jnp.bfloat16))
        tall = jnp.concatenate(parts, axis=0)
        y = jnp.dot(tall, x, preferred_element_type=jnp.float32)
        for k in range(basis):
            lo = 2 * k * cols
            v = y[lo : lo + cols] + y[lo + cols : lo + 2 * cols]
            f_ref[k, r] = v.astype(jnp.bfloat16).astype(jnp.float32)
        return carry

    lax.fori_loop(0, ext_rows, filter_row, 0)

    @pl.when(ctl_ref[0] == 1)
    def _polar():
        slot = ctl_ref[1]
        for k in range(basis):
            for p in range(polar_count):
                va = crev_ref[k, p, pl.ds(0, 1), :]
                vb = crev_ref[k, p, pl.ds(1, 1), :]
                ra_u, ra_w = banded(va, cols, True), banded(va, cols, False)
                rb_u, rb_w = banded(vb, cols, True), banded(vb, cols, False)
                circ = jnp.concatenate([ra_u + rb_w, rb_u + ra_w], axis=1).astype(jnp.bfloat16)
                y = jnp.dot(circ, polar_ref[p], preferred_element_type=jnp.float32)
                f_ref[k, slot + p] = y.astype(jnp.bfloat16).astype(jnp.float32)

    for k in range(basis):
        def band_row(i, carry):
            acc = jnp.zeros((cols, chans), jnp.float32)
            for t in range(band_len):
                r = idx_ref[i * band_len + t]
                w = wgt_ref[(k * out_rows + i) * band_len + t]
                acc = acc + w * f_ref[k, r]
            h_ref[i, :, k * chans : (k + 1) * chans] = acc.astype(jnp.bfloat16)
            return carry

        lax.fori_loop(0, out_rows, band_row, 0)

    def mix_row(i, carry):
        mixed = jnp.dot(h_ref[i], mix_ref[...], preferred_element_type=jnp.float32)
        out_ref[i] = (fields_ref[i].astype(jnp.float32) + mixed).astype(out_ref.dtype)
        return carry

    lax.fori_loop(0, out_rows, mix_row, 0)


def shards(fields, lon_taps, lat_taps, cycle_taps, band_start, band_width, mixing):
    row_count, col_count, chan_count = fields.shape
    basis_count = lon_taps.shape[1]
    taps_count = lon_taps.shape[2]
    reach_cells = (taps_count - 1) // 2
    band_len = lat_taps.shape[2]
    polar_rows = row_count // 2
    lat_count = lax.axis_size("lat")
    lon_count = lax.axis_size("lon")
    cycle_len = lon_count * col_count
    lat_pos = lax.axis_index("lat")
    lon_pos = lax.axis_index("lon")
    ext_rows = row_count + 2 * HALO
    total_rows = lat_count * row_count
    padded = extended_2(fields, (("lon", 1),), reach_cells, True)
    ext = extended_2(padded, (("lat", 0),), HALO, False)
    ext = jnp.pad(ext, ((0, 0), (0, 2 * col_count - ext.shape[1]), (0, 0)))
    taps_padded = jnp.pad(lon_taps, ((HALO, HALO), (0, 0), (0, 0)))
    taps_here = lax.dynamic_slice_in_dim(taps_padded, lat_pos * row_count, ext_rows, 0)
    taps_here = jnp.transpose(taps_here, (1, 0, 2))
    taps_hi = taps_here.astype(jnp.bfloat16).astype(jnp.float32)
    taps_lo = (taps_here - taps_hi).astype(jnp.bfloat16).astype(jnp.float32)
    tap_vec = jnp.stack([taps_hi, taps_lo], axis=1)
    tap_vec = jnp.pad(tap_vec, ((0, 0), (0, 0), (0, 0), (0, LANES - taps_count)))

    at_top = lat_pos == 0
    at_bottom = lat_pos == lat_count - 1
    slot_start = jnp.where(at_top, 0, row_count - polar_rows).astype(jnp.int32)
    slot_rows = lax.dynamic_slice_in_dim(fields, slot_start, polar_rows, 0)
    other_rows = lax.ppermute(slot_rows, "lon", [(i, (i + 1) % lon_count) for i in range(lon_count)])
    pair = [slot_rows, other_rows]
    gathered = jnp.where(lon_pos == 0, jnp.concatenate(pair, axis=1), jnp.concatenate(pair[::-1], axis=1))
    col_start = lon_pos * col_count
    coef_start = jnp.where(at_top, 0, polar_rows).astype(jnp.int32)
    coef = lax.dynamic_slice_in_dim(cycle_taps, coef_start, polar_rows, 1).astype(jnp.float32)
    rev = jnp.roll(jnp.flip(coef, axis=-1), 1, axis=-1)
    rev = jnp.roll(rev, col_start, axis=-1)
    crev = rev.reshape(basis_count, polar_rows, cycle_len // LANES, LANES)

    base_row = lat_pos * row_count
    steps_band = jnp.arange(band_len, dtype=jnp.int32)
    source = band_start[:, None] + steps_band[None, :]
    usable = (steps_band[None, :] < band_width[:, None]) & (source >= 0) & (source < total_rows)
    idx = jnp.clip(source - base_row + HALO, 0, ext_rows - 1).reshape(-1)
    wgt = jnp.where(usable[:, None, :], lat_taps.astype(jnp.float32), 0.0)
    wgt = jnp.transpose(wgt, (1, 0, 2)).reshape(-1)
    is_polar = (at_top | at_bottom).astype(jnp.int32)
    ctl = jnp.stack([is_polar, slot_start + HALO]).astype(jnp.int32)
    mix_flat = mixing.reshape(basis_count * chan_count, chan_count)

    smem = pl.BlockSpec(memory_space=pltpu.SMEM)
    vmem = pl.BlockSpec(memory_space=pltpu.VMEM)
    kernel = functools.partial(conv_kernel, basis_count, ext_rows, row_count, band_len)
    return pl.pallas_call(
        kernel,
        out_shape=jax.ShapeDtypeStruct(fields.shape, fields.dtype),
        in_specs=[smem, smem, smem] + [vmem] * 6,
        out_specs=vmem,
        scratch_shapes=[
            pltpu.VMEM((basis_count, ext_rows, col_count, chan_count), jnp.float32),
            pltpu.VMEM((row_count, col_count, basis_count * chan_count), jnp.bfloat16),
        ],
        compiler_params=pltpu.CompilerParams(vmem_limit_bytes=48 * 1024 * 1024),
    )(ctl, idx, wgt, ext, tap_vec, fields, mix_flat, gathered, crev)


def solution(mesh):
    in_specs = (
        P(("ens", "lat"), "lon", None),
        P(),
        P("lat", None, None),
        P(),
        P("lat"),
        P("lat"),
        P(),
    )
    out_specs = P(("ens", "lat"), "lon", None)
    return jax.shard_map(shards, mesh=mesh, in_specs=in_specs, out_specs=out_specs, check_vma=False)
```

```python
import functools

import jax
import jax.numpy as jnp
from jax import lax
from jax.experimental import pallas as pl
from jax.experimental.pallas import tpu as pltpu
from jax.sharding import PartitionSpec as P

HALO = 4
LANES = 128


def extended_2(cells, sides, width, closed):
    for axis, dim in sides:
        count = lax.axis_size(axis)
        ends = count if closed else count - 1
        head = lax.slice_in_dim(cells, 0, width, axis=dim)
        tail = lax.slice_in_dim(cells, cells.shape[dim] - width, cells.shape[dim], axis=dim)
        cells = jnp.concatenate(
            [
                lax.ppermute(tail, axis, [(i, (i + 1) % count) for i in range(ends)]),
                cells,
                lax.ppermute(head, axis, [((i + 1) % count, i) for i in range(ends)]),
            ],
            axis=dim,
        )
    return cells


def banded(vec, rows, upper):
    rolled = pltpu.roll(jnp.broadcast_to(vec, (rows, LANES)), 0, 1, stride=1, stride_axis=0)
    row = lax.broadcasted_iota(jnp.int32, (rows, LANES), 0)
    col = lax.broadcasted_iota(jnp.int32, (rows, LANES), 1)
    keep = col >= row if upper else col < row
    return jnp.where(keep, rolled, 0.0)


def conv_kernel(basis, ext_rows, out_rows, band_len,
                ctl_ref, idx_ref, wgt_ref, ext_ref, tap_ref, fields_ref, mix_ref,
                polar_ref, crev_ref, out_ref, f_ref, h_ref):
    cols = out_ref.shape[1]
    chans = out_ref.shape[2]
    polar_count = polar_ref.shape[0]

    def filter_row(r, carry):
        x = ext_ref[r]
        parts = []
        for k in range(basis):
            u = tap_ref[k, pl.ds(r, 1), :]
            u_hi = u.astype(jnp.bfloat16).astype(jnp.float32)
            for piece in (u_hi, u - u_hi):
                left = banded(piece, cols, True)
                right = banded(piece, cols, False)
                parts.append(jnp.concatenate([left, right], axis=1).astype(jnp.bfloat16))
        tall = jnp.concatenate(parts, axis=0)
        y = jnp.dot(tall, x, preferred_element_type=jnp.float32)
        for k in range(basis):
            lo = 2 * k * cols
            v = y[lo : lo + cols] + y[lo + cols : lo + 2 * cols]
            f_ref[k, r] = v.astype(jnp.bfloat16).astype(jnp.float32)
        return carry

    lax.fori_loop(0, ext_rows, filter_row, 0)

    @pl.when(ctl_ref[0] == 1)
    def _polar():
        slot = ctl_ref[1]
        for k in range(basis):
            for p in range(polar_count):
                va = crev_ref[k, p, pl.ds(0, 1), :]
                vb = crev_ref[k, p, pl.ds(1, 1), :]
                ra_u, ra_w = banded(va, cols, True), banded(va, cols, False)
                rb_u, rb_w = banded(vb, cols, True), banded(vb, cols, False)
                circ = jnp.concatenate([ra_u + rb_w, rb_u + ra_w], axis=1).astype(jnp.bfloat16)
                y = jnp.dot(circ, polar_ref[p], preferred_element_type=jnp.float32)
                f_ref[k, slot + p] = y.astype(jnp.bfloat16).astype(jnp.float32)

    for k in range(basis):
        def band_row(i, carry):
            acc = jnp.zeros((cols, chans), jnp.float32)
            for t in range(band_len):
                r = idx_ref[i * band_len + t]
                w = wgt_ref[(k * out_rows + i) * band_len + t]
                acc = acc + w * f_ref[k, r]
            h_ref[i, :, k * chans : (k + 1) * chans] = acc.astype(jnp.bfloat16)
            return carry

        lax.fori_loop(0, out_rows, band_row, 0)

    def mix_row(i, carry):
        mixed = jnp.dot(h_ref[i], mix_ref[...], preferred_element_type=jnp.float32)
        out_ref[i] = (fields_ref[i].astype(jnp.float32) + mixed).astype(out_ref.dtype)
        return carry

    lax.fori_loop(0, out_rows, mix_row, 0)


def shards(fields, lon_taps, lat_taps, cycle_taps, band_start, band_width, mixing):
    row_count, col_count, chan_count = fields.shape
    basis_count = lon_taps.shape[1]
    taps_count = lon_taps.shape[2]
    reach_cells = (taps_count - 1) // 2
    band_len = lat_taps.shape[2]
    polar_rows = row_count // 2
    lat_count = lax.axis_size("lat")
    lon_count = lax.axis_size("lon")
    cycle_len = lon_count * col_count
    lat_pos = lax.axis_index("lat")
    lon_pos = lax.axis_index("lon")
    ext_rows = row_count + 2 * HALO
    total_rows = lat_count * row_count
    padded = extended_2(fields, (("lon", 1),), reach_cells, True)
    edges = jnp.concatenate(
        [fields[:, col_count - reach_cells :], fields[:, :reach_cells]], axis=1
    )
    up = [(i, i + 1) for i in range(lat_count - 1)]
    down = [(i + 1, i) for i in range(lat_count - 1)]
    top_mid = lax.ppermute(fields[row_count - HALO :], "lat", up)
    bot_mid = lax.ppermute(fields[:HALO], "lat", down)

    def diag(pairs):
        return [
            (a * lon_count + o, b * lon_count + (o + 1) % lon_count)
            for a, b in pairs
            for o in range(lon_count)
        ]

    top_edge = lax.ppermute(edges[row_count - HALO :], ("lat", "lon"), diag(up))
    bot_edge = lax.ppermute(edges[:HALO], ("lat", "lon"), diag(down))

    def halo_rows(mid, edge):
        return jnp.concatenate([edge[:, :reach_cells], mid, edge[:, reach_cells:]], axis=1)

    ext = jnp.concatenate(
        [halo_rows(top_mid, top_edge), padded, halo_rows(bot_mid, bot_edge)], axis=0
    )
    ext = jnp.pad(ext, ((0, 0), (0, 2 * col_count - ext.shape[1]), (0, 0)))
    taps_padded = jnp.pad(lon_taps, ((HALO, HALO), (0, 0), (0, 0)))
    taps_here = lax.dynamic_slice_in_dim(taps_padded, lat_pos * row_count, ext_rows, 0)
    taps_here = jnp.transpose(taps_here, (1, 0, 2))
    tap_vec = jnp.pad(taps_here, ((0, 0), (0, 0), (0, LANES - taps_count)))

    at_top = lat_pos == 0
    at_bottom = lat_pos == lat_count - 1
    slot_start = jnp.where(at_top, 0, row_count - polar_rows).astype(jnp.int32)
    slot_rows = lax.dynamic_slice_in_dim(fields, slot_start, polar_rows, 0)
    other_rows = lax.ppermute(slot_rows, "lon", [(i, (i + 1) % lon_count) for i in range(lon_count)])
    pair = [slot_rows, other_rows]
    gathered = jnp.where(lon_pos == 0, jnp.concatenate(pair, axis=1), jnp.concatenate(pair[::-1], axis=1))
    col_start = lon_pos * col_count
    coef_start = jnp.where(at_top, 0, polar_rows).astype(jnp.int32)
    coef = lax.dynamic_slice_in_dim(cycle_taps, coef_start, polar_rows, 1).astype(jnp.float32)
    rev = jnp.roll(jnp.flip(coef, axis=-1), 1, axis=-1)
    rev = jnp.roll(rev, col_start, axis=-1)
    crev = rev.reshape(basis_count, polar_rows, cycle_len // LANES, LANES)

    base_row = lat_pos * row_count
    steps_band = jnp.arange(band_len, dtype=jnp.int32)
    source = band_start[:, None] + steps_band[None, :]
    usable = (steps_band[None, :] < band_width[:, None]) & (source >= 0) & (source < total_rows)
    idx = jnp.clip(source - base_row + HALO, 0, ext_rows - 1).reshape(-1)
    wgt = jnp.where(usable[:, None, :], lat_taps.astype(jnp.float32), 0.0)
    wgt = jnp.transpose(wgt, (1, 0, 2)).reshape(-1)
    is_polar = (at_top | at_bottom).astype(jnp.int32)
    ctl = jnp.stack([is_polar, slot_start + HALO]).astype(jnp.int32)
    mix_flat = mixing.reshape(basis_count * chan_count, chan_count)

    smem = pl.BlockSpec(memory_space=pltpu.SMEM)
    vmem = pl.BlockSpec(memory_space=pltpu.VMEM)
    kernel = functools.partial(conv_kernel, basis_count, ext_rows, row_count, band_len)
    return pl.pallas_call(
        kernel,
        out_shape=jax.ShapeDtypeStruct(fields.shape, fields.dtype),
        in_specs=[smem, smem, smem] + [vmem] * 6,
        out_specs=vmem,
        scratch_shapes=[
            pltpu.VMEM((basis_count, ext_rows, col_count, chan_count), jnp.float32),
            pltpu.VMEM((row_count, col_count, basis_count * chan_count), jnp.bfloat16),
        ],
        compiler_params=pltpu.CompilerParams(vmem_limit_bytes=48 * 1024 * 1024),
    )(ctl, idx, wgt, ext, tap_vec, fields, mix_flat, gathered, crev)


def solution(mesh):
    in_specs = (
        P(("ens", "lat"), "lon", None),
        P(),
        P("lat", None, None),
        P(),
        P("lat"),
        P("lat"),
        P(),
    )
    out_specs = P(("ens", "lat"), "lon", None)
    return jax.shard_map(shards, mesh=mesh, in_specs=in_specs, out_specs=out_specs, check_vma=False)
```

```python
import functools

import jax
import jax.numpy as jnp
from jax import lax
from jax.experimental import pallas as pl
from jax.experimental.pallas import tpu as pltpu
from jax.sharding import PartitionSpec as P

HALO = 4
LANES = 128
SENT_ROWS = 144


def banded(vec, rows, upper):
    rolled = pltpu.roll(jnp.broadcast_to(vec, (rows, LANES)), 0, 1, stride=1, stride_axis=0)
    row = lax.broadcasted_iota(jnp.int32, (rows, LANES), 0)
    col = lax.broadcasted_iota(jnp.int32, (rows, LANES), 1)
    keep = col >= row if upper else col < row
    return jnp.where(keep, rolled, 0.0)


def conv_kernel(basis, out_rows, band_len,
                idx_ref, wgt_ref, own_ref, tap_ref, fields_ref, mix_ref,
                polar_ref, crev_ref, out_ref,
                top_ref, bot_ref, f_ref, h_ref, send_sem, recv_sem):
    cols = out_ref.shape[1]
    chans = out_ref.shape[2]
    polar_count = polar_ref.shape[0]
    lat = lax.axis_index("lat")
    last = lax.axis_size("lat") - 1
    has_up = lat < last
    has_down = lat > 0

    pad_rows = top_ref.shape[1] - SENT_ROWS
    zeros = jnp.zeros((HALO, pad_rows, chans), top_ref.dtype)
    top_ref[:, pl.ds(SENT_ROWS, pad_rows), :] = zeros
    bot_ref[:, pl.ds(SENT_ROWS, pad_rows), :] = zeros

    barrier = pltpu.get_barrier_semaphore()

    @pl.when(has_up)
    def _():
        pl.semaphore_signal(barrier, 1, device_id={"lat": lat + 1},
                            device_id_type=pl.DeviceIdType.MESH)

    @pl.when(has_down)
    def _():
        pl.semaphore_signal(barrier, 1, device_id={"lat": lat - 1},
                            device_id_type=pl.DeviceIdType.MESH)

    pl.semaphore_wait(barrier, has_up.astype(jnp.int32) + has_down.astype(jnp.int32))

    up_copy = pltpu.make_async_remote_copy(
        src_ref=own_ref.at[pl.ds(out_rows - HALO, HALO), pl.ds(0, SENT_ROWS)],
        dst_ref=top_ref.at[:, pl.ds(0, SENT_ROWS)],
        send_sem=send_sem.at[0], recv_sem=recv_sem.at[0],
        device_id={"lat": jnp.minimum(lat + 1, last)}, device_id_type=pl.DeviceIdType.MESH)
    down_copy = pltpu.make_async_remote_copy(
        src_ref=own_ref.at[pl.ds(0, HALO), pl.ds(0, SENT_ROWS)],
        dst_ref=bot_ref.at[:, pl.ds(0, SENT_ROWS)],
        send_sem=send_sem.at[1], recv_sem=recv_sem.at[1],
        device_id={"lat": jnp.maximum(lat - 1, 0)}, device_id_type=pl.DeviceIdType.MESH)

    @pl.when(has_up)
    def _():
        up_copy.start()

    @pl.when(has_down)
    def _():
        down_copy.start()

    def filter_rows(src_ref, count, first):
        def filter_row(r, carry):
            x = src_ref[r]
            parts = []
            for k in range(basis):
                u = tap_ref[k, pl.ds(first + r, 1), :]
                u_hi = u.astype(jnp.bfloat16).astype(jnp.float32)
                for piece in (u_hi, u - u_hi):
                    left = banded(piece, cols, True)
                    right = banded(piece, cols, False)
                    parts.append(jnp.concatenate([left, right], axis=1).astype(jnp.bfloat16))
            tall = jnp.concatenate(parts, axis=0)
            y = jnp.dot(tall, x, preferred_element_type=jnp.float32)
            for k in range(basis):
                lo = 2 * k * cols
                v = y[lo : lo + cols] + y[lo + cols : lo + 2 * cols]
                f_ref[k, first + r] = v.astype(jnp.bfloat16).astype(jnp.float32)
            return carry

        lax.fori_loop(0, count, filter_row, 0)

    def zero_rows(first):
        f_ref[:, pl.ds(first, HALO)] = jnp.zeros((basis, HALO, cols, chans), jnp.float32)

    filter_rows(own_ref, out_rows, HALO)

    @pl.when((lat == 0) | (lat == last))
    def _polar():
        slot = HALO + jnp.minimum(lat, 1) * (out_rows - polar_count)
        for k in range(basis):
            for p in range(polar_count):
                va = crev_ref[k, p, pl.ds(0, 1), :]
                vb = crev_ref[k, p, pl.ds(1, 1), :]
                ra_u, ra_w = banded(va, cols, True), banded(va, cols, False)
                rb_u, rb_w = banded(vb, cols, True), banded(vb, cols, False)
                circ = jnp.concatenate([ra_u + rb_w, rb_u + ra_w], axis=1).astype(jnp.bfloat16)
                y = jnp.dot(circ, polar_ref[p], preferred_element_type=jnp.float32)
                f_ref[k, slot + p] = y.astype(jnp.bfloat16).astype(jnp.float32)

    @pl.when(has_up)
    def _():
        up_copy.wait_send()

    @pl.when(has_down)
    def _():
        down_copy.wait_send()

    @pl.when(has_down)
    def _():
        up_copy.wait_recv()
        filter_rows(top_ref, HALO, 0)

    @pl.when(lat == 0)
    def _():
        zero_rows(0)

    @pl.when(has_up)
    def _():
        down_copy.wait_recv()
        filter_rows(bot_ref, HALO, HALO + out_rows)

    @pl.when(lat == last)
    def _():
        zero_rows(HALO + out_rows)

    for k in range(basis):
        def band_row(i, carry):
            acc = jnp.zeros((cols, chans), jnp.float32)
            for t in range(band_len):
                r = idx_ref[i * band_len + t]
                w = wgt_ref[(k * out_rows + i) * band_len + t]
                acc = acc + w * f_ref[k, r]
            h_ref[i, :, k * chans : (k + 1) * chans] = acc.astype(jnp.bfloat16)
            return carry

        lax.fori_loop(0, out_rows, band_row, 0)

    def mix_row(i, carry):
        mixed = jnp.dot(h_ref[i], mix_ref[...], preferred_element_type=jnp.float32)
        out_ref[i] = (fields_ref[i].astype(jnp.float32) + mixed).astype(out_ref.dtype)
        return carry

    lax.fori_loop(0, out_rows, mix_row, 0)


def shards(fields, lon_taps, lat_taps, cycle_taps, band_start, band_width, mixing):
    row_count, col_count, chan_count = fields.shape
    basis_count = lon_taps.shape[1]
    taps_count = lon_taps.shape[2]
    reach_cells = (taps_count - 1) // 2
    band_len = lat_taps.shape[2]
    polar_rows = row_count // 2
    lat_count = lax.axis_size("lat")
    lon_count = lax.axis_size("lon")
    assert lon_count == 2
    cycle_len = lon_count * col_count
    lat_pos = lax.axis_index("lat")
    lon_pos = lax.axis_index("lon")
    ext_rows = row_count + 2 * HALO
    total_rows = lat_count * row_count

    at_top = lat_pos == 0
    at_bottom = lat_pos == lat_count - 1
    slot_start = jnp.where(at_top, 0, row_count - polar_rows).astype(jnp.int32)
    slot_rows = lax.dynamic_slice_in_dim(fields, slot_start, polar_rows, 0)
    edges = jnp.concatenate([fields[:, :reach_cells], fields[:, col_count - reach_cells :]], axis=1)
    payload = jnp.concatenate([edges.reshape(-1), slot_rows.reshape(-1)])
    got = lax.ppermute(payload, "lon", [(0, 1), (1, 0)])
    other_edges = got[: edges.size].reshape(edges.shape)
    other_rows = got[edges.size :].reshape(slot_rows.shape)
    pad_cols = 2 * col_count - col_count - 2 * reach_cells
    own = jnp.concatenate(
        [
            other_edges[:, reach_cells:],
            fields,
            other_edges[:, :reach_cells],
            jnp.zeros((row_count, pad_cols, chan_count), fields.dtype),
        ],
        axis=1,
    )
    pair = [slot_rows, other_rows]
    gathered = jnp.where(lon_pos == 0, jnp.concatenate(pair, axis=1), jnp.concatenate(pair[::-1], axis=1))

    taps_padded = jnp.pad(lon_taps, ((HALO, HALO), (0, 0), (0, 0)))
    taps_here = lax.dynamic_slice_in_dim(taps_padded, lat_pos * row_count, ext_rows, 0)
    taps_here = jnp.transpose(taps_here, (1, 0, 2))
    tap_vec = jnp.pad(taps_here, ((0, 0), (0, 0), (0, LANES - taps_count)))

    col_start = lon_pos * col_count
    coef_start = jnp.where(at_top, 0, polar_rows).astype(jnp.int32)
    coef = lax.dynamic_slice_in_dim(cycle_taps, coef_start, polar_rows, 1).astype(jnp.float32)
    rev = jnp.roll(jnp.flip(coef, axis=-1), 1, axis=-1)
    rev = jnp.roll(rev, col_start, axis=-1)
    crev = rev.reshape(basis_count, polar_rows, cycle_len // LANES, LANES)

    base_row = lat_pos * row_count
    steps_band = jnp.arange(band_len, dtype=jnp.int32)
    source = band_start[:, None] + steps_band[None, :]
    usable = (steps_band[None, :] < band_width[:, None]) & (source >= 0) & (source < total_rows)
    idx = jnp.clip(source - base_row + HALO, 0, ext_rows - 1).reshape(-1)
    wgt = jnp.where(usable[:, None, :], lat_taps.astype(jnp.float32), 0.0)
    wgt = jnp.transpose(wgt, (1, 0, 2)).reshape(-1)
    mix_flat = mixing.reshape(basis_count * chan_count, chan_count)

    smem = pl.BlockSpec(memory_space=pltpu.SMEM)
    vmem = pl.BlockSpec(memory_space=pltpu.VMEM)
    kernel = functools.partial(conv_kernel, basis_count, row_count, band_len)
    return pl.pallas_call(
        kernel,
        out_shape=jax.ShapeDtypeStruct(fields.shape, fields.dtype),
        in_specs=[smem, smem] + [vmem] * 6,
        out_specs=vmem,
        scratch_shapes=[
            pltpu.VMEM((HALO, 2 * col_count, chan_count), fields.dtype),
            pltpu.VMEM((HALO, 2 * col_count, chan_count), fields.dtype),
            pltpu.VMEM((basis_count, ext_rows, col_count, chan_count), jnp.float32),
            pltpu.VMEM((row_count, col_count, basis_count * chan_count), jnp.bfloat16),
            pltpu.SemaphoreType.DMA((2,)),
            pltpu.SemaphoreType.DMA((2,)),
        ],
        compiler_params=pltpu.CompilerParams(
            vmem_limit_bytes=48 * 1024 * 1024, collective_id=0, has_side_effects=True
        ),
    )(idx, wgt, own, tap_vec, fields, mix_flat, gathered, crev)


def solution(mesh):
    in_specs = (
        P(("ens", "lat"), "lon", None),
        P(),
        P("lat", None, None),
        P(),
        P("lat"),
        P("lat"),
        P(),
    )
    out_specs = P(("ens", "lat"), "lon", None)
    return jax.shard_map(shards, mesh=mesh, in_specs=in_specs, out_specs=out_specs, check_vma=False)
```

```python
import functools

import jax
import jax.numpy as jnp
from jax import lax
from jax.experimental import pallas as pl
from jax.experimental.pallas import tpu as pltpu
from jax.sharding import PartitionSpec as P

HALO = 4
LANES = 128
EDGE = 16
MESH = pl.DeviceIdType.MESH


def rolled(vec, rows):
    return pltpu.roll(jnp.broadcast_to(vec, (rows, LANES)), 0, 1, stride=1, stride_axis=0)


def conv_kernel(basis, out_rows, band_len, polar_count,
                idx_ref, wgt_ref, fields_ref, tap_ref, mix_ref, crev_ref, out_ref,
                top_c, bot_c, top_h, bot_h, own_h, polar_o, f_ref, h_ref, send_sem, recv_sem):
    cols = out_ref.shape[1]
    chans = out_ref.shape[2]
    lat = lax.axis_index("lat")
    lon = lax.axis_index("lon")
    last = lax.axis_size("lat") - 1
    has_up = lat < last
    has_down = lat > 0
    is_polar = (lat == 0) | (lat == last)
    slot = jnp.minimum(lat, 1) * (out_rows - polar_count)
    up = jnp.minimum(lat + 1, last)
    down = jnp.maximum(lat - 1, 0)
    side = 1 - lon

    barrier = pltpu.get_barrier_semaphore()

    def greet(where):
        pl.semaphore_signal(barrier, 1, device_id=where, device_id_type=MESH)

    greet({"lat": lat, "lon": side})

    @pl.when(has_up)
    def _():
        greet({"lat": up, "lon": lon})
        greet({"lat": up, "lon": side})

    @pl.when(has_down)
    def _():
        greet({"lat": down, "lon": lon})
        greet({"lat": down, "lon": side})

    pl.semaphore_wait(barrier, 1 + 2 * (has_up.astype(jnp.int32) + has_down.astype(jnp.int32)))

    def copy(n, src, dst, where):
        return pltpu.make_async_remote_copy(
            src_ref=src, dst_ref=dst, send_sem=send_sem.at[n], recv_sem=recv_sem.at[n],
            device_id=where, device_id_type=MESH)

    lo_rows = pl.ds(0, HALO)
    hi_rows = pl.ds(out_rows - HALO, HALO)
    first_cols = pl.ds(0, EDGE)
    last_cols = pl.ds(cols - EDGE, EDGE)
    c_up = copy(0, fields_ref.at[hi_rows], top_c, {"lat": up, "lon": lon})
    c_dn = copy(1, fields_ref.at[lo_rows], bot_c, {"lat": down, "lon": lon})
    h_up = [
        copy(2, fields_ref.at[hi_rows, first_cols], top_h.at[:, first_cols], {"lat": up, "lon": side}),
        copy(3, fields_ref.at[hi_rows, last_cols], top_h.at[:, last_cols], {"lat": up, "lon": side}),
    ]
    h_dn = [
        copy(4, fields_ref.at[lo_rows, first_cols], bot_h.at[:, first_cols], {"lat": down, "lon": side}),
        copy(5, fields_ref.at[lo_rows, last_cols], bot_h.at[:, last_cols], {"lat": down, "lon": side}),
    ]
    h_side = [
        copy(6, fields_ref.at[:, first_cols], own_h.at[:, first_cols], {"lat": lat, "lon": side}),
        copy(7, fields_ref.at[:, last_cols], own_h.at[:, last_cols], {"lat": lat, "lon": side}),
    ]
    pol = copy(8, fields_ref.at[pl.ds(slot, polar_count)], polar_o, {"lat": lat, "lon": side})

    for c in h_side:
        c.start()

    @pl.when(has_up)
    def _():
        c_up.start()
        for c in h_up:
            c.start()

    @pl.when(has_down)
    def _():
        c_dn.start()
        for c in h_dn:
            c.start()

    @pl.when(is_polar)
    def _():
        pol.start()

    row_id = lax.broadcasted_iota(jnp.int32, (cols, LANES), 0)
    col_id = lax.broadcasted_iota(jnp.int32, (cols, LANES), 1)
    near = jnp.abs(col_id - row_id) <= HALO
    edge_row = lax.broadcasted_iota(jnp.int32, (cols, chans), 0)
    edge_keep = (edge_row < HALO) | (edge_row >= cols - HALO)

    def filter_rows(c_ref, e_ref, count, first):
        def filter_row(r, carry):
            x = jnp.concatenate(
                [c_ref[r], jnp.where(edge_keep, e_ref[r], jnp.zeros_like(e_ref[r]))], axis=0
            )
            parts = []
            for k in range(basis):
                u = tap_ref[k, pl.ds(first + r, 1), :]
                u_hi = u.astype(jnp.bfloat16).astype(jnp.float32)
                for piece in (u_hi, u - u_hi):
                    w = rolled(piece, cols)
                    band = jnp.where(near, w, 0.0)
                    wrap = jnp.where(near, 0.0, w)
                    parts.append(jnp.concatenate([band, wrap], axis=1).astype(jnp.bfloat16))
            tall = jnp.concatenate(parts, axis=0)
            y = jnp.dot(tall, x, preferred_element_type=jnp.float32)
            for k in range(basis):
                lo = 2 * k * cols
                v = y[lo : lo + cols] + y[lo + cols : lo + 2 * cols]
                f_ref[k, first + r] = v.astype(jnp.bfloat16).astype(jnp.float32)
            return carry

        lax.fori_loop(0, count, filter_row, 0)

    def zero_rows(first):
        f_ref[:, pl.ds(first, HALO)] = jnp.zeros((basis, HALO, cols, chans), jnp.float32)

    for c in h_side:
        c.wait_recv()
    filter_rows(fields_ref, own_h, out_rows, HALO)

    @pl.when(is_polar)
    def _polar():
        pol.wait_recv()
        upper = col_id >= row_id
        for k in range(basis):
            for p in range(polar_count):
                ra = rolled(crev_ref[k, p, pl.ds(0, 1), :], cols)
                rb = rolled(crev_ref[k, p, pl.ds(1, 1), :], cols)
                circ = jnp.concatenate(
                    [jnp.where(upper, ra, rb), jnp.where(upper, rb, ra)], axis=1
                ).astype(jnp.bfloat16)
                g = jnp.concatenate([fields_ref[slot + p], polar_o[p]], axis=0)
                y = jnp.dot(circ, g, preferred_element_type=jnp.float32)
                f_ref[k, HALO + slot + p] = y.astype(jnp.bfloat16).astype(jnp.float32)

    @pl.when(has_down)
    def _():
        c_up.wait_recv()
        for c in h_up:
            c.wait_recv()
        filter_rows(top_c, top_h, HALO, 0)

    @pl.when(lat == 0)
    def _():
        zero_rows(0)

    @pl.when(has_up)
    def _():
        c_dn.wait_recv()
        for c in h_dn:
            c.wait_recv()
        filter_rows(bot_c, bot_h, HALO, HALO + out_rows)

    @pl.when(lat == last)
    def _():
        zero_rows(HALO + out_rows)

    for k in range(basis):
        def band_row(i, carry):
            acc = jnp.zeros((cols, chans), jnp.float32)
            for t in range(band_len):
                r = idx_ref[i * band_len + t]
                w = wgt_ref[(k * out_rows + i) * band_len + t]
                acc = acc + w * f_ref[k, r]
            h_ref[i, :, k * chans : (k + 1) * chans] = acc.astype(jnp.bfloat16)
            return carry

        lax.fori_loop(0, out_rows, band_row, 0)

    def mix_row(i, carry):
        mixed = jnp.dot(h_ref[i], mix_ref[...], preferred_element_type=jnp.float32)
        out_ref[i] = (fields_ref[i].astype(jnp.float32) + mixed).astype(out_ref.dtype)
        return carry

    lax.fori_loop(0, out_rows, mix_row, 0)

    for c in h_side:
        c.wait_send()

    @pl.when(has_up)
    def _():
        c_up.wait_send()
        for c in h_up:
            c.wait_send()

    @pl.when(has_down)
    def _():
        c_dn.wait_send()
        for c in h_dn:
            c.wait_send()

    @pl.when(is_polar)
    def _():
        pol.wait_send()


def shards(fields, lon_taps, lat_taps, cycle_taps, band_start, band_width, mixing):
    row_count, col_count, chan_count = fields.shape
    basis_count = lon_taps.shape[1]
    taps_count = lon_taps.shape[2]
    reach_cells = (taps_count - 1) // 2
    band_len = lat_taps.shape[2]
    polar_rows = row_count // 2
    lat_count = lax.axis_size("lat")
    lon_count = lax.axis_size("lon")
    assert lon_count == 2 and reach_cells == HALO
    cycle_len = lon_count * col_count
    lat_pos = lax.axis_index("lat")
    ext_rows = row_count + 2 * HALO
    total_rows = lat_count * row_count

    taps_padded = jnp.pad(lon_taps, ((HALO, HALO), (0, 0), (0, 0)))
    taps_here = lax.dynamic_slice_in_dim(taps_padded, lat_pos * row_count, ext_rows, 0)
    taps_here = jnp.transpose(taps_here, (1, 0, 2))
    tap_vec = jnp.concatenate(
        [
            taps_here[..., reach_cells:],
            jnp.zeros(taps_here.shape[:2] + (LANES - taps_count,), jnp.float32),
            taps_here[..., :reach_cells],
        ],
        axis=-1,
    )

    at_top = lat_pos == 0
    coef_start = jnp.where(at_top, 0, polar_rows).astype(jnp.int32)
    coef = lax.dynamic_slice_in_dim(cycle_taps, coef_start, polar_rows, 1).astype(jnp.float32)
    rev = jnp.roll(jnp.flip(coef, axis=-1), 1, axis=-1)
    crev = rev.reshape(basis_count, polar_rows, cycle_len // LANES, LANES)

    base_row = lat_pos * row_count
    steps_band = jnp.arange(band_len, dtype=jnp.int32)
    source = band_start[:, None] + steps_band[None, :]
    usable = (steps_band[None, :] < band_width[:, None]) & (source >= 0) & (source < total_rows)
    idx = jnp.clip(source - base_row + HALO, 0, ext_rows - 1).reshape(-1)
    wgt = jnp.where(usable[:, None, :], lat_taps.astype(jnp.float32), 0.0)
    wgt = jnp.transpose(wgt, (1, 0, 2)).reshape(-1)
    mix_flat = mixing.reshape(basis_count * chan_count, chan_count)

    smem = pl.BlockSpec(memory_space=pltpu.SMEM)
    vmem = pl.BlockSpec(memory_space=pltpu.VMEM)
    kernel = functools.partial(conv_kernel, basis_count, row_count, band_len, polar_rows)
    halo_block = pltpu.VMEM((HALO, col_count, chan_count), fields.dtype)
    return pl.pallas_call(
        kernel,
        out_shape=jax.ShapeDtypeStruct(fields.shape, fields.dtype),
        in_specs=[smem, smem] + [vmem] * 4,
        out_specs=vmem,
        scratch_shapes=[
            halo_block,
            halo_block,
            halo_block,
            halo_block,
            pltpu.VMEM(fields.shape, fields.dtype),
            pltpu.VMEM((polar_rows, col_count, chan_count), fields.dtype),
            pltpu.VMEM((basis_count, ext_rows, col_count, chan_count), jnp.float32),
            pltpu.VMEM((row_count, col_count, basis_count * chan_count), jnp.bfloat16),
            pltpu.SemaphoreType.DMA((9,)),
            pltpu.SemaphoreType.DMA((9,)),
        ],
        compiler_params=pltpu.CompilerParams(
            vmem_limit_bytes=48 * 1024 * 1024, collective_id=0, has_side_effects=True
        ),
    )(idx, wgt, fields, tap_vec, mix_flat, crev)


def solution(mesh):
    in_specs = (
        P(("ens", "lat"), "lon", None),
        P(),
        P("lat", None, None),
        P(),
        P("lat"),
        P("lat"),
        P(),
    )
    out_specs = P(("ens", "lat"), "lon", None)
    return jax.shard_map(shards, mesh=mesh, in_specs=in_specs, out_specs=out_specs, check_vma=False)
```

```python
import functools

import jax
import jax.numpy as jnp
from jax import lax
from jax.experimental import pallas as pl
from jax.experimental.pallas import tpu as pltpu
from jax.sharding import PartitionSpec as P

HALO = 4
LANES = 128
EDGE = 16
MESH = pl.DeviceIdType.MESH


def rolled(vec, rows):
    return pltpu.roll(jnp.broadcast_to(vec, (rows, LANES)), 0, 1, stride=1, stride_axis=0)


def conv_kernel(basis, out_rows, band_len, polar_count, total_rows,
                start_hbm, width_hbm, lat_hbm, lon_hbm, cyc_hbm, fields_hbm, mix_hbm, out_ref,
                start_s, width_s, lat_v, tap_v, cyc_v, fields_ref, mix_ref,
                top_c, bot_c, top_h, bot_h, own_h, polar_o, f_ref, h_ref, send_sem, recv_sem, load_sem):
    cols = out_ref.shape[1]
    chans = out_ref.shape[2]
    ext_rows = out_rows + 2 * HALO
    lat = lax.axis_index("lat")
    tap_first = jnp.clip(lat * out_rows - HALO, 0, total_rows - ext_rows)
    loads = [
        pltpu.make_async_copy(fields_hbm, fields_ref, load_sem.at[0]),
        pltpu.make_async_copy(lon_hbm.at[pl.ds(tap_first, ext_rows)], tap_v, load_sem.at[1]),
        pltpu.make_async_copy(start_hbm, start_s, load_sem.at[2]),
        pltpu.make_async_copy(width_hbm, width_s, load_sem.at[3]),
        pltpu.make_async_copy(lat_hbm, lat_v, load_sem.at[4]),
        pltpu.make_async_copy(cyc_hbm, cyc_v, load_sem.at[5]),
        pltpu.make_async_copy(mix_hbm, mix_ref, load_sem.at[6]),
    ]
    for c in loads:
        c.start()
    lon = lax.axis_index("lon")
    last = lax.axis_size("lat") - 1
    has_up = lat < last
    has_down = lat > 0
    is_polar = (lat == 0) | (lat == last)
    slot = jnp.minimum(lat, 1) * (out_rows - polar_count)
    up = jnp.minimum(lat + 1, last)
    down = jnp.maximum(lat - 1, 0)
    side = 1 - lon

    barrier = pltpu.get_barrier_semaphore()

    def greet(where):
        pl.semaphore_signal(barrier, 1, device_id=where, device_id_type=MESH)

    greet({"lat": lat, "lon": side})

    @pl.when(has_up)
    def _():
        greet({"lat": up, "lon": lon})
        greet({"lat": up, "lon": side})

    @pl.when(has_down)
    def _():
        greet({"lat": down, "lon": lon})
        greet({"lat": down, "lon": side})

    pl.semaphore_wait(barrier, 1 + 2 * (has_up.astype(jnp.int32) + has_down.astype(jnp.int32)))

    def copy(n, src, dst, where):
        return pltpu.make_async_remote_copy(
            src_ref=src, dst_ref=dst, send_sem=send_sem.at[n], recv_sem=recv_sem.at[n],
            device_id=where, device_id_type=MESH)

    lo_rows = pl.ds(0, HALO)
    hi_rows = pl.ds(out_rows - HALO, HALO)
    first_cols = pl.ds(0, EDGE)
    last_cols = pl.ds(cols - EDGE, EDGE)
    c_up = copy(0, fields_ref.at[hi_rows], top_c, {"lat": up, "lon": lon})
    c_dn = copy(1, fields_ref.at[lo_rows], bot_c, {"lat": down, "lon": lon})
    h_up = [
        copy(2, fields_ref.at[hi_rows, first_cols], top_h.at[:, first_cols], {"lat": up, "lon": side}),
        copy(3, fields_ref.at[hi_rows, last_cols], top_h.at[:, last_cols], {"lat": up, "lon": side}),
    ]
    h_dn = [
        copy(4, fields_ref.at[lo_rows, first_cols], bot_h.at[:, first_cols], {"lat": down, "lon": side}),
        copy(5, fields_ref.at[lo_rows, last_cols], bot_h.at[:, last_cols], {"lat": down, "lon": side}),
    ]
    h_side = [
        copy(6, fields_ref.at[:, first_cols], own_h.at[:, first_cols], {"lat": lat, "lon": side}),
        copy(7, fields_ref.at[:, last_cols], own_h.at[:, last_cols], {"lat": lat, "lon": side}),
    ]
    pol = copy(8, fields_ref.at[pl.ds(slot, polar_count)], polar_o, {"lat": lat, "lon": side})

    for c in loads:
        c.wait()

    for c in h_side:
        c.start()

    @pl.when(has_up)
    def _():
        c_up.start()
        for c in h_up:
            c.start()

    @pl.when(has_down)
    def _():
        c_dn.start()
        for c in h_dn:
            c.start()

    @pl.when(is_polar)
    def _():
        pol.start()

    row_id = lax.broadcasted_iota(jnp.int32, (cols, LANES), 0)
    col_id = lax.broadcasted_iota(jnp.int32, (cols, LANES), 1)
    near = jnp.abs(col_id - row_id) <= HALO
    edge_row = lax.broadcasted_iota(jnp.int32, (cols, chans), 0)
    edge_keep = (edge_row < HALO) | (edge_row >= cols - HALO)

    def filter_rows(c_ref, e_ref, count, first):
        def filter_row(r, carry):
            x = jnp.concatenate(
                [c_ref[r], jnp.where(edge_keep, e_ref[r], jnp.zeros_like(e_ref[r]))], axis=0
            )
            parts = []
            local = jnp.clip(lat * out_rows - HALO + first + r - tap_first, 0, ext_rows - 1)
            t9 = tap_v[local]
            t128 = jnp.concatenate(
                [t9, jnp.zeros((basis, LANES - t9.shape[1]), jnp.float32)], axis=1
            )
            centred = pltpu.roll(t128, LANES - HALO, 1)
            for k in range(basis):
                u = centred[k : k + 1]
                u_hi = u.astype(jnp.bfloat16).astype(jnp.float32)
                for piece in (u_hi, u - u_hi):
                    w = rolled(piece, cols)
                    band = jnp.where(near, w, 0.0)
                    wrap = jnp.where(near, 0.0, w)
                    parts.append(jnp.concatenate([band, wrap], axis=1).astype(jnp.bfloat16))
            tall = jnp.concatenate(parts, axis=0)
            y = jnp.dot(tall, x, preferred_element_type=jnp.float32)
            for k in range(basis):
                lo = 2 * k * cols
                v = y[lo : lo + cols] + y[lo + cols : lo + 2 * cols]
                f_ref[k, first + r] = v.astype(jnp.bfloat16).astype(jnp.float32)
            return carry

        lax.fori_loop(0, count, filter_row, 0)

    def zero_rows(first):
        f_ref[:, pl.ds(first, HALO)] = jnp.zeros((basis, HALO, cols, chans), jnp.float32)

    for c in h_side:
        c.wait_recv()
    filter_rows(fields_ref, own_h, out_rows, HALO)

    def polar_rows(pole):
        pol.wait_recv()
        upper = col_id >= row_id
        for k in range(basis):
            for p in range(polar_count):
                a = cyc_v[k, pl.ds(pole * polar_count + p, 1), :].astype(jnp.float32)
                ra = rolled(a[:, :LANES], cols)
                rb = rolled(a[:, LANES:], cols)
                circ_t = jnp.concatenate(
                    [jnp.where(upper, ra, rb), jnp.where(upper, rb, ra)], axis=0
                )
                circ = jnp.transpose(circ_t).astype(jnp.bfloat16)
                g = jnp.concatenate([fields_ref[slot + p], polar_o[p]], axis=0)
                y = jnp.dot(circ, g, preferred_element_type=jnp.float32)
                f_ref[k, HALO + slot + p] = y.astype(jnp.bfloat16).astype(jnp.float32)

    @pl.when(lat == 0)
    def _():
        polar_rows(0)

    @pl.when(lat == last)
    def _():
        polar_rows(1)

    @pl.when(has_down)
    def _():
        c_up.wait_recv()
        for c in h_up:
            c.wait_recv()
        filter_rows(top_c, top_h, HALO, 0)

    @pl.when(lat == 0)
    def _():
        zero_rows(0)

    @pl.when(has_up)
    def _():
        c_dn.wait_recv()
        for c in h_dn:
            c.wait_recv()
        filter_rows(bot_c, bot_h, HALO, HALO + out_rows)

    @pl.when(lat == last)
    def _():
        zero_rows(HALO + out_rows)

    base_row = lat * out_rows

    def band_row(i, carry):
        lw = lat_v[i].astype(jnp.float32)
        begin = start_s[i]
        width = width_s[i]
        rows = []
        for t in range(band_len):
            source = begin + t
            ok = (t < width) & (source >= 0) & (source < total_rows)
            rows.append((ok, jnp.clip(source - base_row + HALO, 0, ext_rows - 1)))
        for k in range(basis):
            acc = jnp.zeros((cols, chans), jnp.float32)
            for t, (ok, r) in enumerate(rows):
                w = jnp.where(ok, lw[k : k + 1, t : t + 1], 0.0)
                acc = acc + w * f_ref[k, r]
            h_ref[i, :, k * chans : (k + 1) * chans] = acc.astype(jnp.bfloat16)
        return carry

    lax.fori_loop(0, out_rows, band_row, 0)

    def mix_row(i, carry):
        mixed = jnp.dot(h_ref[i], mix_ref[...], preferred_element_type=jnp.float32)
        out_ref[i] = (fields_ref[i].astype(jnp.float32) + mixed).astype(out_ref.dtype)
        return carry

    lax.fori_loop(0, out_rows, mix_row, 0)

    for c in h_side:
        c.wait_send()

    @pl.when(has_up)
    def _():
        c_up.wait_send()
        for c in h_up:
            c.wait_send()

    @pl.when(has_down)
    def _():
        c_dn.wait_send()
        for c in h_dn:
            c.wait_send()

    @pl.when(is_polar)
    def _():
        pol.wait_send()


def shards(fields, lon_taps, lat_taps, cycle_taps, band_start, band_width, mixing):
    row_count, col_count, chan_count = fields.shape
    basis_count = lon_taps.shape[1]
    taps_count = lon_taps.shape[2]
    reach_cells = (taps_count - 1) // 2
    band_len = lat_taps.shape[2]
    polar_rows = row_count // 2
    lat_count = lax.axis_size("lat")
    lon_count = lax.axis_size("lon")
    assert lon_count == 2 and reach_cells == HALO
    cycle_len = lon_count * col_count
    lat_pos = lax.axis_index("lat")
    ext_rows = row_count + 2 * HALO
    total_rows = lat_count * row_count

    mix_flat = mixing.reshape(basis_count * chan_count, chan_count)

    hbm = pl.BlockSpec(memory_space=pl.ANY)
    kernel = functools.partial(
        conv_kernel, basis_count, row_count, band_len, polar_rows, total_rows
    )
    halo_block = pltpu.VMEM((HALO, col_count, chan_count), fields.dtype)
    return pl.pallas_call(
        kernel,
        out_shape=jax.ShapeDtypeStruct(fields.shape, fields.dtype),
        in_specs=[hbm] * 7,
        out_specs=pl.BlockSpec(memory_space=pltpu.VMEM),
        scratch_shapes=[
            pltpu.SMEM(band_start.shape, band_start.dtype),
            pltpu.SMEM(band_width.shape, band_width.dtype),
            pltpu.VMEM(lat_taps.shape, lat_taps.dtype),
            pltpu.VMEM((ext_rows,) + lon_taps.shape[1:], lon_taps.dtype),
            pltpu.VMEM(cycle_taps.shape, cycle_taps.dtype),
            pltpu.VMEM(fields.shape, fields.dtype),
            pltpu.VMEM(mix_flat.shape, mix_flat.dtype),
            halo_block,
            halo_block,
            halo_block,
            halo_block,
            pltpu.VMEM(fields.shape, fields.dtype),
            pltpu.VMEM((polar_rows, col_count, chan_count), fields.dtype),
            pltpu.VMEM((basis_count, ext_rows, col_count, chan_count), jnp.float32),
            pltpu.VMEM((row_count, col_count, basis_count * chan_count), jnp.bfloat16),
            pltpu.SemaphoreType.DMA((9,)),
            pltpu.SemaphoreType.DMA((9,)),
            pltpu.SemaphoreType.DMA((7,)),
        ],
        compiler_params=pltpu.CompilerParams(
            vmem_limit_bytes=67043328, collective_id=0, has_side_effects=True
        ),
    )(band_start, band_width, lat_taps, lon_taps, cycle_taps, fields, mix_flat)


def solution(mesh):
    in_specs = (
        P(("ens", "lat"), "lon", None),
        P(),
        P("lat", None, None),
        P(),
        P("lat"),
        P("lat"),
        P(),
    )
    out_specs = P(("ens", "lat"), "lon", None)
    return jax.shard_map(shards, mesh=mesh, in_specs=in_specs, out_specs=out_specs, check_vma=False)
```

```python
import functools

import jax
import jax.numpy as jnp
from jax import lax
from jax.experimental import pallas as pl
from jax.experimental.pallas import tpu as pltpu
from jax.sharding import PartitionSpec as P

HALO = 4
LANES = 128
EDGE = 16
MESH = pl.DeviceIdType.MESH


def rolled(vec, rows):
    return pltpu.roll(jnp.broadcast_to(vec, (rows, LANES)), 0, 1, stride=1, stride_axis=0)


def conv_kernel(basis, out_rows, band_len, polar_count, total_rows,
                start_hbm, width_hbm, lat_hbm, lon_hbm, cyc_hbm, fields_hbm, mix_hbm, out_ref,
                start_s, width_s, lat_v, tap_v, cyc_v, fields_ref, mix_ref,
                top_c, bot_c, top_h, bot_h, own_h, polar_o, f_ref, h_ref, send_sem, recv_sem, load_sem):
    cols = out_ref.shape[1]
    chans = out_ref.shape[2]
    ext_rows = out_rows + 2 * HALO
    lat = lax.axis_index("lat")
    tap_first = jnp.clip(lat * out_rows - HALO, 0, total_rows - ext_rows)
    loads = [
        pltpu.make_async_copy(fields_hbm, fields_ref, load_sem.at[0]),
        pltpu.make_async_copy(lon_hbm.at[pl.ds(tap_first, ext_rows)], tap_v, load_sem.at[1]),
        pltpu.make_async_copy(start_hbm, start_s, load_sem.at[2]),
        pltpu.make_async_copy(width_hbm, width_s, load_sem.at[3]),
        pltpu.make_async_copy(lat_hbm, lat_v, load_sem.at[4]),
        pltpu.make_async_copy(cyc_hbm, cyc_v, load_sem.at[5]),
        pltpu.make_async_copy(mix_hbm, mix_ref, load_sem.at[6]),
    ]
    for c in loads:
        c.start()
    lon = lax.axis_index("lon")
    last = lax.axis_size("lat") - 1
    has_up = lat < last
    has_down = lat > 0
    is_polar = (lat == 0) | (lat == last)
    slot = jnp.minimum(lat, 1) * (out_rows - polar_count)
    up = jnp.minimum(lat + 1, last)
    down = jnp.maximum(lat - 1, 0)
    side = 1 - lon

    middle = pl.ds(EDGE, cols - 2 * EDGE)
    for buf in (top_h, bot_h, own_h):
        buf[:, middle] = jnp.zeros((buf.shape[0], cols - 2 * EDGE, chans), buf.dtype)

    barrier = pltpu.get_barrier_semaphore()

    def greet(where):
        pl.semaphore_signal(barrier, 1, device_id=where, device_id_type=MESH)

    greet({"lat": lat, "lon": side})

    @pl.when(has_up)
    def _():
        greet({"lat": up, "lon": lon})
        greet({"lat": up, "lon": side})

    @pl.when(has_down)
    def _():
        greet({"lat": down, "lon": lon})
        greet({"lat": down, "lon": side})

    pl.semaphore_wait(barrier, 1 + 2 * (has_up.astype(jnp.int32) + has_down.astype(jnp.int32)))

    def copy(n, src, dst, where):
        return pltpu.make_async_remote_copy(
            src_ref=src, dst_ref=dst, send_sem=send_sem.at[n], recv_sem=recv_sem.at[n],
            device_id=where, device_id_type=MESH)

    lo_rows = pl.ds(0, HALO)
    hi_rows = pl.ds(out_rows - HALO, HALO)
    first_cols = pl.ds(0, EDGE)
    last_cols = pl.ds(cols - EDGE, EDGE)
    c_up = copy(0, fields_hbm.at[hi_rows], top_c, {"lat": up, "lon": lon})
    c_dn = copy(1, fields_hbm.at[lo_rows], bot_c, {"lat": down, "lon": lon})
    h_up = [
        copy(2, fields_hbm.at[hi_rows, first_cols], top_h.at[:, first_cols], {"lat": up, "lon": side}),
        copy(3, fields_hbm.at[hi_rows, last_cols], top_h.at[:, last_cols], {"lat": up, "lon": side}),
    ]
    h_dn = [
        copy(4, fields_hbm.at[lo_rows, first_cols], bot_h.at[:, first_cols], {"lat": down, "lon": side}),
        copy(5, fields_hbm.at[lo_rows, last_cols], bot_h.at[:, last_cols], {"lat": down, "lon": side}),
    ]
    h_side = [
        copy(6, fields_hbm.at[:, first_cols], own_h.at[:, first_cols], {"lat": lat, "lon": side}),
        copy(7, fields_hbm.at[:, last_cols], own_h.at[:, last_cols], {"lat": lat, "lon": side}),
    ]
    pol = copy(8, fields_hbm.at[pl.ds(slot, polar_count)], polar_o, {"lat": lat, "lon": side})

    for c in h_side:
        c.start()

    @pl.when(has_up)
    def _():
        c_up.start()
        for c in h_up:
            c.start()

    @pl.when(has_down)
    def _():
        c_dn.start()
        for c in h_dn:
            c.start()

    @pl.when(is_polar)
    def _():
        pol.start()

    row_id = lax.broadcasted_iota(jnp.int32, (cols, LANES), 0)
    col_id = lax.broadcasted_iota(jnp.int32, (cols, LANES), 1)
    near = jnp.abs(col_id - row_id) <= HALO

    near_edge = jnp.concatenate([near[:8], near[cols - 8 :]], axis=0)

    def filter_rows(c_ref, e_ref, count, first):
        def filter_row(r, carry):
            xc = c_ref[r]
            xe = e_ref[r]
            rhs_c = jnp.concatenate([xc, xc], axis=0)
            rhs_e = jnp.concatenate([xe, xe], axis=0)
            local = jnp.clip(lat * out_rows - HALO + first + r - tap_first, 0, ext_rows - 1)
            t9 = tap_v[local]
            t128 = jnp.concatenate(
                [t9, jnp.zeros((basis, LANES - t9.shape[1]), jnp.float32)], axis=1
            )
            centred = pltpu.roll(t128, LANES - HALO, 1)
            main, corr = [], []
            for k in range(basis):
                u = centred[k : k + 1]
                u_hi = u.astype(jnp.bfloat16).astype(jnp.float32)
                w_hi = rolled(u_hi, cols)
                w_lo = rolled(u - u_hi, cols)
                main.append(
                    jnp.concatenate(
                        [jnp.where(near, w_hi, 0.0), jnp.where(near, w_lo, 0.0)], axis=1
                    ).astype(jnp.bfloat16)
                )
                e_hi = jnp.concatenate([w_hi[:8], w_hi[cols - 8 :]], axis=0)
                e_lo = jnp.concatenate([w_lo[:8], w_lo[cols - 8 :]], axis=0)
                corr.append(
                    jnp.concatenate(
                        [jnp.where(near_edge, 0.0, e_hi), jnp.where(near_edge, 0.0, e_lo)], axis=1
                    ).astype(jnp.bfloat16)
                )
            y = jnp.dot(jnp.concatenate(main, axis=0), rhs_c, preferred_element_type=jnp.float32)
            yc = jnp.dot(jnp.concatenate(corr, axis=0), rhs_e, preferred_element_type=jnp.float32)
            for k in range(basis):
                v = y[k * cols : (k + 1) * cols]
                c = yc[k * 16 : (k + 1) * 16]
                v = jnp.concatenate([v[:8] + c[:8], v[8 : cols - 8], v[cols - 8 :] + c[8:]], axis=0)
                f_ref[k, first + r] = v.astype(jnp.bfloat16).astype(jnp.float32)
            return carry

        lax.fori_loop(0, count, filter_row, 0)

    def zero_rows(first):
        f_ref[:, pl.ds(first, HALO)] = jnp.zeros((basis, HALO, cols, chans), jnp.float32)

    for n in (0, 1):
        loads[n].wait()
    for c in h_side:
        c.wait_recv()
    filter_rows(fields_ref, own_h, out_rows, HALO)

    loads[5].wait()

    def polar_rows(pole):
        pol.wait_recv()
        upper = col_id >= row_id
        for k in range(basis):
            for p in range(polar_count):
                a = cyc_v[k, pl.ds(pole * polar_count + p, 1), :].astype(jnp.float32)
                ra = rolled(a[:, :LANES], cols)
                rb = rolled(a[:, LANES:], cols)
                circ_t = jnp.concatenate(
                    [jnp.where(upper, ra, rb), jnp.where(upper, rb, ra)], axis=0
                )
                circ = jnp.transpose(circ_t).astype(jnp.bfloat16)
                g = jnp.concatenate([fields_ref[slot + p], polar_o[p]], axis=0)
                y = jnp.dot(circ, g, preferred_element_type=jnp.float32)
                f_ref[k, HALO + slot + p] = y.astype(jnp.bfloat16).astype(jnp.float32)

    @pl.when(lat == 0)
    def _():
        polar_rows(0)

    @pl.when(lat == last)
    def _():
        polar_rows(1)

    @pl.when(has_down)
    def _():
        c_up.wait_recv()
        for c in h_up:
            c.wait_recv()
        filter_rows(top_c, top_h, HALO, 0)

    @pl.when(lat == 0)
    def _():
        zero_rows(0)

    @pl.when(has_up)
    def _():
        c_dn.wait_recv()
        for c in h_dn:
            c.wait_recv()
        filter_rows(bot_c, bot_h, HALO, HALO + out_rows)

    @pl.when(lat == last)
    def _():
        zero_rows(HALO + out_rows)

    for n in (2, 3, 4, 6):
        loads[n].wait()
    base_row = lat * out_rows

    def band_row(i, carry):
        lw = lat_v[i].astype(jnp.float32)
        begin = start_s[i]
        width = width_s[i]
        rows = []
        for t in range(band_len):
            source = begin + t
            ok = (t < width) & (source >= 0) & (source < total_rows)
            rows.append((ok, jnp.clip(source - base_row + HALO, 0, ext_rows - 1)))
        for k in range(basis):
            acc = jnp.zeros((cols, chans), jnp.float32)
            for t, (ok, r) in enumerate(rows):
                w = jnp.where(ok, lw[k : k + 1, t : t + 1], 0.0)
                acc = acc + w * f_ref[k, r]
            h_ref[i, :, k * chans : (k + 1) * chans] = acc.astype(jnp.bfloat16)
        return carry

    lax.fori_loop(0, out_rows, band_row, 0)

    flat = (out_rows * cols, chans)
    mixed = jnp.dot(
        h_ref[...].reshape(out_rows * cols, basis * chans), mix_ref[...],
        preferred_element_type=jnp.float32,
    )
    out_ref[...] = (fields_ref[...].astype(jnp.float32).reshape(flat) + mixed).astype(
        out_ref.dtype
    ).reshape(out_ref.shape)

    for c in h_side:
        c.wait_send()

    @pl.when(has_up)
    def _():
        c_up.wait_send()
        for c in h_up:
            c.wait_send()

    @pl.when(has_down)
    def _():
        c_dn.wait_send()
        for c in h_dn:
            c.wait_send()

    @pl.when(is_polar)
    def _():
        pol.wait_send()


def shards(fields, lon_taps, lat_taps, cycle_taps, band_start, band_width, mixing):
    row_count, col_count, chan_count = fields.shape
    basis_count = lon_taps.shape[1]
    taps_count = lon_taps.shape[2]
    reach_cells = (taps_count - 1) // 2
    band_len = lat_taps.shape[2]
    polar_rows = row_count // 2
    lat_count = lax.axis_size("lat")
    lon_count = lax.axis_size("lon")
    assert lon_count == 2 and reach_cells == HALO
    cycle_len = lon_count * col_count
    lat_pos = lax.axis_index("lat")
    ext_rows = row_count + 2 * HALO
    total_rows = lat_count * row_count

    mix_flat = mixing.reshape(basis_count * chan_count, chan_count)

    hbm = pl.BlockSpec(memory_space=pl.ANY)
    kernel = functools.partial(
        conv_kernel, basis_count, row_count, band_len, polar_rows, total_rows
    )
    halo_block = pltpu.VMEM((HALO, col_count, chan_count), fields.dtype)
    return pl.pallas_call(
        kernel,
        out_shape=jax.ShapeDtypeStruct(fields.shape, fields.dtype),
        in_specs=[hbm] * 7,
        out_specs=pl.BlockSpec(memory_space=pltpu.VMEM),
        scratch_shapes=[
            pltpu.SMEM(band_start.shape, band_start.dtype),
            pltpu.SMEM(band_width.shape, band_width.dtype),
            pltpu.VMEM(lat_taps.shape, lat_taps.dtype),
            pltpu.VMEM((ext_rows,) + lon_taps.shape[1:], lon_taps.dtype),
            pltpu.VMEM(cycle_taps.shape, cycle_taps.dtype),
            pltpu.VMEM(fields.shape, fields.dtype),
            pltpu.VMEM(mix_flat.shape, mix_flat.dtype),
            halo_block,
            halo_block,
            halo_block,
            halo_block,
            pltpu.VMEM(fields.shape, fields.dtype),
            pltpu.VMEM((polar_rows, col_count, chan_count), fields.dtype),
            pltpu.VMEM((basis_count, ext_rows, col_count, chan_count), jnp.float32),
            pltpu.VMEM((row_count, col_count, basis_count * chan_count), jnp.bfloat16),
            pltpu.SemaphoreType.DMA((9,)),
            pltpu.SemaphoreType.DMA((9,)),
            pltpu.SemaphoreType.DMA((7,)),
        ],
        compiler_params=pltpu.CompilerParams(
            vmem_limit_bytes=67043328, collective_id=0, has_side_effects=True
        ),
    )(band_start, band_width, lat_taps, lon_taps, cycle_taps, fields, mix_flat)


def solution(mesh):
    in_specs = (
        P(("ens", "lat"), "lon", None),
        P(),
        P("lat", None, None),
        P(),
        P("lat"),
        P("lat"),
        P(),
    )
    out_specs = P(("ens", "lat"), "lon", None)
    return jax.shard_map(shards, mesh=mesh, in_specs=in_specs, out_specs=out_specs, check_vma=False)
```

```python
import functools

import jax
import jax.numpy as jnp
from jax import lax
from jax.experimental import pallas as pl
from jax.experimental.pallas import tpu as pltpu
from jax.sharding import PartitionSpec as P

HALO = 4
LANES = 128
EDGE = 16
MESH = pl.DeviceIdType.MESH


def rolled(vec, rows):
    return pltpu.roll(jnp.broadcast_to(vec, (rows, LANES)), 0, 1, stride=1, stride_axis=0)


def conv_kernel(basis, out_rows, band_len, polar_count, total_rows,
                start_hbm, width_hbm, lat_hbm, lon_hbm, cyc_hbm, fields_hbm, mix_hbm, out_ref,
                start_s, width_s, lat_v, tap_v, cyc_v, fields_ref, mix_ref,
                top_c, bot_c, top_h, bot_h, own_h, polar_o, f_ref, h_ref, send_sem, recv_sem, load_sem):
    cols = out_ref.shape[1]
    chans = out_ref.shape[2]
    ext_rows = out_rows + 2 * HALO
    lat = lax.axis_index("lat")
    tap_first = jnp.clip(lat * out_rows - HALO, 0, total_rows - ext_rows)
    loads = [
        pltpu.make_async_copy(fields_hbm, fields_ref, load_sem.at[0]),
        pltpu.make_async_copy(lon_hbm.at[pl.ds(tap_first, ext_rows)], tap_v, load_sem.at[1]),
        pltpu.make_async_copy(start_hbm, start_s, load_sem.at[2]),
        pltpu.make_async_copy(width_hbm, width_s, load_sem.at[3]),
        pltpu.make_async_copy(lat_hbm, lat_v, load_sem.at[4]),
        pltpu.make_async_copy(cyc_hbm, cyc_v, load_sem.at[5]),
        pltpu.make_async_copy(mix_hbm, mix_ref, load_sem.at[6]),
    ]
    for c in loads:
        c.start()
    lon = lax.axis_index("lon")
    last = lax.axis_size("lat") - 1
    has_up = lat < last
    has_down = lat > 0
    is_polar = (lat == 0) | (lat == last)
    slot = jnp.minimum(lat, 1) * (out_rows - polar_count)
    up = jnp.minimum(lat + 1, last)
    down = jnp.maximum(lat - 1, 0)
    side = 1 - lon

    middle = pl.ds(EDGE, cols - 2 * EDGE)
    for buf in (top_h, bot_h, own_h):
        buf[:, middle] = jnp.zeros((buf.shape[0], cols - 2 * EDGE, chans), buf.dtype)

    barrier = pltpu.get_barrier_semaphore()

    def greet(where):
        pl.semaphore_signal(barrier, 1, device_id=where, device_id_type=MESH)

    greet({"lat": lat, "lon": side})

    @pl.when(has_up)
    def _():
        greet({"lat": up, "lon": lon})
        greet({"lat": up, "lon": side})

    @pl.when(has_down)
    def _():
        greet({"lat": down, "lon": lon})
        greet({"lat": down, "lon": side})

    pl.semaphore_wait(barrier, 1 + 2 * (has_up.astype(jnp.int32) + has_down.astype(jnp.int32)))

    def copy(n, src, dst, where):
        return pltpu.make_async_remote_copy(
            src_ref=src, dst_ref=dst, send_sem=send_sem.at[n], recv_sem=recv_sem.at[n],
            device_id=where, device_id_type=MESH)

    lo_rows = pl.ds(0, HALO)
    hi_rows = pl.ds(out_rows - HALO, HALO)
    first_cols = pl.ds(0, EDGE)
    last_cols = pl.ds(cols - EDGE, EDGE)
    c_up = copy(0, fields_hbm.at[hi_rows], top_c, {"lat": up, "lon": lon})
    c_dn = copy(1, fields_hbm.at[lo_rows], bot_c, {"lat": down, "lon": lon})
    h_up = [
        copy(2, fields_hbm.at[hi_rows, first_cols], top_h.at[:, first_cols], {"lat": up, "lon": side}),
        copy(3, fields_hbm.at[hi_rows, last_cols], top_h.at[:, last_cols], {"lat": up, "lon": side}),
    ]
    h_dn = [
        copy(4, fields_hbm.at[lo_rows, first_cols], bot_h.at[:, first_cols], {"lat": down, "lon": side}),
        copy(5, fields_hbm.at[lo_rows, last_cols], bot_h.at[:, last_cols], {"lat": down, "lon": side}),
    ]
    h_side = [
        copy(6, fields_hbm.at[:, first_cols], own_h.at[:, first_cols], {"lat": lat, "lon": side}),
        copy(7, fields_hbm.at[:, last_cols], own_h.at[:, last_cols], {"lat": lat, "lon": side}),
    ]
    pol = copy(8, fields_hbm.at[pl.ds(slot, polar_count)], polar_o, {"lat": lat, "lon": side})

    for c in h_side:
        c.start()

    @pl.when(has_up)
    def _():
        c_up.start()
        for c in h_up:
            c.start()

    @pl.when(has_down)
    def _():
        c_dn.start()
        for c in h_dn:
            c.start()

    @pl.when(is_polar)
    def _():
        pol.start()

    row_id = lax.broadcasted_iota(jnp.int32, (cols, LANES), 0)
    col_id = lax.broadcasted_iota(jnp.int32, (cols, LANES), 1)
    near = jnp.abs(col_id - row_id) <= HALO

    near_edge = jnp.concatenate([near[:8], near[cols - 8 :]], axis=0)

    def filter_rows(c_ref, e_ref, count, first):
        def filter_row(r, carry):
            xc = c_ref[r]
            xe = e_ref[r]
            rhs_c = jnp.concatenate([xc, xc], axis=0)
            rhs_e = jnp.concatenate([xe, xe], axis=0)
            local = jnp.clip(lat * out_rows - HALO + first + r - tap_first, 0, ext_rows - 1)
            t9 = tap_v[local]
            t128 = jnp.concatenate(
                [t9, jnp.zeros((basis, LANES - t9.shape[1]), jnp.float32)], axis=1
            )
            centred = pltpu.roll(t128, LANES - HALO, 1)
            main, corr = [], []
            for k in range(basis):
                u = centred[k : k + 1]
                u_hi = u.astype(jnp.bfloat16).astype(jnp.float32)
                w_hi = rolled(u_hi, cols)
                w_lo = rolled(u - u_hi, cols)
                main.append(
                    jnp.concatenate(
                        [jnp.where(near, w_hi, 0.0), jnp.where(near, w_lo, 0.0)], axis=1
                    ).astype(jnp.bfloat16)
                )
                e_hi = jnp.concatenate([w_hi[:8], w_hi[cols - 8 :]], axis=0)
                e_lo = jnp.concatenate([w_lo[:8], w_lo[cols - 8 :]], axis=0)
                corr.append(
                    jnp.concatenate(
                        [jnp.where(near_edge, 0.0, e_hi), jnp.where(near_edge, 0.0, e_lo)], axis=1
                    ).astype(jnp.bfloat16)
                )
            y = jnp.dot(jnp.concatenate(main, axis=0), rhs_c, preferred_element_type=jnp.float32)
            yc = jnp.dot(jnp.concatenate(corr, axis=0), rhs_e, preferred_element_type=jnp.float32)
            for k in range(basis):
                v = y[k * cols : (k + 1) * cols]
                c = yc[k * 16 : (k + 1) * 16]
                v = jnp.concatenate([v[:8] + c[:8], v[8 : cols - 8], v[cols - 8 :] + c[8:]], axis=0)
                f_ref[k, first + r] = v.astype(jnp.bfloat16).astype(jnp.float32)
            return carry

        lax.fori_loop(0, count, filter_row, 0)

    def zero_rows(first):
        f_ref[:, pl.ds(first, HALO)] = jnp.zeros((basis, HALO, cols, chans), jnp.float32)

    for n in (0, 1):
        loads[n].wait()
    for c in h_side:
        c.wait_recv()
    filter_rows(fields_ref, own_h, out_rows, HALO)

    loads[5].wait()

    def polar_rows(pole):
        pol.wait_recv()
        upper = col_id >= row_id
        for k in range(basis):
            for p in range(polar_count):
                a = cyc_v[k, pl.ds(pole * polar_count + p, 1), :].astype(jnp.float32)
                ra = rolled(a[:, :LANES], cols)
                rb = rolled(a[:, LANES:], cols)
                circ_t = jnp.concatenate(
                    [jnp.where(upper, ra, rb), jnp.where(upper, rb, ra)], axis=0
                )
                circ = jnp.transpose(circ_t).astype(jnp.bfloat16)
                g = jnp.concatenate([fields_ref[slot + p], polar_o[p]], axis=0)
                y = jnp.dot(circ, g, preferred_element_type=jnp.float32)
                f_ref[k, HALO + slot + p] = y.astype(jnp.bfloat16).astype(jnp.float32)

    @pl.when(lat == 0)
    def _():
        polar_rows(0)

    @pl.when(lat == last)
    def _():
        polar_rows(1)

    @pl.when(has_down)
    def _():
        c_up.wait_recv()
        for c in h_up:
            c.wait_recv()
        filter_rows(top_c, top_h, HALO, 0)

    @pl.when(lat == 0)
    def _():
        zero_rows(0)

    @pl.when(has_up)
    def _():
        c_dn.wait_recv()
        for c in h_dn:
            c.wait_recv()
        filter_rows(bot_c, bot_h, HALO, HALO + out_rows)

    @pl.when(lat == last)
    def _():
        zero_rows(HALO + out_rows)

    for n in (2, 3, 4, 6):
        loads[n].wait()
    base_row = lat * out_rows

    def band_row(i, carry):
        lw = lat_v[i].astype(jnp.float32)
        begin = start_s[i]
        width = width_s[i]
        rows = []
        for t in range(band_len):
            source = begin + t
            ok = (t < width) & (source >= 0) & (source < total_rows)
            rows.append((ok, jnp.clip(source - base_row + HALO, 0, ext_rows - 1)))
        for k in range(basis):
            acc = jnp.zeros((cols, chans), jnp.float32)
            for t, (ok, r) in enumerate(rows):
                w = jnp.where(ok, lw[k : k + 1, t : t + 1], 0.0)
                acc = acc + w * f_ref[k, r]
            h_ref[i, :, k * chans : (k + 1) * chans] = acc.astype(jnp.bfloat16)
        return carry

    lax.fori_loop(0, out_rows, band_row, 0)

    flat = (out_rows * cols, chans)
    mixed = jnp.dot(
        h_ref[...].reshape(out_rows * cols, basis * chans), mix_ref[...],
        preferred_element_type=jnp.float32,
    )
    out_ref[...] = (fields_ref[...].astype(jnp.float32).reshape(flat) + mixed).astype(
        out_ref.dtype
    ).reshape(out_ref.shape)

    for c in h_side:
        c.wait_send()

    @pl.when(has_up)
    def _():
        c_up.wait_send()
        for c in h_up:
            c.wait_send()

    @pl.when(has_down)
    def _():
        c_dn.wait_send()
        for c in h_dn:
            c.wait_send()

    @pl.when(is_polar)
    def _():
        pol.wait_send()


def shards(fields, lon_taps, lat_taps, cycle_taps, band_start, band_width, mixing):
    row_count, col_count, chan_count = fields.shape
    basis_count = lon_taps.shape[1]
    taps_count = lon_taps.shape[2]
    reach_cells = (taps_count - 1) // 2
    band_len = lat_taps.shape[2]
    polar_rows = row_count // 2
    lat_count = lax.axis_size("lat")
    lon_count = lax.axis_size("lon")
    assert lon_count == 2 and reach_cells == HALO
    cycle_len = lon_count * col_count
    lat_pos = lax.axis_index("lat")
    ext_rows = row_count + 2 * HALO
    total_rows = lat_count * row_count

    mix_flat = mixing.reshape(basis_count * chan_count, chan_count)

    hbm = pl.BlockSpec(memory_space=pl.ANY)
    kernel = functools.partial(
        conv_kernel, basis_count, row_count, band_len, polar_rows, total_rows
    )
    halo_block = pltpu.VMEM((HALO, col_count, chan_count), fields.dtype)
    return pl.pallas_call(
        kernel,
        out_shape=jax.ShapeDtypeStruct(fields.shape, fields.dtype),
        in_specs=[hbm] * 7,
        out_specs=pl.BlockSpec(memory_space=pltpu.VMEM),
        scratch_shapes=[
            pltpu.SMEM(band_start.shape, band_start.dtype),
            pltpu.SMEM(band_width.shape, band_width.dtype),
            pltpu.VMEM(lat_taps.shape, lat_taps.dtype),
            pltpu.VMEM((ext_rows,) + lon_taps.shape[1:], lon_taps.dtype),
            pltpu.VMEM(cycle_taps.shape, cycle_taps.dtype),
            pltpu.VMEM(fields.shape, fields.dtype),
            pltpu.VMEM(mix_flat.shape, mix_flat.dtype),
            halo_block,
            halo_block,
            halo_block,
            halo_block,
            pltpu.VMEM(fields.shape, fields.dtype),
            pltpu.VMEM((polar_rows, col_count, chan_count), fields.dtype),
            pltpu.VMEM((basis_count, ext_rows, col_count, chan_count), jnp.float32),
            pltpu.VMEM((row_count, col_count, basis_count * chan_count), jnp.bfloat16),
            pltpu.SemaphoreType.DMA((9,)),
            pltpu.SemaphoreType.DMA((9,)),
            pltpu.SemaphoreType.DMA((7,)),
        ],
        compiler_params=pltpu.CompilerParams(
            vmem_limit_bytes=40 * 1024 * 1024, collective_id=0, has_side_effects=True
        ),
    )(band_start, band_width, lat_taps, lon_taps, cycle_taps, fields, mix_flat)


def solution(mesh):
    in_specs = (
        P(("ens", "lat"), "lon", None),
        P(),
        P("lat", None, None),
        P(),
        P("lat"),
        P("lat"),
        P(),
    )
    out_specs = P(("ens", "lat"), "lon", None)
    return jax.shard_map(shards, mesh=mesh, in_specs=in_specs, out_specs=out_specs, check_vma=False)
```

```python
import functools

import jax
import jax.numpy as jnp
from jax import lax
from jax.experimental import pallas as pl
from jax.experimental.pallas import tpu as pltpu
from jax.sharding import PartitionSpec as P

HALO = 4
LANES = 128
EDGE = 16
MESH = pl.DeviceIdType.MESH


def rolled(vec, rows):
    return pltpu.roll(jnp.broadcast_to(vec, (rows, LANES)), 0, 1, stride=1, stride_axis=0)


def conv_kernel(basis, out_rows, band_len, polar_count, total_rows,
                start_hbm, width_hbm, lat_hbm, lon_hbm, cyc_hbm, fields_hbm, mix_hbm, out_ref,
                start_s, width_s, lat_v, tap_v, tap_u, cyc_v, fields_ref, mix_ref,
                top_c, bot_c, top_h, bot_h, own_h, polar_o, f_ref, h_ref, send_sem, recv_sem, load_sem):
    cols = out_ref.shape[1]
    chans = out_ref.shape[2]
    ext_rows = out_rows + 2 * HALO
    lat = lax.axis_index("lat")
    loads = [
        pltpu.make_async_copy(fields_hbm, fields_ref, load_sem.at[0]),
        pltpu.make_async_copy(lon_hbm, tap_v, load_sem.at[1]),
        pltpu.make_async_copy(start_hbm, start_s, load_sem.at[2]),
        pltpu.make_async_copy(width_hbm, width_s, load_sem.at[3]),
        pltpu.make_async_copy(lat_hbm, lat_v, load_sem.at[4]),
        pltpu.make_async_copy(cyc_hbm, cyc_v, load_sem.at[5]),
        pltpu.make_async_copy(mix_hbm, mix_ref, load_sem.at[6]),
    ]
    for c in loads:
        c.start()
    lon = lax.axis_index("lon")
    last = lax.axis_size("lat") - 1
    has_up = lat < last
    has_down = lat > 0
    is_polar = (lat == 0) | (lat == last)
    slot = jnp.minimum(lat, 1) * (out_rows - polar_count)
    up = jnp.minimum(lat + 1, last)
    down = jnp.maximum(lat - 1, 0)
    side = 1 - lon

    middle = pl.ds(EDGE, cols - 2 * EDGE)
    for buf in (top_h, bot_h, own_h):
        buf[:, middle] = jnp.zeros((buf.shape[0], cols - 2 * EDGE, chans), buf.dtype)

    barrier = pltpu.get_barrier_semaphore()

    def greet(where):
        pl.semaphore_signal(barrier, 1, device_id=where, device_id_type=MESH)

    greet({"lat": lat, "lon": side})

    @pl.when(has_up)
    def _():
        greet({"lat": up, "lon": lon})
        greet({"lat": up, "lon": side})

    @pl.when(has_down)
    def _():
        greet({"lat": down, "lon": lon})
        greet({"lat": down, "lon": side})

    pl.semaphore_wait(barrier, 1 + 2 * (has_up.astype(jnp.int32) + has_down.astype(jnp.int32)))

    def copy(n, src, dst, where):
        return pltpu.make_async_remote_copy(
            src_ref=src, dst_ref=dst, send_sem=send_sem.at[n], recv_sem=recv_sem.at[n],
            device_id=where, device_id_type=MESH)

    lo_rows = pl.ds(0, HALO)
    hi_rows = pl.ds(out_rows - HALO, HALO)
    first_cols = pl.ds(0, EDGE)
    last_cols = pl.ds(cols - EDGE, EDGE)
    c_up = copy(0, fields_hbm.at[hi_rows], top_c, {"lat": up, "lon": lon})
    c_dn = copy(1, fields_hbm.at[lo_rows], bot_c, {"lat": down, "lon": lon})
    h_up = [
        copy(2, fields_hbm.at[hi_rows, first_cols], top_h.at[:, first_cols], {"lat": up, "lon": side}),
        copy(3, fields_hbm.at[hi_rows, last_cols], top_h.at[:, last_cols], {"lat": up, "lon": side}),
    ]
    h_dn = [
        copy(4, fields_hbm.at[lo_rows, first_cols], bot_h.at[:, first_cols], {"lat": down, "lon": side}),
        copy(5, fields_hbm.at[lo_rows, last_cols], bot_h.at[:, last_cols], {"lat": down, "lon": side}),
    ]
    h_side = [
        copy(6, fields_hbm.at[:, first_cols], own_h.at[:, first_cols], {"lat": lat, "lon": side}),
        copy(7, fields_hbm.at[:, last_cols], own_h.at[:, last_cols], {"lat": lat, "lon": side}),
    ]
    pol = copy(8, fields_hbm.at[pl.ds(slot, polar_count)], polar_o, {"lat": lat, "lon": side})

    for c in h_side:
        c.start()

    @pl.when(has_up)
    def _():
        c_up.start()
        for c in h_up:
            c.start()

    @pl.when(has_down)
    def _():
        c_dn.start()
        for c in h_dn:
            c.start()

    @pl.when(is_polar)
    def _():
        pol.start()

    row_id = lax.broadcasted_iota(jnp.int32, (cols, LANES), 0)
    col_id = lax.broadcasted_iota(jnp.int32, (cols, LANES), 1)
    near = jnp.abs(col_id - row_id) <= HALO

    near_edge = jnp.concatenate([near[:8], near[cols - 8 :]], axis=0)

    def filter_rows(c_ref, e_ref, count, first):
        def filter_row(r, carry):
            xc = c_ref[r]
            xe = e_ref[r]
            rhs_c = jnp.concatenate([xc, xc], axis=0)
            rhs_e = jnp.concatenate([xe, xe], axis=0)
            centred = tap_u[:, first + r]
            main, corr = [], []
            for k in range(basis):
                u = centred[k : k + 1]
                u_hi = u.astype(jnp.bfloat16).astype(jnp.float32)
                w_hi = rolled(u_hi, cols)
                w_lo = rolled(u - u_hi, cols)
                main.append(
                    jnp.concatenate(
                        [jnp.where(near, w_hi, 0.0), jnp.where(near, w_lo, 0.0)], axis=1
                    ).astype(jnp.bfloat16)
                )
                e_hi = jnp.concatenate([w_hi[:8], w_hi[cols - 8 :]], axis=0)
                e_lo = jnp.concatenate([w_lo[:8], w_lo[cols - 8 :]], axis=0)
                corr.append(
                    jnp.concatenate(
                        [jnp.where(near_edge, 0.0, e_hi), jnp.where(near_edge, 0.0, e_lo)], axis=1
                    ).astype(jnp.bfloat16)
                )
            y = jnp.dot(jnp.concatenate(main, axis=0), rhs_c, preferred_element_type=jnp.float32)
            yc = jnp.dot(jnp.concatenate(corr, axis=0), rhs_e, preferred_element_type=jnp.float32)
            for k in range(basis):
                v = y[k * cols : (k + 1) * cols]
                c = yc[k * 16 : (k + 1) * 16]
                v = jnp.concatenate([v[:8] + c[:8], v[8 : cols - 8], v[cols - 8 :] + c[8:]], axis=0)
                f_ref[k, first + r] = v.astype(jnp.bfloat16).astype(jnp.float32)
            return carry

        lax.fori_loop(0, count, filter_row, 0)

    def zero_rows(first):
        f_ref[:, pl.ds(first, HALO)] = jnp.zeros((basis, HALO, cols, chans), jnp.float32)

    for n in (0, 1):
        loads[n].wait()
    taps_count = tap_v.shape[0]
    shift = lax.rem(total_rows - (lat * out_rows - HALO) + total_rows, total_rows)
    for k in range(basis):
        a = tap_v[:, k, :]
        a = jnp.concatenate([a, jnp.zeros((2 * 8 - taps_count, total_rows), jnp.float32)], axis=0)
        a = pltpu.roll(a, shift, 1)[:, :LANES]
        a = jnp.transpose(a)
        a = jnp.concatenate([a, jnp.zeros((LANES, LANES - 2 * 8), jnp.float32)], axis=1)
        tap_u[k] = pltpu.roll(a, LANES - HALO, 1)[:ext_rows]
    for c in h_side:
        c.wait_recv()
    filter_rows(fields_ref, own_h, out_rows, HALO)

    loads[5].wait()

    def polar_rows(pole):
        pol.wait_recv()
        upper = col_id >= row_id
        for k in range(basis):
            for p in range(polar_count):
                a = cyc_v[k, pl.ds(pole * polar_count + p, 1), :].astype(jnp.float32)
                ra = rolled(a[:, :LANES], cols)
                rb = rolled(a[:, LANES:], cols)
                circ_t = jnp.concatenate(
                    [jnp.where(upper, ra, rb), jnp.where(upper, rb, ra)], axis=0
                )
                circ = jnp.transpose(circ_t).astype(jnp.bfloat16)
                g = jnp.concatenate([fields_ref[slot + p], polar_o[p]], axis=0)
                y = jnp.dot(circ, g, preferred_element_type=jnp.float32)
                f_ref[k, HALO + slot + p] = y.astype(jnp.bfloat16).astype(jnp.float32)

    @pl.when(lat == 0)
    def _():
        polar_rows(0)

    @pl.when(lat == last)
    def _():
        polar_rows(1)

    @pl.when(has_down)
    def _():
        c_up.wait_recv()
        for c in h_up:
            c.wait_recv()
        filter_rows(top_c, top_h, HALO, 0)

    @pl.when(lat == 0)
    def _():
        zero_rows(0)

    @pl.when(has_up)
    def _():
        c_dn.wait_recv()
        for c in h_dn:
            c.wait_recv()
        filter_rows(bot_c, bot_h, HALO, HALO + out_rows)

    @pl.when(lat == last)
    def _():
        zero_rows(HALO + out_rows)

    for n in (2, 3, 4, 6):
        loads[n].wait()
    base_row = lat * out_rows

    lw_all = lat_v[...].astype(jnp.float32)
    for i in range(out_rows):
        begin = start_s[i]
        width = width_s[i]
        rows = []
        for t in range(band_len):
            source = begin + t
            ok = (t < width) & (source >= 0) & (source < total_rows)
            rows.append((ok, jnp.clip(source - base_row + HALO, 0, ext_rows - 1)))
        for k in range(basis):
            acc = jnp.zeros((cols, chans), jnp.float32)
            for t, (ok, r) in enumerate(rows):
                w = jnp.where(ok, lw_all[t, k : k + 1, i : i + 1], 0.0)
                acc = acc + w * f_ref[k, r]
            h_ref[i, :, k * chans : (k + 1) * chans] = acc.astype(jnp.bfloat16)

    flat = (out_rows * cols, chans)
    mixed = jnp.dot(
        h_ref[...].reshape(out_rows * cols, basis * chans), mix_ref[...],
        preferred_element_type=jnp.float32,
    )
    out_ref[...] = (fields_ref[...].astype(jnp.float32).reshape(flat) + mixed).astype(
        out_ref.dtype
    ).reshape(out_ref.shape)

    for c in h_side:
        c.wait_send()

    @pl.when(has_up)
    def _():
        c_up.wait_send()
        for c in h_up:
            c.wait_send()

    @pl.when(has_down)
    def _():
        c_dn.wait_send()
        for c in h_dn:
            c.wait_send()

    @pl.when(is_polar)
    def _():
        pol.wait_send()


def shards(fields, lon_taps, lat_taps, cycle_taps, band_start, band_width, mixing):
    row_count, col_count, chan_count = fields.shape
    basis_count = lon_taps.shape[1]
    taps_count = lon_taps.shape[2]
    reach_cells = (taps_count - 1) // 2
    band_len = lat_taps.shape[2]
    polar_rows = row_count // 2
    lat_count = lax.axis_size("lat")
    lon_count = lax.axis_size("lon")
    assert lon_count == 2 and reach_cells == HALO
    cycle_len = lon_count * col_count
    lat_pos = lax.axis_index("lat")
    ext_rows = row_count + 2 * HALO
    total_rows = lat_count * row_count

    mix_flat = mixing.reshape(basis_count * chan_count, chan_count)
    lon_t = jnp.transpose(lon_taps, (2, 1, 0))
    lat_t = jnp.transpose(lat_taps, (2, 1, 0))

    hbm = pl.BlockSpec(memory_space=pl.ANY)
    kernel = functools.partial(
        conv_kernel, basis_count, row_count, band_len, polar_rows, total_rows
    )
    halo_block = pltpu.VMEM((HALO, col_count, chan_count), fields.dtype)
    return pl.pallas_call(
        kernel,
        out_shape=jax.ShapeDtypeStruct(fields.shape, fields.dtype),
        in_specs=[hbm] * 6 + [pl.BlockSpec(memory_space=pltpu.HBM)],
        out_specs=pl.BlockSpec(memory_space=pltpu.VMEM),
        scratch_shapes=[
            pltpu.SMEM(band_start.shape, band_start.dtype),
            pltpu.SMEM(band_width.shape, band_width.dtype),
            pltpu.VMEM(lat_t.shape, lat_t.dtype),
            pltpu.VMEM(lon_t.shape, lon_t.dtype),
            pltpu.VMEM((basis_count, ext_rows, LANES), jnp.float32),
            pltpu.VMEM(cycle_taps.shape, cycle_taps.dtype),
            pltpu.VMEM(fields.shape, fields.dtype),
            pltpu.VMEM(mix_flat.shape, mix_flat.dtype),
            halo_block,
            halo_block,
            halo_block,
            halo_block,
            pltpu.VMEM(fields.shape, fields.dtype),
            pltpu.VMEM((polar_rows, col_count, chan_count), fields.dtype),
            pltpu.VMEM((basis_count, ext_rows, col_count, chan_count), jnp.float32),
            pltpu.VMEM((row_count, col_count, basis_count * chan_count), jnp.bfloat16),
            pltpu.SemaphoreType.DMA((9,)),
            pltpu.SemaphoreType.DMA((9,)),
            pltpu.SemaphoreType.DMA((7,)),
        ],
        compiler_params=pltpu.CompilerParams(
            vmem_limit_bytes=67043328, collective_id=0, has_side_effects=True
        ),
    )(band_start, band_width, lat_t, lon_t, cycle_taps, fields, mix_flat)


def solution(mesh):
    in_specs = (
        P(("ens", "lat"), "lon", None),
        P(),
        P("lat", None, None),
        P(),
        P("lat"),
        P("lat"),
        P(),
    )
    out_specs = P(("ens", "lat"), "lon", None)
    return jax.shard_map(shards, mesh=mesh, in_specs=in_specs, out_specs=out_specs, check_vma=False)
```

```python
import functools

import jax
import jax.numpy as jnp
from jax import lax
from jax.experimental import pallas as pl
from jax.experimental.pallas import tpu as pltpu
from jax.sharding import PartitionSpec as P

HALO = 4
LANES = 128
EDGE = 16
MESH = pl.DeviceIdType.MESH


def rolled(vec, rows):
    return pltpu.roll(jnp.broadcast_to(vec, (rows, LANES)), 0, 1, stride=1, stride_axis=0)


def conv_kernel(basis, out_rows, band_len, polar_count, total_rows,
                start_hbm, width_hbm, lat_hbm, lon_hbm, cyc_hbm, fields_hbm, mix_hbm, out_ref,
                start_s, width_s, lat_v, tap_v, tap_u, cyc_v, fields_ref, mix_ref,
                top_c, bot_c, top_h, bot_h, own_h, polar_o, f_ref, acc_ref, h_ref,
                send_sem, recv_sem, load_sem):
    cols = out_ref.shape[1]
    chans = out_ref.shape[2]
    ext_rows = out_rows + 2 * HALO
    lat = lax.axis_index("lat")
    loads = [
        pltpu.make_async_copy(fields_hbm, fields_ref, load_sem.at[0]),
        pltpu.make_async_copy(lon_hbm, tap_v, load_sem.at[1]),
        pltpu.make_async_copy(start_hbm, start_s, load_sem.at[2]),
        pltpu.make_async_copy(width_hbm, width_s, load_sem.at[3]),
        pltpu.make_async_copy(lat_hbm, lat_v, load_sem.at[4]),
        pltpu.make_async_copy(cyc_hbm, cyc_v, load_sem.at[5]),
        pltpu.make_async_copy(mix_hbm, mix_ref, load_sem.at[6]),
    ]
    for c in loads:
        c.start()
    lon = lax.axis_index("lon")
    last = lax.axis_size("lat") - 1
    has_up = lat < last
    has_down = lat > 0
    is_polar = (lat == 0) | (lat == last)
    slot = jnp.minimum(lat, 1) * (out_rows - polar_count)
    up = jnp.minimum(lat + 1, last)
    down = jnp.maximum(lat - 1, 0)
    side = 1 - lon

    middle = pl.ds(EDGE, cols - 2 * EDGE)
    for buf in (top_h, bot_h, own_h):
        buf[:, middle] = jnp.zeros((buf.shape[0], cols - 2 * EDGE, chans), buf.dtype)

    barrier = pltpu.get_barrier_semaphore()

    def greet(where):
        pl.semaphore_signal(barrier, 1, device_id=where, device_id_type=MESH)

    greet({"lat": lat, "lon": side})

    @pl.when(has_up)
    def _():
        greet({"lat": up, "lon": lon})
        greet({"lat": up, "lon": side})

    @pl.when(has_down)
    def _():
        greet({"lat": down, "lon": lon})
        greet({"lat": down, "lon": side})

    pl.semaphore_wait(barrier, 1 + 2 * (has_up.astype(jnp.int32) + has_down.astype(jnp.int32)))

    def copy(n, src, dst, where):
        return pltpu.make_async_remote_copy(
            src_ref=src, dst_ref=dst, send_sem=send_sem.at[n], recv_sem=recv_sem.at[n],
            device_id=where, device_id_type=MESH)

    lo_rows = pl.ds(0, HALO)
    hi_rows = pl.ds(out_rows - HALO, HALO)
    first_cols = pl.ds(0, EDGE)
    last_cols = pl.ds(cols - EDGE, EDGE)
    c_up = copy(0, fields_hbm.at[hi_rows], top_c, {"lat": up, "lon": lon})
    c_dn = copy(1, fields_hbm.at[lo_rows], bot_c, {"lat": down, "lon": lon})
    h_up = [
        copy(2, fields_hbm.at[hi_rows, first_cols], top_h.at[:, first_cols], {"lat": up, "lon": side}),
        copy(3, fields_hbm.at[hi_rows, last_cols], top_h.at[:, last_cols], {"lat": up, "lon": side}),
    ]
    h_dn = [
        copy(4, fields_hbm.at[lo_rows, first_cols], bot_h.at[:, first_cols], {"lat": down, "lon": side}),
        copy(5, fields_hbm.at[lo_rows, last_cols], bot_h.at[:, last_cols], {"lat": down, "lon": side}),
    ]
    h_side = [
        copy(6, fields_hbm.at[:, first_cols], own_h.at[:, first_cols], {"lat": lat, "lon": side}),
        copy(7, fields_hbm.at[:, last_cols], own_h.at[:, last_cols], {"lat": lat, "lon": side}),
    ]
    pol = copy(8, fields_hbm.at[pl.ds(slot, polar_count)], polar_o, {"lat": lat, "lon": side})

    for c in h_side:
        c.start()

    @pl.when(has_up)
    def _():
        c_up.start()
        for c in h_up:
            c.start()

    @pl.when(has_down)
    def _():
        c_dn.start()
        for c in h_dn:
            c.start()

    @pl.when(is_polar)
    def _():
        pol.start()

    row_id = lax.broadcasted_iota(jnp.int32, (cols, LANES), 0)
    col_id = lax.broadcasted_iota(jnp.int32, (cols, LANES), 1)
    near = jnp.abs(col_id - row_id) <= HALO

    near_edge = jnp.concatenate([near[:8], near[cols - 8 :]], axis=0)

    def filter_rows(c_ref, e_ref, count, first):
        def filter_row(r, carry):
            xc = c_ref[r]
            xe = e_ref[r]
            rhs_c = jnp.concatenate([xc, xc], axis=0)
            rhs_e = jnp.concatenate([xe, xe], axis=0)
            centred = tap_u[:, first + r]
            main, corr = [], []
            for k in range(basis):
                u = centred[k : k + 1]
                u_hi = u.astype(jnp.bfloat16).astype(jnp.float32)
                w_hi = rolled(u_hi, cols)
                w_lo = rolled(u - u_hi, cols)
                main.append(
                    jnp.concatenate(
                        [jnp.where(near, w_hi, 0.0), jnp.where(near, w_lo, 0.0)], axis=1
                    ).astype(jnp.bfloat16)
                )
                e_hi = jnp.concatenate([w_hi[:8], w_hi[cols - 8 :]], axis=0)
                e_lo = jnp.concatenate([w_lo[:8], w_lo[cols - 8 :]], axis=0)
                corr.append(
                    jnp.concatenate(
                        [jnp.where(near_edge, 0.0, e_hi), jnp.where(near_edge, 0.0, e_lo)], axis=1
                    ).astype(jnp.bfloat16)
                )
            y = jnp.dot(jnp.concatenate(main, axis=0), rhs_c, preferred_element_type=jnp.float32)
            yc = jnp.dot(jnp.concatenate(corr, axis=0), rhs_e, preferred_element_type=jnp.float32)
            for k in range(basis):
                v = y[k * cols : (k + 1) * cols]
                c = yc[k * 16 : (k + 1) * 16]
                v = jnp.concatenate([v[:8] + c[:8], v[8 : cols - 8], v[cols - 8 :] + c[8:]], axis=0)
                f_ref[k, first + r] = v.astype(jnp.bfloat16).astype(jnp.float32)
            return carry

        lax.fori_loop(0, count, filter_row, 0)

    def zero_rows(first):
        f_ref[:, pl.ds(first, HALO)] = jnp.zeros((basis, HALO, cols, chans), jnp.float32)

    for n in (0, 1):
        loads[n].wait()
    taps_count = tap_v.shape[0]
    shift = lax.rem(total_rows - (lat * out_rows - HALO) + total_rows, total_rows)
    for k in range(basis):
        a = tap_v[:, k, :]
        a = jnp.concatenate([a, jnp.zeros((2 * 8 - taps_count, total_rows), jnp.float32)], axis=0)
        a = pltpu.roll(a, shift, 1)[:, :LANES]
        a = jnp.transpose(a)
        a = jnp.concatenate([a, jnp.zeros((LANES, LANES - 2 * 8), jnp.float32)], axis=1)
        tap_u[k] = pltpu.roll(a, LANES - HALO, 1)[:ext_rows]
    for c in h_side:
        c.wait_recv()
    filter_rows(fields_ref, own_h, out_rows, HALO)

    loads[5].wait()

    def polar_rows(pole):
        pol.wait_recv()
        upper = col_id >= row_id
        for k in range(basis):
            for p in range(polar_count):
                a = cyc_v[k, pl.ds(pole * polar_count + p, 1), :].astype(jnp.float32)
                ra = rolled(a[:, :LANES], cols)
                rb = rolled(a[:, LANES:], cols)
                circ_t = jnp.concatenate(
                    [jnp.where(upper, ra, rb), jnp.where(upper, rb, ra)], axis=0
                )
                circ = jnp.transpose(circ_t).astype(jnp.bfloat16)
                g = jnp.concatenate([fields_ref[slot + p], polar_o[p]], axis=0)
                y = jnp.dot(circ, g, preferred_element_type=jnp.float32)
                f_ref[k, HALO + slot + p] = y.astype(jnp.bfloat16).astype(jnp.float32)

    @pl.when(lat == 0)
    def _():
        polar_rows(0)

    @pl.when(lat == last)
    def _():
        polar_rows(1)

    for n in (2, 3, 4, 6):
        loads[n].wait()
    base_row = lat * out_rows
    lw_all = lat_v[...].astype(jnp.float32)
    terms = []
    for i in range(out_rows):
        begin = start_s[i]
        width = width_s[i]
        row_terms = []
        for t in range(band_len):
            source = begin + t
            ok = (t < width) & (source >= 0) & (source < total_rows)
            r = jnp.clip(source - base_row + HALO, 0, ext_rows - 1)
            row_terms.append((ok, r))
        terms.append(row_terms)

    def weight(i, k, t, keep):
        ok, r = terms[i][t]
        return jnp.where(ok & keep(r), lw_all[t, k : k + 1, i : i + 1], 0.0)

    def own(r):
        return (r >= HALO) & (r < HALO + out_rows)

    for i in range(out_rows):
        for k in range(basis):
            acc = jnp.zeros((cols, chans), jnp.float32)
            for t in range(band_len):
                r = jnp.clip(terms[i][t][1], HALO, HALO + out_rows - 1)
                acc = acc + weight(i, k, t, own) * f_ref[k, r]
            acc_ref[i, k] = acc

    def finish(rows, steps, keep):
        for i in rows:
            for k in range(basis):
                acc = acc_ref[i, k]
                for t in steps(i):
                    acc = acc + weight(i, k, t, keep) * f_ref[k, terms[i][t][1]]
                h_ref[i, :, k * chans : (k + 1) * chans] = acc.astype(jnp.bfloat16)
        first, count = rows[0], len(rows)
        flat = (count * cols, chans)
        mixed = jnp.dot(
            h_ref[pl.ds(first, count)].reshape(count * cols, basis * chans), mix_ref[...],
            preferred_element_type=jnp.float32,
        )
        own_rows = fields_ref[pl.ds(first, count)].astype(jnp.float32).reshape(flat)
        out_ref[pl.ds(first, count)] = (own_rows + mixed).astype(out_ref.dtype).reshape(
            (count, cols, chans)
        )

    half = out_rows // 2

    @pl.when(has_down)
    def _():
        c_up.wait_recv()
        for c in h_up:
            c.wait_recv()
        filter_rows(top_c, top_h, HALO, 0)

    @pl.when(lat == 0)
    def _():
        zero_rows(0)

    finish(list(range(half)), lambda i: range(0, HALO - i), lambda r: r < HALO)

    @pl.when(has_up)
    def _():
        c_dn.wait_recv()
        for c in h_dn:
            c.wait_recv()
        filter_rows(bot_c, bot_h, HALO, HALO + out_rows)

    @pl.when(lat == last)
    def _():
        zero_rows(HALO + out_rows)

    finish(
        list(range(half, out_rows)),
        lambda i: range(out_rows + 1 - i, band_len),
        lambda r: r >= HALO + out_rows,
    )

    for c in h_side:
        c.wait_send()

    @pl.when(has_up)
    def _():
        c_up.wait_send()
        for c in h_up:
            c.wait_send()

    @pl.when(has_down)
    def _():
        c_dn.wait_send()
        for c in h_dn:
            c.wait_send()

    @pl.when(is_polar)
    def _():
        pol.wait_send()


def shards(fields, lon_taps, lat_taps, cycle_taps, band_start, band_width, mixing):
    row_count, col_count, chan_count = fields.shape
    basis_count = lon_taps.shape[1]
    taps_count = lon_taps.shape[2]
    reach_cells = (taps_count - 1) // 2
    band_len = lat_taps.shape[2]
    polar_rows = row_count // 2
    lat_count = lax.axis_size("lat")
    lon_count = lax.axis_size("lon")
    assert lon_count == 2 and reach_cells == HALO
    cycle_len = lon_count * col_count
    lat_pos = lax.axis_index("lat")
    ext_rows = row_count + 2 * HALO
    total_rows = lat_count * row_count

    mix_flat = mixing.reshape(basis_count * chan_count, chan_count)
    lon_t = jnp.transpose(lon_taps, (2, 1, 0))
    lat_t = jnp.transpose(lat_taps, (2, 1, 0))

    hbm = pl.BlockSpec(memory_space=pl.ANY)
    kernel = functools.partial(
        conv_kernel, basis_count, row_count, band_len, polar_rows, total_rows
    )
    halo_block = pltpu.VMEM((HALO, col_count, chan_count), fields.dtype)
    return pl.pallas_call(
        kernel,
        out_shape=jax.ShapeDtypeStruct(fields.shape, fields.dtype),
        in_specs=[hbm] * 6 + [pl.BlockSpec(memory_space=pltpu.HBM)],
        out_specs=pl.BlockSpec(memory_space=pltpu.VMEM),
        scratch_shapes=[
            pltpu.SMEM(band_start.shape, band_start.dtype),
            pltpu.SMEM(band_width.shape, band_width.dtype),
            pltpu.VMEM(lat_t.shape, lat_t.dtype),
            pltpu.VMEM(lon_t.shape, lon_t.dtype),
            pltpu.VMEM((basis_count, ext_rows, LANES), jnp.float32),
            pltpu.VMEM(cycle_taps.shape, cycle_taps.dtype),
            pltpu.VMEM(fields.shape, fields.dtype),
            pltpu.VMEM(mix_flat.shape, mix_flat.dtype),
            halo_block,
            halo_block,
            halo_block,
            halo_block,
            pltpu.VMEM(fields.shape, fields.dtype),
            pltpu.VMEM((polar_rows, col_count, chan_count), fields.dtype),
            pltpu.VMEM((basis_count, ext_rows, col_count, chan_count), jnp.float32),
            pltpu.VMEM((row_count, basis_count, col_count, chan_count), jnp.float32),
            pltpu.VMEM((row_count, col_count, basis_count * chan_count), jnp.bfloat16),
            pltpu.SemaphoreType.DMA((9,)),
            pltpu.SemaphoreType.DMA((9,)),
            pltpu.SemaphoreType.DMA((7,)),
        ],
        compiler_params=pltpu.CompilerParams(
            vmem_limit_bytes=67043328, collective_id=0, has_side_effects=True
        ),
    )(band_start, band_width, lat_t, lon_t, cycle_taps, fields, mix_flat)


def solution(mesh):
    in_specs = (
        P(("ens", "lat"), "lon", None),
        P(),
        P("lat", None, None),
        P(),
        P("lat"),
        P("lat"),
        P(),
    )
    out_specs = P(("ens", "lat"), "lon", None)
    return jax.shard_map(shards, mesh=mesh, in_specs=in_specs, out_specs=out_specs, check_vma=False)
```

```python
import functools

import jax
import jax.numpy as jnp
from jax import lax
from jax.experimental import pallas as pl
from jax.experimental.pallas import tpu as pltpu
from jax.sharding import PartitionSpec as P

HALO = 4
LANES = 128
EDGE = 16
MESH = pl.DeviceIdType.MESH


def rolled(vec, rows):
    return pltpu.roll(jnp.broadcast_to(vec, (rows, LANES)), 0, 1, stride=1, stride_axis=0)


def conv_kernel(basis, out_rows, band_len, polar_count, total_rows,
                start_hbm, width_hbm, lat_hbm, lon_hbm, cyc_hbm, fields_hbm, mix_hbm, out_ref,
                start_s, width_s, lat_v, tap_v, tap_u, cyc_v, fields_ref, mix_ref,
                top_c, bot_c, top_h, bot_h, own_h, polar_o, f_ref, acc_ref, h_ref,
                send_sem, recv_sem, load_sem):
    cols = out_ref.shape[1]
    chans = out_ref.shape[2]
    ext_rows = out_rows + 2 * HALO
    lat = lax.axis_index("lat")
    loads = [
        pltpu.make_async_copy(fields_hbm, fields_ref, load_sem.at[0]),
        pltpu.make_async_copy(lon_hbm, tap_v, load_sem.at[1]),
        pltpu.make_async_copy(start_hbm, start_s, load_sem.at[2]),
        pltpu.make_async_copy(width_hbm, width_s, load_sem.at[3]),
        pltpu.make_async_copy(lat_hbm, lat_v, load_sem.at[4]),
        pltpu.make_async_copy(cyc_hbm, cyc_v, load_sem.at[5]),
        pltpu.make_async_copy(mix_hbm, mix_ref, load_sem.at[6]),
    ]
    for c in loads:
        c.start()
    lon = lax.axis_index("lon")
    last = lax.axis_size("lat") - 1
    has_up = lat < last
    has_down = lat > 0
    is_polar = (lat == 0) | (lat == last)
    slot = jnp.minimum(lat, 1) * (out_rows - polar_count)
    up = jnp.minimum(lat + 1, last)
    down = jnp.maximum(lat - 1, 0)
    side = 1 - lon

    middle = pl.ds(EDGE, cols - 2 * EDGE)
    for buf in (top_h, bot_h, own_h):
        buf[:, middle] = jnp.zeros((buf.shape[0], cols - 2 * EDGE, chans), buf.dtype)

    barrier = pltpu.get_barrier_semaphore()

    def greet(where):
        pl.semaphore_signal(barrier, 1, device_id=where, device_id_type=MESH)

    greet({"lat": lat, "lon": side})

    @pl.when(has_up)
    def _():
        greet({"lat": up, "lon": lon})
        greet({"lat": up, "lon": side})

    @pl.when(has_down)
    def _():
        greet({"lat": down, "lon": lon})
        greet({"lat": down, "lon": side})

    pl.semaphore_wait(barrier, 1 + 2 * (has_up.astype(jnp.int32) + has_down.astype(jnp.int32)))

    def copy(n, src, dst, where):
        return pltpu.make_async_remote_copy(
            src_ref=src, dst_ref=dst, send_sem=send_sem.at[n], recv_sem=recv_sem.at[n],
            device_id=where, device_id_type=MESH)

    lo_rows = pl.ds(0, HALO)
    hi_rows = pl.ds(out_rows - HALO, HALO)
    first_cols = pl.ds(0, EDGE)
    last_cols = pl.ds(cols - EDGE, EDGE)
    c_up = copy(0, fields_hbm.at[hi_rows], top_c, {"lat": up, "lon": lon})
    c_dn = copy(1, fields_hbm.at[lo_rows], bot_c, {"lat": down, "lon": lon})
    h_up = [
        copy(2, fields_hbm.at[hi_rows, first_cols], top_h.at[:, first_cols], {"lat": up, "lon": side}),
        copy(3, fields_hbm.at[hi_rows, last_cols], top_h.at[:, last_cols], {"lat": up, "lon": side}),
    ]
    h_dn = [
        copy(4, fields_hbm.at[lo_rows, first_cols], bot_h.at[:, first_cols], {"lat": down, "lon": side}),
        copy(5, fields_hbm.at[lo_rows, last_cols], bot_h.at[:, last_cols], {"lat": down, "lon": side}),
    ]
    h_side = [
        copy(6, fields_hbm.at[:, first_cols], own_h.at[:, first_cols], {"lat": lat, "lon": side}),
        copy(7, fields_hbm.at[:, last_cols], own_h.at[:, last_cols], {"lat": lat, "lon": side}),
    ]
    pol = copy(8, fields_hbm.at[pl.ds(slot, polar_count)], polar_o, {"lat": lat, "lon": side})

    for c in h_side:
        c.start()

    @pl.when(has_up)
    def _():
        c_up.start()
        for c in h_up:
            c.start()

    @pl.when(has_down)
    def _():
        c_dn.start()
        for c in h_dn:
            c.start()

    @pl.when(is_polar)
    def _():
        pol.start()

    row_id = lax.broadcasted_iota(jnp.int32, (cols, LANES), 0)
    col_id = lax.broadcasted_iota(jnp.int32, (cols, LANES), 1)
    near = jnp.abs(col_id - row_id) <= HALO

    near_edge = jnp.concatenate([near[:8], near[cols - 8 :]], axis=0)

    def filter_rows(c_ref, e_ref, count, first):
        def filter_row(r, carry):
            xc = c_ref[r]
            xe = e_ref[r]
            rhs_c = jnp.concatenate([xc, xc], axis=0)
            rhs_e = jnp.concatenate([xe, xe], axis=0)
            centred = tap_u[:, first + r]
            main, corr = [], []
            for k in range(basis):
                u = centred[k : k + 1]
                u_hi = u.astype(jnp.bfloat16).astype(jnp.float32)
                w_hi = rolled(u_hi, cols)
                w_lo = rolled(u - u_hi, cols)
                main.append(
                    jnp.concatenate(
                        [jnp.where(near, w_hi, 0.0), jnp.where(near, w_lo, 0.0)], axis=1
                    ).astype(jnp.bfloat16)
                )
                e_hi = jnp.concatenate([w_hi[:8], w_hi[cols - 8 :]], axis=0)
                e_lo = jnp.concatenate([w_lo[:8], w_lo[cols - 8 :]], axis=0)
                corr.append(
                    jnp.concatenate(
                        [jnp.where(near_edge, 0.0, e_hi), jnp.where(near_edge, 0.0, e_lo)], axis=1
                    ).astype(jnp.bfloat16)
                )
            y = jnp.dot(jnp.concatenate(main, axis=0), rhs_c, preferred_element_type=jnp.float32)
            yc = jnp.dot(jnp.concatenate(corr, axis=0), rhs_e, preferred_element_type=jnp.float32)
            for k in range(basis):
                v = y[k * cols : (k + 1) * cols]
                c = yc[k * 16 : (k + 1) * 16]
                v = jnp.concatenate([v[:8] + c[:8], v[8 : cols - 8], v[cols - 8 :] + c[8:]], axis=0)
                f_ref[k, first + r] = v.astype(jnp.bfloat16).astype(jnp.float32)
            return carry

        lax.fori_loop(0, count, filter_row, 0)

    def zero_rows(first):
        f_ref[:, pl.ds(first, HALO)] = jnp.zeros((basis, HALO, cols, chans), jnp.float32)

    for n in (0, 1):
        loads[n].wait()
    taps_count = tap_v.shape[0]
    shift = lax.rem(total_rows - (lat * out_rows - HALO) + total_rows, total_rows)
    for k in range(basis):
        a = tap_v[:, k, :]
        a = jnp.concatenate([a, jnp.zeros((2 * 8 - taps_count, total_rows), jnp.float32)], axis=0)
        a = pltpu.roll(a, shift, 1)[:, :LANES]
        a = jnp.transpose(a)
        a = jnp.concatenate([a, jnp.zeros((LANES, LANES - 2 * 8), jnp.float32)], axis=1)
        tap_u[k] = pltpu.roll(a, LANES - HALO, 1)[:ext_rows]
    for c in h_side:
        c.wait_recv()
    filter_rows(fields_ref, own_h, out_rows, HALO)

    loads[5].wait()

    def polar_rows(pole):
        pol.wait_recv()
        upper = col_id >= row_id
        for k in range(basis):
            for p in range(polar_count):
                a = cyc_v[k, pl.ds(pole * polar_count + p, 1), :].astype(jnp.float32)
                ra = rolled(a[:, :LANES], cols)
                rb = rolled(a[:, LANES:], cols)
                circ_t = jnp.concatenate(
                    [jnp.where(upper, ra, rb), jnp.where(upper, rb, ra)], axis=0
                )
                circ = jnp.transpose(circ_t).astype(jnp.bfloat16)
                g = jnp.concatenate([fields_ref[slot + p], polar_o[p]], axis=0)
                y = jnp.dot(circ, g, preferred_element_type=jnp.float32)
                f_ref[k, HALO + slot + p] = y.astype(jnp.bfloat16).astype(jnp.float32)

    @pl.when(lat == 0)
    def _():
        polar_rows(0)

    @pl.when(lat == last)
    def _():
        polar_rows(1)

    for n in (2, 3, 4, 6):
        loads[n].wait()
    base_row = lat * out_rows
    lw_all = lat_v[...].astype(jnp.float32)
    terms = []
    for i in range(out_rows):
        begin = start_s[i]
        width = width_s[i]
        row_terms = []
        for t in range(band_len):
            source = begin + t
            ok = (t < width) & (source >= 0) & (source < total_rows)
            r = jnp.clip(source - base_row + HALO, 0, ext_rows - 1)
            row_terms.append((ok, r))
        terms.append(row_terms)

    def weight(i, k, t, keep):
        ok, r = terms[i][t]
        return jnp.where(ok & keep(r), lw_all[t, k : k + 1, i : i + 1], 0.0)

    def own(r):
        return (r >= HALO) & (r < HALO + out_rows)

    for i in range(out_rows):
        for k in range(basis):
            acc = jnp.zeros((cols, chans), jnp.float32)
            for t in range(band_len):
                r = jnp.clip(terms[i][t][1], HALO, HALO + out_rows - 1)
                acc = acc + weight(i, k, t, own) * f_ref[k, r]
            acc_ref[i, k] = acc

    def finish(rows, steps, keep):
        for i in rows:
            for k in range(basis):
                acc = acc_ref[i, k]
                for t in steps(i):
                    acc = acc + weight(i, k, t, keep) * f_ref[k, terms[i][t][1]]
                h_ref[i, :, k * chans : (k + 1) * chans] = acc.astype(jnp.bfloat16)
        first, count = rows[0], len(rows)
        flat = (count * cols, chans)
        mixed = jnp.dot(
            h_ref[pl.ds(first, count)].reshape(count * cols, basis * chans), mix_ref[...],
            preferred_element_type=jnp.float32,
        )
        own_rows = fields_ref[pl.ds(first, count)].astype(jnp.float32).reshape(flat)
        out_ref[pl.ds(first, count)] = (own_rows + mixed).astype(out_ref.dtype).reshape(
            (count, cols, chans)
        )

    half = out_rows // 2

    @pl.when(has_down)
    def _():
        c_up.wait_recv()
        for c in h_up:
            c.wait_recv()
        filter_rows(top_c, top_h, HALO, 0)

    @pl.when(lat == 0)
    def _():
        zero_rows(0)

    finish(list(range(half)), lambda i: range(0, HALO - i), lambda r: r < HALO)

    @pl.when(has_up)
    def _():
        c_dn.wait_recv()
        for c in h_dn:
            c.wait_recv()
        filter_rows(bot_c, bot_h, HALO, HALO + out_rows)

    @pl.when(lat == last)
    def _():
        zero_rows(HALO + out_rows)

    finish(
        list(range(half, out_rows)),
        lambda i: range(out_rows + 1 - i, band_len),
        lambda r: r >= HALO + out_rows,
    )

    for c in h_side:
        c.wait_send()

    @pl.when(has_up)
    def _():
        c_up.wait_send()
        for c in h_up:
            c.wait_send()

    @pl.when(has_down)
    def _():
        c_dn.wait_send()
        for c in h_dn:
            c.wait_send()

    @pl.when(is_polar)
    def _():
        pol.wait_send()


def shards(fields, lon_taps, lat_taps, cycle_taps, band_start, band_width, mixing):
    row_count, col_count, chan_count = fields.shape
    basis_count = lon_taps.shape[1]
    taps_count = lon_taps.shape[2]
    reach_cells = (taps_count - 1) // 2
    band_len = lat_taps.shape[2]
    polar_rows = row_count // 2
    lat_count = lax.axis_size("lat")
    lon_count = lax.axis_size("lon")
    assert lon_count == 2 and reach_cells == HALO
    cycle_len = lon_count * col_count
    lat_pos = lax.axis_index("lat")
    ext_rows = row_count + 2 * HALO
    total_rows = lat_count * row_count

    mix_flat = mixing.reshape(basis_count * chan_count, chan_count)
    lon_t = jnp.transpose(lon_taps, (2, 1, 0))
    lat_t = jnp.transpose(lat_taps, (2, 1, 0))

    hbm = pl.BlockSpec(memory_space=pl.ANY)
    kernel = functools.partial(
        conv_kernel, basis_count, row_count, band_len, polar_rows, total_rows
    )
    halo_block = pltpu.VMEM((HALO, col_count, chan_count), fields.dtype)
    return copy_out(pl.pallas_call(
        kernel,
        out_shape=jax.ShapeDtypeStruct(fields.shape, fields.dtype),
        in_specs=[hbm] * 6 + [pl.BlockSpec(memory_space=pltpu.HBM)],
        out_specs=pl.BlockSpec(memory_space=pltpu.VMEM),
        scratch_shapes=[
            pltpu.SMEM(band_start.shape, band_start.dtype),
            pltpu.SMEM(band_width.shape, band_width.dtype),
            pltpu.VMEM(lat_t.shape, lat_t.dtype),
            pltpu.VMEM(lon_t.shape, lon_t.dtype),
            pltpu.VMEM((basis_count, ext_rows, LANES), jnp.float32),
            pltpu.VMEM(cycle_taps.shape, cycle_taps.dtype),
            pltpu.VMEM(fields.shape, fields.dtype),
            pltpu.VMEM(mix_flat.shape, mix_flat.dtype),
            halo_block,
            halo_block,
            halo_block,
            halo_block,
            pltpu.VMEM(fields.shape, fields.dtype),
            pltpu.VMEM((polar_rows, col_count, chan_count), fields.dtype),
            pltpu.VMEM((basis_count, ext_rows, col_count, chan_count), jnp.float32),
            pltpu.VMEM((row_count, basis_count, col_count, chan_count), jnp.float32),
            pltpu.VMEM((row_count, col_count, basis_count * chan_count), jnp.bfloat16),
            pltpu.SemaphoreType.DMA((9,)),
            pltpu.SemaphoreType.DMA((9,)),
            pltpu.SemaphoreType.DMA((7,)),
        ],
        compiler_params=pltpu.CompilerParams(
            vmem_limit_bytes=67043328, collective_id=0, has_side_effects=True
        ),
    )(band_start, band_width, lat_t, lon_t, cycle_taps, fields, mix_flat))


def copy_out(block):
    def body(src, dst):
        dst[...] = src[...]

    rows = block.shape[0]
    step = 2
    spec = pl.BlockSpec((step,) + block.shape[1:], lambda i: (i, 0, 0))
    return pl.pallas_call(
        body,
        out_shape=jax.ShapeDtypeStruct(block.shape, block.dtype),
        grid=(rows // step,),
        in_specs=[spec],
        out_specs=spec,
    )(block)


def solution(mesh):
    in_specs = (
        P(("ens", "lat"), "lon", None),
        P(),
        P("lat", None, None),
        P(),
        P("lat"),
        P("lat"),
        P(),
    )
    out_specs = P(("ens", "lat"), "lon", None)
    return jax.shard_map(shards, mesh=mesh, in_specs=in_specs, out_specs=out_specs, check_vma=False)
```

```python
import functools

import jax
import jax.numpy as jnp
from jax import lax
from jax.experimental import pallas as pl
from jax.experimental.pallas import tpu as pltpu
from jax.sharding import PartitionSpec as P

HALO = 4
LANES = 128
EDGE = 16
MESH = pl.DeviceIdType.MESH


def rolled(vec, rows):
    return pltpu.roll(jnp.broadcast_to(vec, (rows, LANES)), 0, 1, stride=1, stride_axis=0)


def conv_kernel(basis, out_rows, band_len, polar_count, total_rows,
                start_hbm, width_hbm, lat_hbm, lon_hbm, cyc_hbm, fields_hbm, mix_hbm, out_ref,
                start_s, width_s, lat_v, tap_v, tap_u, cyc_v, fields_ref, mix_ref,
                top_c, bot_c, top_h, bot_h, own_h, polar_o, f_ref, acc_ref, h_ref,
                send_sem, recv_sem, load_sem):
    cols = out_ref.shape[1]
    chans = out_ref.shape[2]
    ext_rows = out_rows + 2 * HALO
    lat = lax.axis_index("lat")
    loads = [
        pltpu.make_async_copy(fields_hbm, fields_ref, load_sem.at[0]),
        pltpu.make_async_copy(lon_hbm, tap_v, load_sem.at[1]),
        pltpu.make_async_copy(start_hbm, start_s, load_sem.at[2]),
        pltpu.make_async_copy(width_hbm, width_s, load_sem.at[3]),
        pltpu.make_async_copy(lat_hbm, lat_v, load_sem.at[4]),
        pltpu.make_async_copy(cyc_hbm, cyc_v, load_sem.at[5]),
        pltpu.make_async_copy(mix_hbm, mix_ref, load_sem.at[6]),
    ]
    for c in loads:
        c.start()
    lon = lax.axis_index("lon")
    last = lax.axis_size("lat") - 1
    has_up = lat < last
    has_down = lat > 0
    is_polar = (lat == 0) | (lat == last)
    slot = jnp.minimum(lat, 1) * (out_rows - polar_count)
    up = jnp.minimum(lat + 1, last)
    down = jnp.maximum(lat - 1, 0)
    side = 1 - lon

    middle = pl.ds(EDGE, cols - 2 * EDGE)
    for buf in (top_h, bot_h, own_h):
        buf[:, middle] = jnp.zeros((buf.shape[0], cols - 2 * EDGE, chans), buf.dtype)

    barrier = pltpu.get_barrier_semaphore()

    def greet(where):
        pl.semaphore_signal(barrier, 1, device_id=where, device_id_type=MESH)

    greet({"lat": lat, "lon": side})

    @pl.when(has_up)
    def _():
        greet({"lat": up, "lon": lon})
        greet({"lat": up, "lon": side})

    @pl.when(has_down)
    def _():
        greet({"lat": down, "lon": lon})
        greet({"lat": down, "lon": side})

    pl.semaphore_wait(barrier, 1 + 2 * (has_up.astype(jnp.int32) + has_down.astype(jnp.int32)))

    def copy(n, src, dst, where):
        return pltpu.make_async_remote_copy(
            src_ref=src, dst_ref=dst, send_sem=send_sem.at[n], recv_sem=recv_sem.at[n],
            device_id=where, device_id_type=MESH)

    lo_rows = pl.ds(0, HALO)
    hi_rows = pl.ds(out_rows - HALO, HALO)
    first_cols = pl.ds(0, EDGE)
    last_cols = pl.ds(cols - EDGE, EDGE)
    c_up = copy(0, fields_hbm.at[hi_rows], top_c, {"lat": up, "lon": lon})
    c_dn = copy(1, fields_hbm.at[lo_rows], bot_c, {"lat": down, "lon": lon})
    h_up = [
        copy(2, fields_hbm.at[hi_rows, first_cols], top_h.at[:, first_cols], {"lat": up, "lon": side}),
        copy(3, fields_hbm.at[hi_rows, last_cols], top_h.at[:, last_cols], {"lat": up, "lon": side}),
    ]
    h_dn = [
        copy(4, fields_hbm.at[lo_rows, first_cols], bot_h.at[:, first_cols], {"lat": down, "lon": side}),
        copy(5, fields_hbm.at[lo_rows, last_cols], bot_h.at[:, last_cols], {"lat": down, "lon": side}),
    ]
    h_side = [
        copy(6, fields_hbm.at[:, first_cols], own_h.at[:, first_cols], {"lat": lat, "lon": side}),
        copy(7, fields_hbm.at[:, last_cols], own_h.at[:, last_cols], {"lat": lat, "lon": side}),
    ]
    pol = copy(8, fields_hbm.at[pl.ds(slot, polar_count)], polar_o, {"lat": lat, "lon": side})

    for c in h_side:
        c.start()

    @pl.when(has_up)
    def _():
        c_up.start()
        for c in h_up:
            c.start()

    @pl.when(has_down)
    def _():
        c_dn.start()
        for c in h_dn:
            c.start()

    @pl.when(is_polar)
    def _():
        pol.start()

    row_id = lax.broadcasted_iota(jnp.int32, (cols, LANES), 0)
    col_id = lax.broadcasted_iota(jnp.int32, (cols, LANES), 1)
    near = jnp.abs(col_id - row_id) <= HALO

    near_edge = jnp.concatenate([near[:8], near[cols - 8 :]], axis=0)

    def filter_rows(c_ref, e_ref, count, first):
        def filter_row(r, carry):
            xc = c_ref[r]
            xe = e_ref[r]
            rhs_c = jnp.concatenate([xc, xc], axis=0)
            rhs_e = jnp.concatenate([xe, xe], axis=0)
            centred = tap_u[:, first + r]
            main, corr = [], []
            for k in range(basis):
                u = centred[k : k + 1]
                u_hi = u.astype(jnp.bfloat16).astype(jnp.float32)
                w_hi = rolled(u_hi, cols)
                w_lo = rolled(u - u_hi, cols)
                main.append(
                    jnp.concatenate(
                        [jnp.where(near, w_hi, 0.0), jnp.where(near, w_lo, 0.0)], axis=1
                    ).astype(jnp.bfloat16)
                )
                e_hi = jnp.concatenate([w_hi[:8], w_hi[cols - 8 :]], axis=0)
                e_lo = jnp.concatenate([w_lo[:8], w_lo[cols - 8 :]], axis=0)
                corr.append(
                    jnp.concatenate(
                        [jnp.where(near_edge, 0.0, e_hi), jnp.where(near_edge, 0.0, e_lo)], axis=1
                    ).astype(jnp.bfloat16)
                )
            y = jnp.dot(jnp.concatenate(main, axis=0), rhs_c, preferred_element_type=jnp.float32)
            yc = jnp.dot(jnp.concatenate(corr, axis=0), rhs_e, preferred_element_type=jnp.float32)
            for k in range(basis):
                v = y[k * cols : (k + 1) * cols]
                c = yc[k * 16 : (k + 1) * 16]
                v = jnp.concatenate([v[:8] + c[:8], v[8 : cols - 8], v[cols - 8 :] + c[8:]], axis=0)
                f_ref[k, first + r] = v.astype(jnp.bfloat16).astype(jnp.float32)
            return carry

        lax.fori_loop(0, count, filter_row, 0)

    def zero_rows(first):
        f_ref[:, pl.ds(first, HALO)] = jnp.zeros((basis, HALO, cols, chans), jnp.float32)

    for n in (0, 1):
        loads[n].wait()
    taps_count = tap_v.shape[0]
    shift = lax.rem(total_rows - (lat * out_rows - HALO) + total_rows, total_rows)
    for k in range(basis):
        a = tap_v[:, k, :]
        a = jnp.concatenate([a, jnp.zeros((2 * 8 - taps_count, total_rows), jnp.float32)], axis=0)
        a = pltpu.roll(a, shift, 1)[:, :LANES]
        a = jnp.transpose(a)
        a = jnp.concatenate([a, jnp.zeros((LANES, LANES - 2 * 8), jnp.float32)], axis=1)
        tap_u[k] = pltpu.roll(a, LANES - HALO, 1)[:ext_rows]
    for c in h_side:
        c.wait_recv()
    filter_rows(fields_ref, own_h, out_rows, HALO)

    loads[5].wait()

    def polar_rows(pole):
        pol.wait_recv()
        upper = col_id >= row_id
        for k in range(basis):
            for p in range(polar_count):
                a = cyc_v[k, pl.ds(pole * polar_count + p, 1), :].astype(jnp.float32)
                ra = rolled(a[:, :LANES], cols)
                rb = rolled(a[:, LANES:], cols)
                circ_t = jnp.concatenate(
                    [jnp.where(upper, ra, rb), jnp.where(upper, rb, ra)], axis=0
                )
                circ = jnp.transpose(circ_t).astype(jnp.bfloat16)
                g = jnp.concatenate([fields_ref[slot + p], polar_o[p]], axis=0)
                y = jnp.dot(circ, g, preferred_element_type=jnp.float32)
                f_ref[k, HALO + slot + p] = y.astype(jnp.bfloat16).astype(jnp.float32)

    @pl.when(lat == 0)
    def _():
        polar_rows(0)

    @pl.when(lat == last)
    def _():
        polar_rows(1)

    for n in (2, 3, 4, 6):
        loads[n].wait()
    base_row = lat * out_rows
    lw_all = lat_v[...].astype(jnp.float32)
    terms = []
    for i in range(out_rows):
        begin = start_s[i]
        width = width_s[i]
        row_terms = []
        for t in range(band_len):
            source = begin + t
            ok = (t < width) & (source >= 0) & (source < total_rows)
            r = jnp.clip(source - base_row + HALO, 0, ext_rows - 1)
            row_terms.append((ok, r))
        terms.append(row_terms)

    def weight(i, k, t, keep):
        ok, r = terms[i][t]
        return jnp.where(ok & keep(r), lw_all[t, k : k + 1, i : i + 1], 0.0)

    def own(r):
        return (r >= HALO) & (r < HALO + out_rows)

    for i in range(out_rows):
        for k in range(basis):
            acc = jnp.zeros((cols, chans), jnp.float32)
            for t in range(band_len):
                r = jnp.clip(terms[i][t][1], HALO, HALO + out_rows - 1)
                acc = acc + weight(i, k, t, own) * f_ref[k, r]
            acc_ref[i, k] = acc

    def finish(rows, steps, keep):
        for i in rows:
            for k in range(basis):
                acc = acc_ref[i, k]
                for t in steps(i):
                    acc = acc + weight(i, k, t, keep) * f_ref[k, terms[i][t][1]]
                h_ref[i, :, k * chans : (k + 1) * chans] = acc.astype(jnp.bfloat16)
        first, count = rows[0], len(rows)
        flat = (count * cols, chans)
        mixed = jnp.dot(
            h_ref[pl.ds(first, count)].reshape(count * cols, basis * chans), mix_ref[...],
            preferred_element_type=jnp.float32,
        )
        own_rows = fields_ref[pl.ds(first, count)].astype(jnp.float32).reshape(flat)
        out_ref[pl.ds(first, count)] = (own_rows + mixed).astype(out_ref.dtype).reshape(
            (count, cols, chans)
        )

    half = out_rows // 2

    @pl.when(has_down)
    def _():
        c_up.wait_recv()
        for c in h_up:
            c.wait_recv()
        filter_rows(top_c, top_h, HALO, 0)

    @pl.when(lat == 0)
    def _():
        zero_rows(0)

    finish(list(range(half)), lambda i: range(0, HALO - i), lambda r: r < HALO)

    @pl.when(has_up)
    def _():
        c_dn.wait_recv()
        for c in h_dn:
            c.wait_recv()
        filter_rows(bot_c, bot_h, HALO, HALO + out_rows)

    @pl.when(lat == last)
    def _():
        zero_rows(HALO + out_rows)

    finish(
        list(range(half, out_rows)),
        lambda i: range(out_rows + 1 - i, band_len),
        lambda r: r >= HALO + out_rows,
    )

    for c in h_side:
        c.wait_send()

    @pl.when(has_up)
    def _():
        c_up.wait_send()
        for c in h_up:
            c.wait_send()

    @pl.when(has_down)
    def _():
        c_dn.wait_send()
        for c in h_dn:
            c.wait_send()

    @pl.when(is_polar)
    def _():
        pol.wait_send()


def shards(fields, lon_taps, lat_taps, cycle_taps, band_start, band_width, mixing):
    row_count, col_count, chan_count = fields.shape
    basis_count = lon_taps.shape[1]
    taps_count = lon_taps.shape[2]
    reach_cells = (taps_count - 1) // 2
    band_len = lat_taps.shape[2]
    polar_rows = row_count // 2
    lat_count = lax.axis_size("lat")
    lon_count = lax.axis_size("lon")
    assert lon_count == 2 and reach_cells == HALO
    cycle_len = lon_count * col_count
    lat_pos = lax.axis_index("lat")
    ext_rows = row_count + 2 * HALO
    total_rows = lat_count * row_count

    mix_flat = mixing.reshape(basis_count * chan_count, chan_count)
    lon_t = jnp.transpose(lon_taps, (2, 1, 0))
    lat_t = jnp.transpose(lat_taps, (2, 1, 0))

    hbm = pl.BlockSpec(memory_space=pl.ANY)
    kernel = functools.partial(
        conv_kernel, basis_count, row_count, band_len, polar_rows, total_rows
    )
    halo_block = pltpu.VMEM((HALO, col_count, chan_count), fields.dtype)
    return copy_out(pl.pallas_call(
        kernel,
        out_shape=jax.ShapeDtypeStruct(fields.shape, fields.dtype),
        in_specs=[hbm] * 6 + [pl.BlockSpec(memory_space=pltpu.HBM)],
        out_specs=pl.BlockSpec(memory_space=pltpu.VMEM),
        scratch_shapes=[
            pltpu.SMEM(band_start.shape, band_start.dtype),
            pltpu.SMEM(band_width.shape, band_width.dtype),
            pltpu.VMEM(lat_t.shape, lat_t.dtype),
            pltpu.VMEM(lon_t.shape, lon_t.dtype),
            pltpu.VMEM((basis_count, ext_rows, LANES), jnp.float32),
            pltpu.VMEM(cycle_taps.shape, cycle_taps.dtype),
            pltpu.VMEM(fields.shape, fields.dtype),
            pltpu.VMEM(mix_flat.shape, mix_flat.dtype),
            halo_block,
            halo_block,
            halo_block,
            halo_block,
            pltpu.VMEM(fields.shape, fields.dtype),
            pltpu.VMEM((polar_rows, col_count, chan_count), fields.dtype),
            pltpu.VMEM((basis_count, ext_rows, col_count, chan_count), jnp.float32),
            pltpu.VMEM((row_count, basis_count, col_count, chan_count), jnp.float32),
            pltpu.VMEM((row_count, col_count, basis_count * chan_count), jnp.bfloat16),
            pltpu.SemaphoreType.DMA((9,)),
            pltpu.SemaphoreType.DMA((9,)),
            pltpu.SemaphoreType.DMA((7,)),
        ],
        compiler_params=pltpu.CompilerParams(
            vmem_limit_bytes=67043328, collective_id=0, has_side_effects=True
        ),
    )(band_start, band_width, lat_t, lon_t, cycle_taps, fields, mix_flat))


def copy_out(block):
    pieces = 4
    step = block.shape[0] // pieces

    def body(src, dst, stage, sem_in, sem_out):
        ins = [
            pltpu.make_async_copy(src.at[pl.ds(n * step, step)], stage.at[pl.ds(n * step, step)], sem_in.at[n])
            for n in range(pieces)
        ]
        outs = [
            pltpu.make_async_copy(stage.at[pl.ds(n * step, step)], dst.at[pl.ds(n * step, step)], sem_out.at[n])
            for n in range(pieces)
        ]
        for c in ins:
            c.start()
        for c_in, c_out in zip(ins, outs):
            c_in.wait()
            c_out.start()
        for c in outs:
            c.wait()

    hbm = pl.BlockSpec(memory_space=pl.ANY)
    return pl.pallas_call(
        body,
        out_shape=jax.ShapeDtypeStruct(block.shape, block.dtype),
        in_specs=[hbm],
        out_specs=hbm,
        scratch_shapes=[
            pltpu.VMEM(block.shape, block.dtype),
            pltpu.SemaphoreType.DMA((pieces,)),
            pltpu.SemaphoreType.DMA((pieces,)),
        ],
    )(block)


def solution(mesh):
    in_specs = (
        P(("ens", "lat"), "lon", None),
        P(),
        P("lat", None, None),
        P(),
        P("lat"),
        P("lat"),
        P(),
    )
    out_specs = P(("ens", "lat"), "lon", None)
    return jax.shard_map(shards, mesh=mesh, in_specs=in_specs, out_specs=out_specs, check_vma=False)
```

```python
import functools

import jax
import jax.numpy as jnp
from jax import lax
from jax.experimental import pallas as pl
from jax.experimental.pallas import tpu as pltpu
from jax.sharding import PartitionSpec as P

HALO = 4
LANES = 128
EDGE = 16
X_CHIPS = 4
MESH = pl.DeviceIdType.MESH


def rolled(vec, rows):
    return pltpu.roll(jnp.broadcast_to(vec, (rows, LANES)), 0, 1, stride=1, stride_axis=0)


def conv_kernel(basis, out_rows, band_len, polar_count, total_rows,
                start_hbm, width_hbm, lat_hbm, lon_hbm, cyc_hbm, fields_hbm, mix_hbm, out_ref,
                start_s, width_s, lat_v, tap_v, tap_u, cyc_v, fields_ref, mix_ref,
                top_c, bot_c, top_h, bot_h, own_h, polar_o, f_ref, acc_ref, h_ref,
                send_sem, recv_sem, load_sem):
    cols = out_ref.shape[1]
    chans = out_ref.shape[2]
    ext_rows = out_rows + 2 * HALO
    lat = lax.axis_index("lat")
    loads = [
        pltpu.make_async_copy(fields_hbm, fields_ref, load_sem.at[0]),
        pltpu.make_async_copy(lon_hbm, tap_v, load_sem.at[1]),
        pltpu.make_async_copy(start_hbm, start_s, load_sem.at[2]),
        pltpu.make_async_copy(width_hbm, width_s, load_sem.at[3]),
        pltpu.make_async_copy(lat_hbm, lat_v, load_sem.at[4]),
        pltpu.make_async_copy(cyc_hbm, cyc_v, load_sem.at[5]),
        pltpu.make_async_copy(mix_hbm, mix_ref, load_sem.at[6]),
    ]
    for c in loads:
        c.start()
    lon = lax.axis_index("lon")
    last = lax.axis_size("lat") - 1
    has_up = lat < last
    has_down = lat > 0
    is_polar = (lat == 0) | (lat == last)
    slot = jnp.minimum(lat, 1) * (out_rows - polar_count)
    up = jnp.minimum(lat + 1, last)
    down = jnp.maximum(lat - 1, 0)
    side = 1 - lon

    middle = pl.ds(EDGE, cols - 2 * EDGE)
    for buf in (top_h, bot_h, own_h):
        buf[:, middle] = jnp.zeros((buf.shape[0], cols - 2 * EDGE, chans), buf.dtype)

    barrier = pltpu.get_barrier_semaphore()

    def greet(where):
        pl.semaphore_signal(barrier, 1, device_id=where, device_id_type=MESH)

    greet({"lat": lat, "lon": side})

    @pl.when(has_up)
    def _():
        greet({"lat": up, "lon": lon})
        greet({"lat": up, "lon": side})

    @pl.when(has_down)
    def _():
        greet({"lat": down, "lon": lon})
        greet({"lat": down, "lon": side})

    pl.semaphore_wait(barrier, 1 + 2 * (has_up.astype(jnp.int32) + has_down.astype(jnp.int32)))

    def copy(n, src, dst, where):
        return pltpu.make_async_remote_copy(
            src_ref=src, dst_ref=dst, send_sem=send_sem.at[n], recv_sem=recv_sem.at[n],
            device_id=where, device_id_type=MESH)

    lo_rows = pl.ds(0, HALO)
    hi_rows = pl.ds(out_rows - HALO, HALO)
    first_cols = pl.ds(0, EDGE)
    last_cols = pl.ds(cols - EDGE, EDGE)
    c_up = copy(0, fields_hbm.at[hi_rows], top_c, {"lat": up, "lon": lon})
    c_dn = copy(1, fields_hbm.at[lo_rows], bot_c, {"lat": down, "lon": lon})
    h_up = [
        copy(2, fields_hbm.at[hi_rows, first_cols], top_h.at[:, first_cols], {"lat": up, "lon": side}),
        copy(3, fields_hbm.at[hi_rows, last_cols], top_h.at[:, last_cols], {"lat": up, "lon": side}),
    ]
    h_dn = [
        copy(4, fields_hbm.at[lo_rows, first_cols], bot_h.at[:, first_cols], {"lat": down, "lon": side}),
        copy(5, fields_hbm.at[lo_rows, last_cols], bot_h.at[:, last_cols], {"lat": down, "lon": side}),
    ]
    h_side = [
        copy(6, fields_hbm.at[:, first_cols], own_h.at[:, first_cols], {"lat": lat, "lon": side}),
        copy(7, fields_hbm.at[:, last_cols], own_h.at[:, last_cols], {"lat": lat, "lon": side}),
    ]
    pol = copy(8, fields_hbm.at[pl.ds(slot, polar_count)], polar_o, {"lat": lat, "lon": side})

    for c in h_side:
        c.start()

    @pl.when(has_up)
    def _():
        c_up.start()
        for c in h_up:
            c.start()

    @pl.when(has_down)
    def _():
        c_dn.start()
        for c in h_dn:
            c.start()

    @pl.when(is_polar)
    def _():
        pol.start()

    row_id = lax.broadcasted_iota(jnp.int32, (cols, LANES), 0)
    col_id = lax.broadcasted_iota(jnp.int32, (cols, LANES), 1)
    near = jnp.abs(col_id - row_id) <= HALO

    near_edge = jnp.concatenate([near[:8], near[cols - 8 :]], axis=0)

    def filter_rows(c_ref, e_ref, count, first):
        def filter_row(r, carry):
            xc = c_ref[r]
            xe = e_ref[r]
            rhs_c = jnp.concatenate([xc, xc], axis=0)
            rhs_e = jnp.concatenate([xe, xe], axis=0)
            centred = tap_u[:, first + r]
            main, corr = [], []
            for k in range(basis):
                u = centred[k : k + 1]
                u_hi = u.astype(jnp.bfloat16).astype(jnp.float32)
                w_hi = rolled(u_hi, cols)
                w_lo = rolled(u - u_hi, cols)
                main.append(
                    jnp.concatenate(
                        [jnp.where(near, w_hi, 0.0), jnp.where(near, w_lo, 0.0)], axis=1
                    ).astype(jnp.bfloat16)
                )
                e_hi = jnp.concatenate([w_hi[:8], w_hi[cols - 8 :]], axis=0)
                e_lo = jnp.concatenate([w_lo[:8], w_lo[cols - 8 :]], axis=0)
                corr.append(
                    jnp.concatenate(
                        [jnp.where(near_edge, 0.0, e_hi), jnp.where(near_edge, 0.0, e_lo)], axis=1
                    ).astype(jnp.bfloat16)
                )
            y = jnp.dot(jnp.concatenate(main, axis=0), rhs_c, preferred_element_type=jnp.float32)
            yc = jnp.dot(jnp.concatenate(corr, axis=0), rhs_e, preferred_element_type=jnp.float32)
            for k in range(basis):
                v = y[k * cols : (k + 1) * cols]
                c = yc[k * 16 : (k + 1) * 16]
                v = jnp.concatenate([v[:8] + c[:8], v[8 : cols - 8], v[cols - 8 :] + c[8:]], axis=0)
                f_ref[k, first + r] = v.astype(jnp.bfloat16).astype(jnp.float32)
            return carry

        lax.fori_loop(0, count, filter_row, 0)

    def zero_rows(first):
        f_ref[:, pl.ds(first, HALO)] = jnp.zeros((basis, HALO, cols, chans), jnp.float32)

    for n in (0, 1):
        loads[n].wait()
    taps_count = tap_v.shape[0]
    shift = lax.rem(total_rows - (lat * out_rows - HALO) + total_rows, total_rows)
    for k in range(basis):
        a = tap_v[:, k, :]
        a = jnp.concatenate([a, jnp.zeros((2 * 8 - taps_count, total_rows), jnp.float32)], axis=0)
        a = pltpu.roll(a, shift, 1)[:, :LANES]
        a = jnp.transpose(a)
        a = jnp.concatenate([a, jnp.zeros((LANES, LANES - 2 * 8), jnp.float32)], axis=1)
        tap_u[k] = pltpu.roll(a, LANES - HALO, 1)[:ext_rows]
    for c in h_side:
        c.wait_recv()
    filter_rows(fields_ref, own_h, out_rows, HALO)

    loads[5].wait()

    def polar_rows(pole):
        pol.wait_recv()
        upper = col_id >= row_id
        for k in range(basis):
            for p in range(polar_count):
                a = cyc_v[k, pl.ds(pole * polar_count + p, 1), :].astype(jnp.float32)
                ra = rolled(a[:, :LANES], cols)
                rb = rolled(a[:, LANES:], cols)
                circ_t = jnp.concatenate(
                    [jnp.where(upper, ra, rb), jnp.where(upper, rb, ra)], axis=0
                )
                circ = jnp.transpose(circ_t).astype(jnp.bfloat16)
                g = jnp.concatenate([fields_ref[slot + p], polar_o[p]], axis=0)
                y = jnp.dot(circ, g, preferred_element_type=jnp.float32)
                f_ref[k, HALO + slot + p] = y.astype(jnp.bfloat16).astype(jnp.float32)

    @pl.when(lat == 0)
    def _():
        polar_rows(0)

    @pl.when(lat == last)
    def _():
        polar_rows(1)

    for n in (2, 3, 4, 6):
        loads[n].wait()
    base_row = lat * out_rows
    lw_all = lat_v[...].astype(jnp.float32)
    terms = []
    for i in range(out_rows):
        begin = start_s[i]
        width = width_s[i]
        row_terms = []
        for t in range(band_len):
            source = begin + t
            ok = (t < width) & (source >= 0) & (source < total_rows)
            r = jnp.clip(source - base_row + HALO, 0, ext_rows - 1)
            row_terms.append((ok, r))
        terms.append(row_terms)

    def weight(i, k, t, keep):
        ok, r = terms[i][t]
        return jnp.where(ok & keep(r), lw_all[t, k : k + 1, i : i + 1], 0.0)

    def own(r):
        return (r >= HALO) & (r < HALO + out_rows)

    for i in range(out_rows):
        for k in range(basis):
            acc = jnp.zeros((cols, chans), jnp.float32)
            for t in range(band_len):
                r = jnp.clip(terms[i][t][1], HALO, HALO + out_rows - 1)
                acc = acc + weight(i, k, t, own) * f_ref[k, r]
            acc_ref[i, k] = acc

    def finish(rows, steps, keep):
        for i in rows:
            for k in range(basis):
                acc = acc_ref[i, k]
                for t in steps(i):
                    acc = acc + weight(i, k, t, keep) * f_ref[k, terms[i][t][1]]
                h_ref[i, :, k * chans : (k + 1) * chans] = acc.astype(jnp.bfloat16)
        first, count = rows[0], len(rows)
        flat = (count * cols, chans)
        mixed = jnp.dot(
            h_ref[pl.ds(first, count)].reshape(count * cols, basis * chans), mix_ref[...],
            preferred_element_type=jnp.float32,
        )
        own_rows = fields_ref[pl.ds(first, count)].astype(jnp.float32).reshape(flat)
        out_ref[pl.ds(first, count)] = (own_rows + mixed).astype(out_ref.dtype).reshape(
            (count, cols, chans)
        )

    half = out_rows // 2

    def top_half():
        @pl.when(has_down)
        def _():
            c_up.wait_recv()
            for c in h_up:
                c.wait_recv()
            filter_rows(top_c, top_h, HALO, 0)

        @pl.when(lat == 0)
        def _():
            zero_rows(0)

        finish(list(range(half)), lambda i: range(0, HALO - i), lambda r: r < HALO)

    def bottom_half():
        @pl.when(has_up)
        def _():
            c_dn.wait_recv()
            for c in h_dn:
                c.wait_recv()
            filter_rows(bot_c, bot_h, HALO, HALO + out_rows)

        @pl.when(lat == last)
        def _():
            zero_rows(HALO + out_rows)

        finish(
            list(range(half, out_rows)),
            lambda i: range(out_rows + 1 - i, band_len),
            lambda r: r >= HALO + out_rows,
        )

    far_above = lax.rem(lat, X_CHIPS) == 0

    @pl.when(jnp.logical_not(far_above))
    def _():
        top_half()
        bottom_half()

    @pl.when(far_above)
    def _():
        bottom_half()
        top_half()

    for c in h_side:
        c.wait_send()

    @pl.when(has_up)
    def _():
        c_up.wait_send()
        for c in h_up:
            c.wait_send()

    @pl.when(has_down)
    def _():
        c_dn.wait_send()
        for c in h_dn:
            c.wait_send()

    @pl.when(is_polar)
    def _():
        pol.wait_send()


def shards(fields, lon_taps, lat_taps, cycle_taps, band_start, band_width, mixing):
    row_count, col_count, chan_count = fields.shape
    basis_count = lon_taps.shape[1]
    taps_count = lon_taps.shape[2]
    reach_cells = (taps_count - 1) // 2
    band_len = lat_taps.shape[2]
    polar_rows = row_count // 2
    lat_count = lax.axis_size("lat")
    lon_count = lax.axis_size("lon")
    assert lon_count == 2 and reach_cells == HALO
    cycle_len = lon_count * col_count
    lat_pos = lax.axis_index("lat")
    ext_rows = row_count + 2 * HALO
    total_rows = lat_count * row_count

    mix_flat = mixing.reshape(basis_count * chan_count, chan_count)
    lon_t = jnp.transpose(lon_taps, (2, 1, 0))
    lat_t = jnp.transpose(lat_taps, (2, 1, 0))

    hbm = pl.BlockSpec(memory_space=pl.ANY)
    kernel = functools.partial(
        conv_kernel, basis_count, row_count, band_len, polar_rows, total_rows
    )
    halo_block = pltpu.VMEM((HALO, col_count, chan_count), fields.dtype)
    return copy_out(pl.pallas_call(
        kernel,
        out_shape=jax.ShapeDtypeStruct(fields.shape, fields.dtype),
        in_specs=[hbm] * 6 + [pl.BlockSpec(memory_space=pltpu.HBM)],
        out_specs=pl.BlockSpec(memory_space=pltpu.VMEM),
        scratch_shapes=[
            pltpu.SMEM(band_start.shape, band_start.dtype),
            pltpu.SMEM(band_width.shape, band_width.dtype),
            pltpu.VMEM(lat_t.shape, lat_t.dtype),
            pltpu.VMEM(lon_t.shape, lon_t.dtype),
            pltpu.VMEM((basis_count, ext_rows, LANES), jnp.float32),
            pltpu.VMEM(cycle_taps.shape, cycle_taps.dtype),
            pltpu.VMEM(fields.shape, fields.dtype),
            pltpu.VMEM(mix_flat.shape, mix_flat.dtype),
            halo_block,
            halo_block,
            halo_block,
            halo_block,
            pltpu.VMEM(fields.shape, fields.dtype),
            pltpu.VMEM((polar_rows, col_count, chan_count), fields.dtype),
            pltpu.VMEM((basis_count, ext_rows, col_count, chan_count), jnp.float32),
            pltpu.VMEM((row_count, basis_count, col_count, chan_count), jnp.float32),
            pltpu.VMEM((row_count, col_count, basis_count * chan_count), jnp.bfloat16),
            pltpu.SemaphoreType.DMA((9,)),
            pltpu.SemaphoreType.DMA((9,)),
            pltpu.SemaphoreType.DMA((7,)),
        ],
        compiler_params=pltpu.CompilerParams(
            vmem_limit_bytes=67043328, collective_id=0, has_side_effects=True
        ),
    )(band_start, band_width, lat_t, lon_t, cycle_taps, fields, mix_flat))


def copy_out(block):
    pieces = 4
    step = block.shape[0] // pieces

    def body(src, dst, stage, sem_in, sem_out):
        ins = [
            pltpu.make_async_copy(src.at[pl.ds(n * step, step)], stage.at[pl.ds(n * step, step)], sem_in.at[n])
            for n in range(pieces)
        ]
        outs = [
            pltpu.make_async_copy(stage.at[pl.ds(n * step, step)], dst.at[pl.ds(n * step, step)], sem_out.at[n])
            for n in range(pieces)
        ]
        for c in ins:
            c.start()
        for c_in, c_out in zip(ins, outs):
            c_in.wait()
            c_out.start()
        for c in outs:
            c.wait()

    hbm = pl.BlockSpec(memory_space=pl.ANY)
    return pl.pallas_call(
        body,
        out_shape=jax.ShapeDtypeStruct(block.shape, block.dtype),
        in_specs=[hbm],
        out_specs=hbm,
        scratch_shapes=[
            pltpu.VMEM(block.shape, block.dtype),
            pltpu.SemaphoreType.DMA((pieces,)),
            pltpu.SemaphoreType.DMA((pieces,)),
        ],
    )(block)


def solution(mesh):
    in_specs = (
        P(("ens", "lat"), "lon", None),
        P(),
        P("lat", None, None),
        P(),
        P("lat"),
        P("lat"),
        P(),
    )
    out_specs = P(("ens", "lat"), "lon", None)
    return jax.shard_map(shards, mesh=mesh, in_specs=in_specs, out_specs=out_specs, check_vma=False)
```

```python
import functools

import jax
import jax.numpy as jnp
from jax import lax
from jax.experimental import pallas as pl
from jax.experimental.pallas import tpu as pltpu
from jax.sharding import PartitionSpec as P

HALO = 4
LANES = 128
EDGE = 16
X_CHIPS = 4
MESH = pl.DeviceIdType.MESH


def rolled(vec, rows):
    return pltpu.roll(jnp.broadcast_to(vec, (rows, LANES)), 0, 1, stride=1, stride_axis=0)


def conv_kernel(basis, out_rows, band_len, polar_count, total_rows,
                start_hbm, width_hbm, lat_hbm, lon_hbm, cyc_hbm, fields_hbm, mix_hbm, out_ref,
                start_s, width_s, lat_v, tap_v, tap_u, cyc_v, fields_ref, mix_ref,
                top_c, bot_c, top_h, bot_h, own_h, polar_o, f_ref, acc_ref, h_ref,
                send_sem, recv_sem, load_sem):
    cols = out_ref.shape[1]
    chans = out_ref.shape[2]
    ext_rows = out_rows + 2 * HALO
    lat = lax.axis_index("lat")
    loads = [
        pltpu.make_async_copy(fields_hbm, fields_ref, load_sem.at[0]),
        pltpu.make_async_copy(lon_hbm, tap_v, load_sem.at[1]),
        pltpu.make_async_copy(start_hbm, start_s, load_sem.at[2]),
        pltpu.make_async_copy(width_hbm, width_s, load_sem.at[3]),
        pltpu.make_async_copy(lat_hbm, lat_v, load_sem.at[4]),
        pltpu.make_async_copy(cyc_hbm, cyc_v, load_sem.at[5]),
        pltpu.make_async_copy(mix_hbm, mix_ref, load_sem.at[6]),
    ]
    for c in loads:
        c.start()
    lon = lax.axis_index("lon")
    last = lax.axis_size("lat") - 1
    has_up = lat < last
    has_down = lat > 0
    is_polar = (lat == 0) | (lat == last)
    slot = jnp.minimum(lat, 1) * (out_rows - polar_count)
    up = jnp.minimum(lat + 1, last)
    down = jnp.maximum(lat - 1, 0)
    side = 1 - lon

    middle = pl.ds(EDGE, cols - 2 * EDGE)
    for buf in (top_h, bot_h, own_h):
        buf[:, middle] = jnp.zeros((buf.shape[0], cols - 2 * EDGE, chans), buf.dtype)

    barrier = pltpu.get_barrier_semaphore()

    def greet(where):
        pl.semaphore_signal(barrier, 1, device_id=where, device_id_type=MESH)

    greet({"lat": lat, "lon": side})

    @pl.when(has_up)
    def _():
        greet({"lat": up, "lon": lon})
        greet({"lat": up, "lon": side})

    @pl.when(has_down)
    def _():
        greet({"lat": down, "lon": lon})
        greet({"lat": down, "lon": side})

    pl.semaphore_wait(barrier, 1 + 2 * (has_up.astype(jnp.int32) + has_down.astype(jnp.int32)))

    def copy(n, src, dst, where):
        return pltpu.make_async_remote_copy(
            src_ref=src, dst_ref=dst, send_sem=send_sem.at[n], recv_sem=recv_sem.at[n],
            device_id=where, device_id_type=MESH)

    lo_rows = pl.ds(0, HALO)
    hi_rows = pl.ds(out_rows - HALO, HALO)
    first_cols = pl.ds(0, EDGE)
    last_cols = pl.ds(cols - EDGE, EDGE)
    c_up = copy(0, fields_hbm.at[hi_rows], top_c, {"lat": up, "lon": lon})
    c_dn = copy(1, fields_hbm.at[lo_rows], bot_c, {"lat": down, "lon": lon})
    h_up = [
        copy(2, fields_hbm.at[hi_rows, first_cols], top_h.at[:, first_cols], {"lat": up, "lon": side}),
        copy(3, fields_hbm.at[hi_rows, last_cols], top_h.at[:, last_cols], {"lat": up, "lon": side}),
    ]
    h_dn = [
        copy(4, fields_hbm.at[lo_rows, first_cols], bot_h.at[:, first_cols], {"lat": down, "lon": side}),
        copy(5, fields_hbm.at[lo_rows, last_cols], bot_h.at[:, last_cols], {"lat": down, "lon": side}),
    ]
    h_side = [
        copy(6, fields_hbm.at[:, first_cols], own_h.at[:, first_cols], {"lat": lat, "lon": side}),
        copy(7, fields_hbm.at[:, last_cols], own_h.at[:, last_cols], {"lat": lat, "lon": side}),
    ]
    pol = copy(8, fields_hbm.at[pl.ds(slot, polar_count)], polar_o, {"lat": lat, "lon": side})

    for c in h_side:
        c.start()

    @pl.when(has_up)
    def _():
        c_up.start()
        for c in h_up:
            c.start()

    @pl.when(has_down)
    def _():
        c_dn.start()
        for c in h_dn:
            c.start()

    @pl.when(is_polar)
    def _():
        pol.start()

    row_id = lax.broadcasted_iota(jnp.int32, (cols, LANES), 0)
    col_id = lax.broadcasted_iota(jnp.int32, (cols, LANES), 1)
    near = jnp.abs(col_id - row_id) <= HALO

    row8 = lax.broadcasted_iota(jnp.int32, (8, chans), 0)

    def filter_rows(c_ref, e_ref, count, first):
        def filter_row(r, carry):
            xc = c_ref[r]
            xe = e_ref[r]
            rhs_c = jnp.concatenate([xc, xc], axis=0)
            lt = xe[cols - 8 :].astype(jnp.float32)
            rt = xe[:8].astype(jnp.float32)
            left = [
                jnp.where(row8 < HALO - d, pltpu.roll(lt, HALO - d, 0), 0.0) for d in range(HALO)
            ]
            right = [
                jnp.where(row8 >= HALO + e, pltpu.roll(rt, (HALO + e) % 8, 0), 0.0)
                for e in range(HALO)
            ]
            centred = tap_u[:, first + r]
            main = []
            for k in range(basis):
                u = centred[k : k + 1]
                u_hi = u.astype(jnp.bfloat16).astype(jnp.float32)
                w_hi = rolled(u_hi, cols)
                w_lo = rolled(u - u_hi, cols)
                main.append(
                    jnp.concatenate(
                        [jnp.where(near, w_hi, 0.0), jnp.where(near, w_lo, 0.0)], axis=1
                    ).astype(jnp.bfloat16)
                )
            y = jnp.dot(jnp.concatenate(main, axis=0), rhs_c, preferred_element_type=jnp.float32)
            for k in range(basis):
                u = centred[k : k + 1]

                def tap(d):
                    lane = (d - HALO) % LANES
                    return jnp.broadcast_to(u[:, lane : lane + 1], (8, chans))

                top = sum(tap(d) * left[d] for d in range(HALO))
                bottom = sum(tap(2 * HALO - e) * right[e] for e in range(HALO))
                v = y[k * cols : (k + 1) * cols]
                v = jnp.concatenate([v[:8] + top, v[8 : cols - 8], v[cols - 8 :] + bottom], axis=0)
                f_ref[k, first + r] = v.astype(jnp.bfloat16).astype(jnp.float32)
            return carry

        lax.fori_loop(0, count, filter_row, 0)

    def zero_rows(first):
        f_ref[:, pl.ds(first, HALO)] = jnp.zeros((basis, HALO, cols, chans), jnp.float32)

    for n in (0, 1):
        loads[n].wait()
    taps_count = tap_v.shape[0]
    shift = lax.rem(total_rows - (lat * out_rows - HALO) + total_rows, total_rows)
    for k in range(basis):
        a = tap_v[:, k, :]
        a = jnp.concatenate([a, jnp.zeros((2 * 8 - taps_count, total_rows), jnp.float32)], axis=0)
        a = pltpu.roll(a, shift, 1)[:, :LANES]
        a = jnp.transpose(a)
        a = jnp.concatenate([a, jnp.zeros((LANES, LANES - 2 * 8), jnp.float32)], axis=1)
        tap_u[k] = pltpu.roll(a, LANES - HALO, 1)[:ext_rows]
    for c in h_side:
        c.wait_recv()
    filter_rows(fields_ref, own_h, out_rows, HALO)

    loads[5].wait()

    def polar_rows(pole):
        pol.wait_recv()
        upper = col_id >= row_id
        for k in range(basis):
            for p in range(polar_count):
                a = cyc_v[k, pl.ds(pole * polar_count + p, 1), :].astype(jnp.float32)
                ra = rolled(a[:, :LANES], cols)
                rb = rolled(a[:, LANES:], cols)
                circ_t = jnp.concatenate(
                    [jnp.where(upper, ra, rb), jnp.where(upper, rb, ra)], axis=0
                )
                circ = jnp.transpose(circ_t).astype(jnp.bfloat16)
                g = jnp.concatenate([fields_ref[slot + p], polar_o[p]], axis=0)
                y = jnp.dot(circ, g, preferred_element_type=jnp.float32)
                f_ref[k, HALO + slot + p] = y.astype(jnp.bfloat16).astype(jnp.float32)

    @pl.when(lat == 0)
    def _():
        polar_rows(0)

    @pl.when(lat == last)
    def _():
        polar_rows(1)

    for n in (2, 3, 4, 6):
        loads[n].wait()
    base_row = lat * out_rows
    lw_all = lat_v[...].astype(jnp.float32)
    terms = []
    for i in range(out_rows):
        begin = start_s[i]
        width = width_s[i]
        row_terms = []
        for t in range(band_len):
            source = begin + t
            ok = (t < width) & (source >= 0) & (source < total_rows)
            r = jnp.clip(source - base_row + HALO, 0, ext_rows - 1)
            row_terms.append((ok, r))
        terms.append(row_terms)

    def weight(i, k, t, keep):
        ok, r = terms[i][t]
        return jnp.where(ok & keep(r), lw_all[t, k : k + 1, i : i + 1], 0.0)

    def own(r):
        return (r >= HALO) & (r < HALO + out_rows)

    for i in range(out_rows):
        for k in range(basis):
            acc = jnp.zeros((cols, chans), jnp.float32)
            for t in range(band_len):
                r = jnp.clip(terms[i][t][1], HALO, HALO + out_rows - 1)
                acc = acc + weight(i, k, t, own) * f_ref[k, r]
            acc_ref[i, k] = acc

    def finish(rows, steps, keep):
        for i in rows:
            for k in range(basis):
                acc = acc_ref[i, k]
                for t in steps(i):
                    acc = acc + weight(i, k, t, keep) * f_ref[k, terms[i][t][1]]
                h_ref[i, :, k * chans : (k + 1) * chans] = acc.astype(jnp.bfloat16)
        first, count = rows[0], len(rows)
        flat = (count * cols, chans)
        mixed = jnp.dot(
            h_ref[pl.ds(first, count)].reshape(count * cols, basis * chans), mix_ref[...],
            preferred_element_type=jnp.float32,
        )
        own_rows = fields_ref[pl.ds(first, count)].astype(jnp.float32).reshape(flat)
        out_ref[pl.ds(first, count)] = (own_rows + mixed).astype(out_ref.dtype).reshape(
            (count, cols, chans)
        )

    half = out_rows // 2

    def top_half():
        @pl.when(has_down)
        def _():
            c_up.wait_recv()
            for c in h_up:
                c.wait_recv()
            filter_rows(top_c, top_h, HALO, 0)

        @pl.when(lat == 0)
        def _():
            zero_rows(0)

        finish(list(range(half)), lambda i: range(0, HALO - i), lambda r: r < HALO)

    def bottom_half():
        @pl.when(has_up)
        def _():
            c_dn.wait_recv()
            for c in h_dn:
                c.wait_recv()
            filter_rows(bot_c, bot_h, HALO, HALO + out_rows)

        @pl.when(lat == last)
        def _():
            zero_rows(HALO + out_rows)

        finish(
            list(range(half, out_rows)),
            lambda i: range(out_rows + 1 - i, band_len),
            lambda r: r >= HALO + out_rows,
        )

    far_above = lax.rem(lat, X_CHIPS) == 0

    @pl.when(jnp.logical_not(far_above))
    def _():
        top_half()
        bottom_half()

    @pl.when(far_above)
    def _():
        bottom_half()
        top_half()

    for c in h_side:
        c.wait_send()

    @pl.when(has_up)
    def _():
        c_up.wait_send()
        for c in h_up:
            c.wait_send()

    @pl.when(has_down)
    def _():
        c_dn.wait_send()
        for c in h_dn:
            c.wait_send()

    @pl.when(is_polar)
    def _():
        pol.wait_send()


def shards(fields, lon_taps, lat_taps, cycle_taps, band_start, band_width, mixing):
    row_count, col_count, chan_count = fields.shape
    basis_count = lon_taps.shape[1]
    taps_count = lon_taps.shape[2]
    reach_cells = (taps_count - 1) // 2
    band_len = lat_taps.shape[2]
    polar_rows = row_count // 2
    lat_count = lax.axis_size("lat")
    lon_count = lax.axis_size("lon")
    assert lon_count == 2 and reach_cells == HALO
    cycle_len = lon_count * col_count
    lat_pos = lax.axis_index("lat")
    ext_rows = row_count + 2 * HALO
    total_rows = lat_count * row_count

    mix_flat = mixing.reshape(basis_count * chan_count, chan_count)
    lon_t = jnp.transpose(lon_taps, (2, 1, 0))
    lat_t = jnp.transpose(lat_taps, (2, 1, 0))

    hbm = pl.BlockSpec(memory_space=pl.ANY)
    kernel = functools.partial(
        conv_kernel, basis_count, row_count, band_len, polar_rows, total_rows
    )
    halo_block = pltpu.VMEM((HALO, col_count, chan_count), fields.dtype)
    return copy_out(pl.pallas_call(
        kernel,
        out_shape=jax.ShapeDtypeStruct(fields.shape, fields.dtype),
        in_specs=[hbm] * 6 + [pl.BlockSpec(memory_space=pltpu.HBM)],
        out_specs=pl.BlockSpec(memory_space=pltpu.VMEM),
        scratch_shapes=[
            pltpu.SMEM(band_start.shape, band_start.dtype),
            pltpu.SMEM(band_width.shape, band_width.dtype),
            pltpu.VMEM(lat_t.shape, lat_t.dtype),
            pltpu.VMEM(lon_t.shape, lon_t.dtype),
            pltpu.VMEM((basis_count, ext_rows, LANES), jnp.float32),
            pltpu.VMEM(cycle_taps.shape, cycle_taps.dtype),
            pltpu.VMEM(fields.shape, fields.dtype),
            pltpu.VMEM(mix_flat.shape, mix_flat.dtype),
            halo_block,
            halo_block,
            halo_block,
            halo_block,
            pltpu.VMEM(fields.shape, fields.dtype),
            pltpu.VMEM((polar_rows, col_count, chan_count), fields.dtype),
            pltpu.VMEM((basis_count, ext_rows, col_count, chan_count), jnp.float32),
            pltpu.VMEM((row_count, basis_count, col_count, chan_count), jnp.float32),
            pltpu.VMEM((row_count, col_count, basis_count * chan_count), jnp.bfloat16),
            pltpu.SemaphoreType.DMA((9,)),
            pltpu.SemaphoreType.DMA((9,)),
            pltpu.SemaphoreType.DMA((7,)),
        ],
        compiler_params=pltpu.CompilerParams(
            vmem_limit_bytes=67043328, collective_id=0, has_side_effects=True
        ),
    )(band_start, band_width, lat_t, lon_t, cycle_taps, fields, mix_flat))


def copy_out(block):
    pieces = 4
    step = block.shape[0] // pieces

    def body(src, dst, stage, sem_in, sem_out):
        ins = [
            pltpu.make_async_copy(src.at[pl.ds(n * step, step)], stage.at[pl.ds(n * step, step)], sem_in.at[n])
            for n in range(pieces)
        ]
        outs = [
            pltpu.make_async_copy(stage.at[pl.ds(n * step, step)], dst.at[pl.ds(n * step, step)], sem_out.at[n])
            for n in range(pieces)
        ]
        for c in ins:
            c.start()
        for c_in, c_out in zip(ins, outs):
            c_in.wait()
            c_out.start()
        for c in outs:
            c.wait()

    hbm = pl.BlockSpec(memory_space=pl.ANY)
    return pl.pallas_call(
        body,
        out_shape=jax.ShapeDtypeStruct(block.shape, block.dtype),
        in_specs=[hbm],
        out_specs=hbm,
        scratch_shapes=[
            pltpu.VMEM(block.shape, block.dtype),
            pltpu.SemaphoreType.DMA((pieces,)),
            pltpu.SemaphoreType.DMA((pieces,)),
        ],
    )(block)


def solution(mesh):
    in_specs = (
        P(("ens", "lat"), "lon", None),
        P(),
        P("lat", None, None),
        P(),
        P("lat"),
        P("lat"),
        P(),
    )
    out_specs = P(("ens", "lat"), "lon", None)
    return jax.shard_map(shards, mesh=mesh, in_specs=in_specs, out_specs=out_specs, check_vma=False)
```

```python
import functools

import jax
import jax.numpy as jnp
from jax import lax
from jax.experimental import pallas as pl
from jax.experimental.pallas import tpu as pltpu
from jax.sharding import PartitionSpec as P

HALO = 4
LANES = 128
EDGE = 16
X_CHIPS = 4
MESH = pl.DeviceIdType.MESH


def rolled(vec, rows):
    return pltpu.roll(jnp.broadcast_to(vec, (rows, LANES)), 0, 1, stride=1, stride_axis=0)


def conv_kernel(basis, out_rows, band_len, polar_count, total_rows,
                start_hbm, width_hbm, lat_hbm, lon_hbm, cyc_hbm, fields_hbm, mix_hbm, out_ref,
                start_s, width_s, lat_v, tap_v, tap_u, cyc_v, fields_ref, mix_ref,
                top_c, bot_c, top_h, bot_h, own_h, polar_o, f_ref, acc_ref, h_ref,
                send_sem, recv_sem, load_sem):
    cols = out_ref.shape[1]
    chans = out_ref.shape[2]
    ext_rows = out_rows + 2 * HALO
    lat = lax.axis_index("lat")
    loads = [
        pltpu.make_async_copy(fields_hbm, fields_ref, load_sem.at[0]),
        pltpu.make_async_copy(lon_hbm, tap_v, load_sem.at[1]),
        pltpu.make_async_copy(start_hbm, start_s, load_sem.at[2]),
        pltpu.make_async_copy(width_hbm, width_s, load_sem.at[3]),
        pltpu.make_async_copy(lat_hbm, lat_v, load_sem.at[4]),
        pltpu.make_async_copy(cyc_hbm, cyc_v, load_sem.at[5]),
        pltpu.make_async_copy(mix_hbm, mix_ref, load_sem.at[6]),
    ]
    for c in loads:
        c.start()
    lon = lax.axis_index("lon")
    last = lax.axis_size("lat") - 1
    has_up = lat < last
    has_down = lat > 0
    is_polar = (lat == 0) | (lat == last)
    slot = jnp.minimum(lat, 1) * (out_rows - polar_count)
    up = jnp.minimum(lat + 1, last)
    down = jnp.maximum(lat - 1, 0)
    side = 1 - lon

    middle = pl.ds(EDGE, cols - 2 * EDGE)
    for buf in (top_h, bot_h, own_h):
        buf[:, middle] = jnp.zeros((buf.shape[0], cols - 2 * EDGE, chans), buf.dtype)

    barrier = pltpu.get_barrier_semaphore()

    def greet(where):
        pl.semaphore_signal(barrier, 1, device_id=where, device_id_type=MESH)

    greet({"lat": lat, "lon": side})

    @pl.when(has_up)
    def _():
        greet({"lat": up, "lon": lon})
        greet({"lat": up, "lon": side})

    @pl.when(has_down)
    def _():
        greet({"lat": down, "lon": lon})
        greet({"lat": down, "lon": side})

    pl.semaphore_wait(barrier, 1 + 2 * (has_up.astype(jnp.int32) + has_down.astype(jnp.int32)))

    def copy(n, src, dst, where):
        return pltpu.make_async_remote_copy(
            src_ref=src, dst_ref=dst, send_sem=send_sem.at[n], recv_sem=recv_sem.at[n],
            device_id=where, device_id_type=MESH)

    lo_rows = pl.ds(0, HALO)
    hi_rows = pl.ds(out_rows - HALO, HALO)
    first_cols = pl.ds(0, EDGE)
    last_cols = pl.ds(cols - EDGE, EDGE)
    c_up = [
        copy(9 + j, fields_hbm.at[pl.ds(out_rows - HALO + j, 1)], top_c.at[pl.ds(j, 1)],
             {"lat": up, "lon": lon})
        for j in range(HALO)
    ]
    c_dn = [
        copy(9 + HALO + j, fields_hbm.at[pl.ds(j, 1)], bot_c.at[pl.ds(j, 1)],
             {"lat": down, "lon": lon})
        for j in range(HALO)
    ]
    h_up = [
        copy(2, fields_hbm.at[hi_rows, first_cols], top_h.at[:, first_cols], {"lat": up, "lon": side}),
        copy(3, fields_hbm.at[hi_rows, last_cols], top_h.at[:, last_cols], {"lat": up, "lon": side}),
    ]
    h_dn = [
        copy(4, fields_hbm.at[lo_rows, first_cols], bot_h.at[:, first_cols], {"lat": down, "lon": side}),
        copy(5, fields_hbm.at[lo_rows, last_cols], bot_h.at[:, last_cols], {"lat": down, "lon": side}),
    ]
    h_side = [
        copy(6, fields_hbm.at[:, first_cols], own_h.at[:, first_cols], {"lat": lat, "lon": side}),
        copy(7, fields_hbm.at[:, last_cols], own_h.at[:, last_cols], {"lat": lat, "lon": side}),
    ]
    pol = copy(8, fields_hbm.at[pl.ds(slot, polar_count)], polar_o, {"lat": lat, "lon": side})

    for c in h_side:
        c.start()

    @pl.when(has_up)
    def _():
        for c in c_up:
            c.start()
        for c in h_up:
            c.start()

    @pl.when(has_down)
    def _():
        for c in c_dn:
            c.start()
        for c in h_dn:
            c.start()

    @pl.when(is_polar)
    def _():
        pol.start()

    row_id = lax.broadcasted_iota(jnp.int32, (cols, LANES), 0)
    col_id = lax.broadcasted_iota(jnp.int32, (cols, LANES), 1)
    near = jnp.abs(col_id - row_id) <= HALO

    row8 = lax.broadcasted_iota(jnp.int32, (8, chans), 0)

    def filter_rows(c_ref, e_ref, count, first, arrivals=None):
        def filter_row(r, carry):
            xc = c_ref[r]
            xe = e_ref[r]
            rhs_c = jnp.concatenate([xc, xc], axis=0)
            lt = xe[cols - 8 :].astype(jnp.float32)
            rt = xe[:8].astype(jnp.float32)
            left = [
                jnp.where(row8 < HALO - d, pltpu.roll(lt, HALO - d, 0), 0.0) for d in range(HALO)
            ]
            right = [
                jnp.where(row8 >= HALO + e, pltpu.roll(rt, (HALO + e) % 8, 0), 0.0)
                for e in range(HALO)
            ]
            centred = tap_u[:, first + r]
            main = []
            for k in range(basis):
                u = centred[k : k + 1]
                u_hi = u.astype(jnp.bfloat16).astype(jnp.float32)
                w_hi = rolled(u_hi, cols)
                w_lo = rolled(u - u_hi, cols)
                main.append(
                    jnp.concatenate(
                        [jnp.where(near, w_hi, 0.0), jnp.where(near, w_lo, 0.0)], axis=1
                    ).astype(jnp.bfloat16)
                )
            y = jnp.dot(jnp.concatenate(main, axis=0), rhs_c, preferred_element_type=jnp.float32)
            for k in range(basis):
                u = centred[k : k + 1]

                def tap(d):
                    lane = (d - HALO) % LANES
                    return jnp.broadcast_to(u[:, lane : lane + 1], (8, chans))

                top = sum(tap(d) * left[d] for d in range(HALO))
                bottom = sum(tap(2 * HALO - e) * right[e] for e in range(HALO))
                v = y[k * cols : (k + 1) * cols]
                v = jnp.concatenate([v[:8] + top, v[8 : cols - 8], v[cols - 8 :] + bottom], axis=0)
                f_ref[k, first + r] = v.astype(jnp.bfloat16).astype(jnp.float32)
            return carry

        if arrivals is None:
            lax.fori_loop(0, count, filter_row, 0)
        else:
            for j in range(count):
                arrivals[j].wait_recv()
                filter_row(j, 0)

    def zero_rows(first):
        f_ref[:, pl.ds(first, HALO)] = jnp.zeros((basis, HALO, cols, chans), jnp.float32)

    for n in (0, 1):
        loads[n].wait()
    taps_count = tap_v.shape[0]
    shift = lax.rem(total_rows - (lat * out_rows - HALO) + total_rows, total_rows)
    for k in range(basis):
        a = tap_v[:, k, :]
        a = jnp.concatenate([a, jnp.zeros((2 * 8 - taps_count, total_rows), jnp.float32)], axis=0)
        a = pltpu.roll(a, shift, 1)[:, :LANES]
        a = jnp.transpose(a)
        a = jnp.concatenate([a, jnp.zeros((LANES, LANES - 2 * 8), jnp.float32)], axis=1)
        tap_u[k] = pltpu.roll(a, LANES - HALO, 1)[:ext_rows]
    for c in h_side:
        c.wait_recv()
    filter_rows(fields_ref, own_h, out_rows, HALO)

    loads[5].wait()

    def polar_rows(pole):
        pol.wait_recv()
        upper = col_id >= row_id
        for k in range(basis):
            for p in range(polar_count):
                a = cyc_v[k, pl.ds(pole * polar_count + p, 1), :].astype(jnp.float32)
                ra = rolled(a[:, :LANES], cols)
                rb = rolled(a[:, LANES:], cols)
                circ_t = jnp.concatenate(
                    [jnp.where(upper, ra, rb), jnp.where(upper, rb, ra)], axis=0
                )
                circ = jnp.transpose(circ_t).astype(jnp.bfloat16)
                g = jnp.concatenate([fields_ref[slot + p], polar_o[p]], axis=0)
                y = jnp.dot(circ, g, preferred_element_type=jnp.float32)
                f_ref[k, HALO + slot + p] = y.astype(jnp.bfloat16).astype(jnp.float32)

    @pl.when(lat == 0)
    def _():
        polar_rows(0)

    @pl.when(lat == last)
    def _():
        polar_rows(1)

    for n in (2, 3, 4, 6):
        loads[n].wait()
    base_row = lat * out_rows
    lw_all = lat_v[...].astype(jnp.float32)
    terms = []
    for i in range(out_rows):
        begin = start_s[i]
        width = width_s[i]
        row_terms = []
        for t in range(band_len):
            source = begin + t
            ok = (t < width) & (source >= 0) & (source < total_rows)
            r = jnp.clip(source - base_row + HALO, 0, ext_rows - 1)
            row_terms.append((ok, r))
        terms.append(row_terms)

    def weight(i, k, t, keep):
        ok, r = terms[i][t]
        return jnp.where(ok & keep(r), lw_all[t, k : k + 1, i : i + 1], 0.0)

    def own(r):
        return (r >= HALO) & (r < HALO + out_rows)

    for i in range(out_rows):
        for k in range(basis):
            acc = jnp.zeros((cols, chans), jnp.float32)
            for t in range(band_len):
                r = jnp.clip(terms[i][t][1], HALO, HALO + out_rows - 1)
                acc = acc + weight(i, k, t, own) * f_ref[k, r]
            acc_ref[i, k] = acc

    def finish(rows, steps, keep):
        for i in rows:
            for k in range(basis):
                acc = acc_ref[i, k]
                for t in steps(i):
                    acc = acc + weight(i, k, t, keep) * f_ref[k, terms[i][t][1]]
                h_ref[i, :, k * chans : (k + 1) * chans] = acc.astype(jnp.bfloat16)
        first, count = rows[0], len(rows)
        flat = (count * cols, chans)
        mixed = jnp.dot(
            h_ref[pl.ds(first, count)].reshape(count * cols, basis * chans), mix_ref[...],
            preferred_element_type=jnp.float32,
        )
        own_rows = fields_ref[pl.ds(first, count)].astype(jnp.float32).reshape(flat)
        out_ref[pl.ds(first, count)] = (own_rows + mixed).astype(out_ref.dtype).reshape(
            (count, cols, chans)
        )

    half = out_rows // 2

    def top_half():
        @pl.when(has_down)
        def _():
            for c in h_up:
                c.wait_recv()
            filter_rows(top_c, top_h, HALO, 0, c_up)

        @pl.when(lat == 0)
        def _():
            zero_rows(0)

        finish(list(range(half)), lambda i: range(0, HALO - i), lambda r: r < HALO)

    def bottom_half():
        @pl.when(has_up)
        def _():
            for c in h_dn:
                c.wait_recv()
            filter_rows(bot_c, bot_h, HALO, HALO + out_rows, c_dn)

        @pl.when(lat == last)
        def _():
            zero_rows(HALO + out_rows)

        finish(
            list(range(half, out_rows)),
            lambda i: range(out_rows + 1 - i, band_len),
            lambda r: r >= HALO + out_rows,
        )

    far_above = lax.rem(lat, X_CHIPS) == 0

    @pl.when(jnp.logical_not(far_above))
    def _():
        top_half()
        bottom_half()

    @pl.when(far_above)
    def _():
        bottom_half()
        top_half()

    for c in h_side:
        c.wait_send()

    @pl.when(has_up)
    def _():
        for c in c_up:
            c.wait_send()
        for c in h_up:
            c.wait_send()

    @pl.when(has_down)
    def _():
        for c in c_dn:
            c.wait_send()
        for c in h_dn:
            c.wait_send()

    @pl.when(is_polar)
    def _():
        pol.wait_send()


def shards(fields, lon_taps, lat_taps, cycle_taps, band_start, band_width, mixing):
    row_count, col_count, chan_count = fields.shape
    basis_count = lon_taps.shape[1]
    taps_count = lon_taps.shape[2]
    reach_cells = (taps_count - 1) // 2
    band_len = lat_taps.shape[2]
    polar_rows = row_count // 2
    lat_count = lax.axis_size("lat")
    lon_count = lax.axis_size("lon")
    assert lon_count == 2 and reach_cells == HALO
    cycle_len = lon_count * col_count
    lat_pos = lax.axis_index("lat")
    ext_rows = row_count + 2 * HALO
    total_rows = lat_count * row_count

    mix_flat = mixing.reshape(basis_count * chan_count, chan_count)
    lon_t = jnp.transpose(lon_taps, (2, 1, 0))
    lat_t = jnp.transpose(lat_taps, (2, 1, 0))

    hbm = pl.BlockSpec(memory_space=pl.ANY)
    kernel = functools.partial(
        conv_kernel, basis_count, row_count, band_len, polar_rows, total_rows
    )
    halo_block = pltpu.VMEM((HALO, col_count, chan_count), fields.dtype)
    return copy_out(pl.pallas_call(
        kernel,
        out_shape=jax.ShapeDtypeStruct(fields.shape, fields.dtype),
        in_specs=[hbm] * 6 + [pl.BlockSpec(memory_space=pltpu.HBM)],
        out_specs=pl.BlockSpec(memory_space=pltpu.VMEM),
        scratch_shapes=[
            pltpu.SMEM(band_start.shape, band_start.dtype),
            pltpu.SMEM(band_width.shape, band_width.dtype),
            pltpu.VMEM(lat_t.shape, lat_t.dtype),
            pltpu.VMEM(lon_t.shape, lon_t.dtype),
            pltpu.VMEM((basis_count, ext_rows, LANES), jnp.float32),
            pltpu.VMEM(cycle_taps.shape, cycle_taps.dtype),
            pltpu.VMEM(fields.shape, fields.dtype),
            pltpu.VMEM(mix_flat.shape, mix_flat.dtype),
            halo_block,
            halo_block,
            halo_block,
            halo_block,
            pltpu.VMEM(fields.shape, fields.dtype),
            pltpu.VMEM((polar_rows, col_count, chan_count), fields.dtype),
            pltpu.VMEM((basis_count, ext_rows, col_count, chan_count), jnp.float32),
            pltpu.VMEM((row_count, basis_count, col_count, chan_count), jnp.float32),
            pltpu.VMEM((row_count, col_count, basis_count * chan_count), jnp.bfloat16),
            pltpu.SemaphoreType.DMA((9 + 2 * HALO,)),
            pltpu.SemaphoreType.DMA((9 + 2 * HALO,)),
            pltpu.SemaphoreType.DMA((7,)),
        ],
        compiler_params=pltpu.CompilerParams(
            vmem_limit_bytes=67043328, collective_id=0, has_side_effects=True
        ),
    )(band_start, band_width, lat_t, lon_t, cycle_taps, fields, mix_flat))


def copy_out(block):
    pieces = 4
    step = block.shape[0] // pieces

    def body(src, dst, stage, sem_in, sem_out):
        ins = [
            pltpu.make_async_copy(src.at[pl.ds(n * step, step)], stage.at[pl.ds(n * step, step)], sem_in.at[n])
            for n in range(pieces)
        ]
        outs = [
            pltpu.make_async_copy(stage.at[pl.ds(n * step, step)], dst.at[pl.ds(n * step, step)], sem_out.at[n])
            for n in range(pieces)
        ]
        for c in ins:
            c.start()
        for c_in, c_out in zip(ins, outs):
            c_in.wait()
            c_out.start()
        for c in outs:
            c.wait()

    hbm = pl.BlockSpec(memory_space=pl.ANY)
    return pl.pallas_call(
        body,
        out_shape=jax.ShapeDtypeStruct(block.shape, block.dtype),
        in_specs=[hbm],
        out_specs=hbm,
        scratch_shapes=[
            pltpu.VMEM(block.shape, block.dtype),
            pltpu.SemaphoreType.DMA((pieces,)),
            pltpu.SemaphoreType.DMA((pieces,)),
        ],
    )(block)


def solution(mesh):
    in_specs = (
        P(("ens", "lat"), "lon", None),
        P(),
        P("lat", None, None),
        P(),
        P("lat"),
        P("lat"),
        P(),
    )
    out_specs = P(("ens", "lat"), "lon", None)
    return jax.shard_map(shards, mesh=mesh, in_specs=in_specs, out_specs=out_specs, check_vma=False)
```

```python
import functools

import jax
import jax.numpy as jnp
from jax import lax
from jax.experimental import pallas as pl
from jax.experimental.pallas import tpu as pltpu
from jax.sharding import PartitionSpec as P

HALO = 4
LANES = 128
EDGE = 16
X_CHIPS = 4
MESH = pl.DeviceIdType.MESH


def rolled(vec, rows):
    return pltpu.roll(jnp.broadcast_to(vec, (rows, LANES)), 0, 1, stride=1, stride_axis=0)


def conv_kernel(basis, out_rows, band_len, polar_count, total_rows,
                start_hbm, width_hbm, lat_hbm, lon_hbm, cyc_hbm, fields_hbm, mix_hbm, out_ref,
                start_s, width_s, lat_v, tap_v, tap_u, cyc_v, fields_ref, mix_ref,
                top_c, bot_c, top_h, bot_h, own_h, polar_o, f_ref, acc_ref, h_ref,
                send_sem, recv_sem, load_sem):
    cols = out_ref.shape[1]
    chans = out_ref.shape[2]
    ext_rows = out_rows + 2 * HALO
    lat = lax.axis_index("lat")
    loads = [
        pltpu.make_async_copy(fields_hbm, fields_ref, load_sem.at[0]),
        pltpu.make_async_copy(lon_hbm, tap_v, load_sem.at[1]),
        pltpu.make_async_copy(start_hbm, start_s, load_sem.at[2]),
        pltpu.make_async_copy(width_hbm, width_s, load_sem.at[3]),
        pltpu.make_async_copy(lat_hbm, lat_v, load_sem.at[4]),
        pltpu.make_async_copy(cyc_hbm, cyc_v, load_sem.at[5]),
        pltpu.make_async_copy(mix_hbm, mix_ref, load_sem.at[6]),
    ]
    for c in loads:
        c.start()
    lon = lax.axis_index("lon")
    last = lax.axis_size("lat") - 1
    has_up = lat < last
    has_down = lat > 0
    is_polar = (lat == 0) | (lat == last)
    slot = jnp.minimum(lat, 1) * (out_rows - polar_count)
    up = jnp.minimum(lat + 1, last)
    down = jnp.maximum(lat - 1, 0)
    side = 1 - lon

    middle = pl.ds(EDGE, cols - 2 * EDGE)
    for buf in (top_h, bot_h, own_h):
        buf[:, middle] = jnp.zeros((buf.shape[0], cols - 2 * EDGE, chans), buf.dtype)

    barrier = pltpu.get_barrier_semaphore()

    def greet(where):
        pl.semaphore_signal(barrier, 1, device_id=where, device_id_type=MESH)

    greet({"lat": lat, "lon": side})

    @pl.when(has_up)
    def _():
        greet({"lat": up, "lon": lon})
        greet({"lat": up, "lon": side})

    @pl.when(has_down)
    def _():
        greet({"lat": down, "lon": lon})
        greet({"lat": down, "lon": side})

    pl.semaphore_wait(barrier, 1 + 2 * (has_up.astype(jnp.int32) + has_down.astype(jnp.int32)))

    def copy(n, src, dst, where):
        return pltpu.make_async_remote_copy(
            src_ref=src, dst_ref=dst, send_sem=send_sem.at[n], recv_sem=recv_sem.at[n],
            device_id=where, device_id_type=MESH)

    lo_rows = pl.ds(0, HALO)
    hi_rows = pl.ds(out_rows - HALO, HALO)
    first_cols = pl.ds(0, EDGE)
    last_cols = pl.ds(cols - EDGE, EDGE)
    c_up = copy(0, fields_hbm.at[hi_rows], top_c, {"lat": up, "lon": lon})
    c_dn = copy(1, fields_hbm.at[lo_rows], bot_c, {"lat": down, "lon": lon})
    h_up = [
        copy(2, fields_hbm.at[hi_rows, first_cols], top_h.at[:, first_cols], {"lat": up, "lon": side}),
        copy(3, fields_hbm.at[hi_rows, last_cols], top_h.at[:, last_cols], {"lat": up, "lon": side}),
    ]
    h_dn = [
        copy(4, fields_hbm.at[lo_rows, first_cols], bot_h.at[:, first_cols], {"lat": down, "lon": side}),
        copy(5, fields_hbm.at[lo_rows, last_cols], bot_h.at[:, last_cols], {"lat": down, "lon": side}),
    ]
    h_side = [
        copy(6, fields_hbm.at[:, first_cols], own_h.at[:, first_cols], {"lat": lat, "lon": side}),
        copy(7, fields_hbm.at[:, last_cols], own_h.at[:, last_cols], {"lat": lat, "lon": side}),
    ]
    pol = copy(8, fields_hbm.at[pl.ds(slot, polar_count)], polar_o, {"lat": lat, "lon": side})

    for c in h_side:
        c.start()

    @pl.when(has_up)
    def _():
        c_up.start()
        for c in h_up:
            c.start()

    @pl.when(has_down)
    def _():
        c_dn.start()
        for c in h_dn:
            c.start()

    @pl.when(is_polar)
    def _():
        pol.start()

    row_id = lax.broadcasted_iota(jnp.int32, (cols, LANES), 0)
    col_id = lax.broadcasted_iota(jnp.int32, (cols, LANES), 1)
    near = jnp.abs(col_id - row_id) <= HALO

    near_edge = jnp.concatenate([near[:8], near[cols - 8 :]], axis=0)

    def filter_rows(c_ref, e_ref, count, first):
        def filter_row(r, carry):
            xc = c_ref[r]
            xe = e_ref[r]
            rhs_c = jnp.concatenate([xc, xc], axis=0)
            rhs_e = jnp.concatenate([xe, xe], axis=0)
            centred = tap_u[:, first + r]
            main, corr = [], []
            for k in range(basis):
                u = centred[k : k + 1]
                u_hi = u.astype(jnp.bfloat16).astype(jnp.float32)
                w_hi = rolled(u_hi, cols)
                w_lo = rolled(u - u_hi, cols)
                main.append(
                    jnp.concatenate(
                        [jnp.where(near, w_hi, 0.0), jnp.where(near, w_lo, 0.0)], axis=1
                    ).astype(jnp.bfloat16)
                )
                e_hi = jnp.concatenate([w_hi[:8], w_hi[cols - 8 :]], axis=0)
                e_lo = jnp.concatenate([w_lo[:8], w_lo[cols - 8 :]], axis=0)
                corr.append(
                    jnp.concatenate(
                        [jnp.where(near_edge, 0.0, e_hi), jnp.where(near_edge, 0.0, e_lo)], axis=1
                    ).astype(jnp.bfloat16)
                )
            y = jnp.dot(jnp.concatenate(main, axis=0), rhs_c, preferred_element_type=jnp.float32)
            yc = jnp.dot(jnp.concatenate(corr, axis=0), rhs_e, preferred_element_type=jnp.float32)
            for k in range(basis):
                v = y[k * cols : (k + 1) * cols]
                c = yc[k * 16 : (k + 1) * 16]
                v = jnp.concatenate([v[:8] + c[:8], v[8 : cols - 8], v[cols - 8 :] + c[8:]], axis=0)
                f_ref[k, first + r] = v.astype(jnp.bfloat16).astype(jnp.float32)
            return carry

        lax.fori_loop(0, count, filter_row, 0)

    def zero_rows(first):
        f_ref[:, pl.ds(first, HALO)] = jnp.zeros((basis, HALO, cols, chans), jnp.float32)

    for n in (0, 1):
        loads[n].wait()
    taps_count = tap_v.shape[0]
    shift = lax.rem(total_rows - (lat * out_rows - HALO) + total_rows, total_rows)
    for k in range(basis):
        a = tap_v[:, k, :]
        a = jnp.concatenate([a, jnp.zeros((2 * 8 - taps_count, total_rows), jnp.float32)], axis=0)
        a = pltpu.roll(a, shift, 1)[:, :LANES]
        a = jnp.transpose(a)
        a = jnp.concatenate([a, jnp.zeros((LANES, LANES - 2 * 8), jnp.float32)], axis=1)
        tap_u[k] = pltpu.roll(a, LANES - HALO, 1)[:ext_rows]
    for c in h_side:
        c.wait_recv()
    filter_rows(fields_ref, own_h, out_rows, HALO)

    loads[5].wait()

    def polar_rows(pole):
        pol.wait_recv()
        upper = col_id >= row_id
        for k in range(basis):
            for p in range(polar_count):
                a = cyc_v[k, pl.ds(pole * polar_count + p, 1), :].astype(jnp.float32)
                ra = rolled(a[:, :LANES], cols)
                rb = rolled(a[:, LANES:], cols)
                circ_t = jnp.concatenate(
                    [jnp.where(upper, ra, rb), jnp.where(upper, rb, ra)], axis=0
                )
                circ = jnp.transpose(circ_t).astype(jnp.bfloat16)
                g = jnp.concatenate([fields_ref[slot + p], polar_o[p]], axis=0)
                y = jnp.dot(circ, g, preferred_element_type=jnp.float32)
                f_ref[k, HALO + slot + p] = y.astype(jnp.bfloat16).astype(jnp.float32)

    @pl.when(lat == 0)
    def _():
        polar_rows(0)

    @pl.when(lat == last)
    def _():
        polar_rows(1)

    for n in (2, 3, 4, 6):
        loads[n].wait()
    base_row = lat * out_rows
    lw_all = lat_v[...].astype(jnp.float32)
    terms = []
    for i in range(out_rows):
        begin = start_s[i]
        width = width_s[i]
        row_terms = []
        for t in range(band_len):
            source = begin + t
            ok = (t < width) & (source >= 0) & (source < total_rows)
            r = jnp.clip(source - base_row + HALO, 0, ext_rows - 1)
            row_terms.append((ok, r))
        terms.append(row_terms)

    def weight(i, k, t, keep):
        ok, r = terms[i][t]
        return jnp.where(ok & keep(r), lw_all[t, k : k + 1, i : i + 1], 0.0)

    def own(r):
        return (r >= HALO) & (r < HALO + out_rows)

    for i in range(out_rows):
        for k in range(basis):
            acc = jnp.zeros((cols, chans), jnp.float32)
            for t in range(band_len):
                r = jnp.clip(terms[i][t][1], HALO, HALO + out_rows - 1)
                acc = acc + weight(i, k, t, own) * f_ref[k, r]
            acc_ref[i, k] = acc

    def finish(rows, steps, keep):
        for i in rows:
            for k in range(basis):
                acc = acc_ref[i, k]
                for t in steps(i):
                    acc = acc + weight(i, k, t, keep) * f_ref[k, terms[i][t][1]]
                h_ref[i, :, k * chans : (k + 1) * chans] = acc.astype(jnp.bfloat16)
        first, count = rows[0], len(rows)
        flat = (count * cols, chans)
        mixed = jnp.dot(
            h_ref[pl.ds(first, count)].reshape(count * cols, basis * chans), mix_ref[...],
            preferred_element_type=jnp.float32,
        )
        out_ref[pl.ds(first, count)] = mixed.reshape((count, cols, chans))

    half = out_rows // 2

    def top_half():
        @pl.when(has_down)
        def _():
            c_up.wait_recv()
            for c in h_up:
                c.wait_recv()
            filter_rows(top_c, top_h, HALO, 0)

        @pl.when(lat == 0)
        def _():
            zero_rows(0)

        finish(list(range(half)), lambda i: range(0, HALO - i), lambda r: r < HALO)

    def bottom_half():
        @pl.when(has_up)
        def _():
            c_dn.wait_recv()
            for c in h_dn:
                c.wait_recv()
            filter_rows(bot_c, bot_h, HALO, HALO + out_rows)

        @pl.when(lat == last)
        def _():
            zero_rows(HALO + out_rows)

        finish(
            list(range(half, out_rows)),
            lambda i: range(out_rows + 1 - i, band_len),
            lambda r: r >= HALO + out_rows,
        )

    far_above = lax.rem(lat, X_CHIPS) == 0

    @pl.when(jnp.logical_not(far_above))
    def _():
        top_half()
        bottom_half()

    @pl.when(far_above)
    def _():
        bottom_half()
        top_half()

    for c in h_side:
        c.wait_send()

    @pl.when(has_up)
    def _():
        c_up.wait_send()
        for c in h_up:
            c.wait_send()

    @pl.when(has_down)
    def _():
        c_dn.wait_send()
        for c in h_dn:
            c.wait_send()

    @pl.when(is_polar)
    def _():
        pol.wait_send()


def shards(fields, lon_taps, lat_taps, cycle_taps, band_start, band_width, mixing):
    row_count, col_count, chan_count = fields.shape
    basis_count = lon_taps.shape[1]
    taps_count = lon_taps.shape[2]
    reach_cells = (taps_count - 1) // 2
    band_len = lat_taps.shape[2]
    polar_rows = row_count // 2
    lat_count = lax.axis_size("lat")
    lon_count = lax.axis_size("lon")
    assert lon_count == 2 and reach_cells == HALO
    cycle_len = lon_count * col_count
    lat_pos = lax.axis_index("lat")
    ext_rows = row_count + 2 * HALO
    total_rows = lat_count * row_count

    mix_flat = mixing.reshape(basis_count * chan_count, chan_count)
    lon_t = jnp.transpose(lon_taps, (2, 1, 0))
    lat_t = jnp.transpose(lat_taps, (2, 1, 0))

    hbm = pl.BlockSpec(memory_space=pl.ANY)
    kernel = functools.partial(
        conv_kernel, basis_count, row_count, band_len, polar_rows, total_rows
    )
    halo_block = pltpu.VMEM((HALO, col_count, chan_count), fields.dtype)
    mixed = pl.pallas_call(
        kernel,
        out_shape=jax.ShapeDtypeStruct(fields.shape, jnp.float32),
        in_specs=[hbm] * 6 + [pl.BlockSpec(memory_space=pltpu.HBM)],
        out_specs=pl.BlockSpec(memory_space=pltpu.VMEM),
        scratch_shapes=[
            pltpu.SMEM(band_start.shape, band_start.dtype),
            pltpu.SMEM(band_width.shape, band_width.dtype),
            pltpu.VMEM(lat_t.shape, lat_t.dtype),
            pltpu.VMEM(lon_t.shape, lon_t.dtype),
            pltpu.VMEM((basis_count, ext_rows, LANES), jnp.float32),
            pltpu.VMEM(cycle_taps.shape, cycle_taps.dtype),
            pltpu.VMEM(fields.shape, fields.dtype),
            pltpu.VMEM(mix_flat.shape, mix_flat.dtype),
            halo_block,
            halo_block,
            halo_block,
            halo_block,
            pltpu.VMEM(fields.shape, fields.dtype),
            pltpu.VMEM((polar_rows, col_count, chan_count), fields.dtype),
            pltpu.VMEM((basis_count, ext_rows, col_count, chan_count), jnp.float32),
            pltpu.VMEM((row_count, basis_count, col_count, chan_count), jnp.float32),
            pltpu.VMEM((row_count, col_count, basis_count * chan_count), jnp.bfloat16),
            pltpu.SemaphoreType.DMA((9,)),
            pltpu.SemaphoreType.DMA((9,)),
            pltpu.SemaphoreType.DMA((7,)),
        ],
        compiler_params=pltpu.CompilerParams(
            vmem_limit_bytes=67043328, collective_id=0, has_side_effects=True
        ),
    )(band_start, band_width, lat_t, lon_t, cycle_taps, fields, mix_flat)
    return (fields.astype(jnp.float32) + mixed).astype(fields.dtype)


def solution(mesh):
    in_specs = (
        P(("ens", "lat"), "lon", None),
        P(),
        P("lat", None, None),
        P(),
        P("lat"),
        P("lat"),
        P(),
    )
    out_specs = P(("ens", "lat"), "lon", None)
    return jax.shard_map(shards, mesh=mesh, in_specs=in_specs, out_specs=out_specs, check_vma=False)
```

```python
import functools

import jax
import jax.numpy as jnp
from jax import lax
from jax.experimental import pallas as pl
from jax.experimental.pallas import tpu as pltpu
from jax.sharding import PartitionSpec as P

HALO = 4
LANES = 128
EDGE = 16
X_CHIPS = 4
MESH = pl.DeviceIdType.MESH


def rolled(vec, rows):
    return pltpu.roll(jnp.broadcast_to(vec, (rows, LANES)), 0, 1, stride=1, stride_axis=0)


def conv_kernel(basis, out_rows, band_len, polar_count, total_rows,
                start_hbm, width_hbm, lat_hbm, lon_hbm, cyc_hbm, fields_hbm, mix_hbm, out_ref,
                start_s, width_s, lat_v, tap_v, tap_u, cyc_v, fields_ref, mix_ref,
                top_c, bot_c, top_h, bot_h, own_h, polar_o, f_ref, acc_ref, h_ref, tm_ref, tc_ref,
                send_sem, recv_sem, load_sem):
    cols = out_ref.shape[1]
    chans = out_ref.shape[2]
    ext_rows = out_rows + 2 * HALO
    lat = lax.axis_index("lat")
    loads = [
        pltpu.make_async_copy(fields_hbm, fields_ref, load_sem.at[0]),
        pltpu.make_async_copy(lon_hbm, tap_v, load_sem.at[1]),
        pltpu.make_async_copy(start_hbm, start_s, load_sem.at[2]),
        pltpu.make_async_copy(width_hbm, width_s, load_sem.at[3]),
        pltpu.make_async_copy(lat_hbm, lat_v, load_sem.at[4]),
        pltpu.make_async_copy(cyc_hbm, cyc_v, load_sem.at[5]),
        pltpu.make_async_copy(mix_hbm, mix_ref, load_sem.at[6]),
    ]
    for c in loads:
        c.start()
    lon = lax.axis_index("lon")
    last = lax.axis_size("lat") - 1
    has_up = lat < last
    has_down = lat > 0
    is_polar = (lat == 0) | (lat == last)
    slot = jnp.minimum(lat, 1) * (out_rows - polar_count)
    up = jnp.minimum(lat + 1, last)
    down = jnp.maximum(lat - 1, 0)
    side = 1 - lon

    middle = pl.ds(EDGE, cols - 2 * EDGE)
    for buf in (top_h, bot_h, own_h):
        buf[:, middle] = jnp.zeros((buf.shape[0], cols - 2 * EDGE, chans), buf.dtype)

    barrier = pltpu.get_barrier_semaphore()

    def greet(where):
        pl.semaphore_signal(barrier, 1, device_id=where, device_id_type=MESH)

    greet({"lat": lat, "lon": side})

    @pl.when(has_up)
    def _():
        greet({"lat": up, "lon": lon})
        greet({"lat": up, "lon": side})

    @pl.when(has_down)
    def _():
        greet({"lat": down, "lon": lon})
        greet({"lat": down, "lon": side})

    pl.semaphore_wait(barrier, 1 + 2 * (has_up.astype(jnp.int32) + has_down.astype(jnp.int32)))

    def copy(n, src, dst, where):
        return pltpu.make_async_remote_copy(
            src_ref=src, dst_ref=dst, send_sem=send_sem.at[n], recv_sem=recv_sem.at[n],
            device_id=where, device_id_type=MESH)

    lo_rows = pl.ds(0, HALO)
    hi_rows = pl.ds(out_rows - HALO, HALO)
    first_cols = pl.ds(0, EDGE)
    last_cols = pl.ds(cols - EDGE, EDGE)
    c_up = copy(0, fields_hbm.at[hi_rows], top_c, {"lat": up, "lon": lon})
    c_dn = copy(1, fields_hbm.at[lo_rows], bot_c, {"lat": down, "lon": lon})
    h_up = [
        copy(2, fields_hbm.at[hi_rows, first_cols], top_h.at[:, first_cols], {"lat": up, "lon": side}),
        copy(3, fields_hbm.at[hi_rows, last_cols], top_h.at[:, last_cols], {"lat": up, "lon": side}),
    ]
    h_dn = [
        copy(4, fields_hbm.at[lo_rows, first_cols], bot_h.at[:, first_cols], {"lat": down, "lon": side}),
        copy(5, fields_hbm.at[lo_rows, last_cols], bot_h.at[:, last_cols], {"lat": down, "lon": side}),
    ]
    h_side = [
        copy(6, fields_hbm.at[:, first_cols], own_h.at[:, first_cols], {"lat": lat, "lon": side}),
        copy(7, fields_hbm.at[:, last_cols], own_h.at[:, last_cols], {"lat": lat, "lon": side}),
    ]
    pol = copy(8, fields_hbm.at[pl.ds(slot, polar_count)], polar_o, {"lat": lat, "lon": side})

    for c in h_side:
        c.start()

    @pl.when(has_up)
    def _():
        c_up.start()
        for c in h_up:
            c.start()

    @pl.when(has_down)
    def _():
        c_dn.start()
        for c in h_dn:
            c.start()

    @pl.when(is_polar)
    def _():
        pol.start()

    row_id = lax.broadcasted_iota(jnp.int32, (cols, LANES), 0)
    col_id = lax.broadcasted_iota(jnp.int32, (cols, LANES), 1)
    near = jnp.abs(col_id - row_id) <= HALO

    near_edge = jnp.concatenate([near[:8], near[cols - 8 :]], axis=0)

    def build(e):
        centred = tap_u[:, e]
        main, corr = [], []
        for k in range(basis):
            u = centred[k : k + 1]
            u_hi = u.astype(jnp.bfloat16).astype(jnp.float32)
            w_hi = rolled(u_hi, cols)
            w_lo = rolled(u - u_hi, cols)
            main.append(
                jnp.concatenate(
                    [jnp.where(near, w_hi, 0.0), jnp.where(near, w_lo, 0.0)], axis=1
                ).astype(jnp.bfloat16)
            )
            e_hi = jnp.concatenate([w_hi[:8], w_hi[cols - 8 :]], axis=0)
            e_lo = jnp.concatenate([w_lo[:8], w_lo[cols - 8 :]], axis=0)
            corr.append(
                jnp.concatenate(
                    [jnp.where(near_edge, 0.0, e_hi), jnp.where(near_edge, 0.0, e_lo)], axis=1
                ).astype(jnp.bfloat16)
            )
        return jnp.concatenate(main, axis=0), jnp.concatenate(corr, axis=0)

    def apply(xc, xe, tall, tall_e, e):
        rhs_c = jnp.concatenate([xc, xc], axis=0)
        rhs_e = jnp.concatenate([xe, xe], axis=0)
        y = jnp.dot(tall, rhs_c, preferred_element_type=jnp.float32)
        yc = jnp.dot(tall_e, rhs_e, preferred_element_type=jnp.float32)
        for k in range(basis):
            v = y[k * cols : (k + 1) * cols]
            c = yc[k * 16 : (k + 1) * 16]
            v = jnp.concatenate([v[:8] + c[:8], v[8 : cols - 8], v[cols - 8 :] + c[8:]], axis=0)
            f_ref[k, e] = v.astype(jnp.bfloat16).astype(jnp.float32)

    def filter_rows(c_ref, e_ref, count, first):
        def filter_row(r, carry):
            tall, tall_e = build(first + r)
            apply(c_ref[r], e_ref[r], tall, tall_e, first + r)
            return carry

        lax.fori_loop(0, count, filter_row, 0)

    def build_halo(slot, first):
        def one(r, carry):
            tall, tall_e = build(first + r)
            tm_ref[slot + r] = tall
            tc_ref[slot + r] = tall_e
            return carry

        lax.fori_loop(0, HALO, one, 0)

    def filter_halo(c_ref, e_ref, slot, first):
        def one(r, carry):
            apply(c_ref[r], e_ref[r], tm_ref[slot + r], tc_ref[slot + r], first + r)
            return carry

        lax.fori_loop(0, HALO, one, 0)

    def zero_rows(first):
        f_ref[:, pl.ds(first, HALO)] = jnp.zeros((basis, HALO, cols, chans), jnp.float32)

    for n in (0, 1):
        loads[n].wait()
    taps_count = tap_v.shape[0]
    shift = lax.rem(total_rows - (lat * out_rows - HALO) + total_rows, total_rows)
    for k in range(basis):
        a = tap_v[:, k, :]
        a = jnp.concatenate([a, jnp.zeros((2 * 8 - taps_count, total_rows), jnp.float32)], axis=0)
        a = pltpu.roll(a, shift, 1)[:, :LANES]
        a = jnp.transpose(a)
        a = jnp.concatenate([a, jnp.zeros((LANES, LANES - 2 * 8), jnp.float32)], axis=1)
        tap_u[k] = pltpu.roll(a, LANES - HALO, 1)[:ext_rows]
    for c in h_side:
        c.wait_recv()
    filter_rows(fields_ref, own_h, out_rows, HALO)

    build_halo(0, 0)
    build_halo(HALO, HALO + out_rows)
    loads[5].wait()

    def polar_rows(pole):
        pol.wait_recv()
        upper = col_id >= row_id
        for k in range(basis):
            for p in range(polar_count):
                a = cyc_v[k, pl.ds(pole * polar_count + p, 1), :].astype(jnp.float32)
                ra = rolled(a[:, :LANES], cols)
                rb = rolled(a[:, LANES:], cols)
                circ_t = jnp.concatenate(
                    [jnp.where(upper, ra, rb), jnp.where(upper, rb, ra)], axis=0
                )
                circ = jnp.transpose(circ_t).astype(jnp.bfloat16)
                g = jnp.concatenate([fields_ref[slot + p], polar_o[p]], axis=0)
                y = jnp.dot(circ, g, preferred_element_type=jnp.float32)
                f_ref[k, HALO + slot + p] = y.astype(jnp.bfloat16).astype(jnp.float32)

    @pl.when(lat == 0)
    def _():
        polar_rows(0)

    @pl.when(lat == last)
    def _():
        polar_rows(1)

    for n in (2, 3, 4, 6):
        loads[n].wait()
    base_row = lat * out_rows
    lw_all = lat_v[...].astype(jnp.float32)
    terms = []
    for i in range(out_rows):
        begin = start_s[i]
        width = width_s[i]
        row_terms = []
        for t in range(band_len):
            source = begin + t
            ok = (t < width) & (source >= 0) & (source < total_rows)
            r = jnp.clip(source - base_row + HALO, 0, ext_rows - 1)
            row_terms.append((ok, r))
        terms.append(row_terms)

    def weight(i, k, t, keep):
        ok, r = terms[i][t]
        return jnp.where(ok & keep(r), lw_all[t, k : k + 1, i : i + 1], 0.0)

    def own(r):
        return (r >= HALO) & (r < HALO + out_rows)

    for i in range(out_rows):
        for k in range(basis):
            acc = jnp.zeros((cols, chans), jnp.float32)
            for t in range(band_len):
                r = jnp.clip(terms[i][t][1], HALO, HALO + out_rows - 1)
                acc = acc + weight(i, k, t, own) * f_ref[k, r]
            acc_ref[i, k] = acc

    def finish(rows, steps, keep):
        for i in rows:
            for k in range(basis):
                acc = acc_ref[i, k]
                for t in steps(i):
                    acc = acc + weight(i, k, t, keep) * f_ref[k, terms[i][t][1]]
                h_ref[i, :, k * chans : (k + 1) * chans] = acc.astype(jnp.bfloat16)
        first, count = rows[0], len(rows)
        flat = (count * cols, chans)
        mixed = jnp.dot(
            h_ref[pl.ds(first, count)].reshape(count * cols, basis * chans), mix_ref[...],
            preferred_element_type=jnp.float32,
        )
        own_rows = fields_ref[pl.ds(first, count)].astype(jnp.float32).reshape(flat)
        out_ref[pl.ds(first, count)] = (own_rows + mixed).astype(out_ref.dtype).reshape(
            (count, cols, chans)
        )

    half = out_rows // 2

    def top_half():
        @pl.when(has_down)
        def _():
            c_up.wait_recv()
            for c in h_up:
                c.wait_recv()
            filter_halo(top_c, top_h, 0, 0)

        @pl.when(lat == 0)
        def _():
            zero_rows(0)

        finish(list(range(half)), lambda i: range(0, HALO - i), lambda r: r < HALO)

    def bottom_half():
        @pl.when(has_up)
        def _():
            c_dn.wait_recv()
            for c in h_dn:
                c.wait_recv()
            filter_halo(bot_c, bot_h, HALO, HALO + out_rows)

        @pl.when(lat == last)
        def _():
            zero_rows(HALO + out_rows)

        finish(
            list(range(half, out_rows)),
            lambda i: range(out_rows + 1 - i, band_len),
            lambda r: r >= HALO + out_rows,
        )

    far_above = lax.rem(lat, X_CHIPS) == 0

    @pl.when(jnp.logical_not(far_above))
    def _():
        top_half()
        bottom_half()

    @pl.when(far_above)
    def _():
        bottom_half()
        top_half()

    for c in h_side:
        c.wait_send()

    @pl.when(has_up)
    def _():
        c_up.wait_send()
        for c in h_up:
            c.wait_send()

    @pl.when(has_down)
    def _():
        c_dn.wait_send()
        for c in h_dn:
            c.wait_send()

    @pl.when(is_polar)
    def _():
        pol.wait_send()


def shards(fields, lon_taps, lat_taps, cycle_taps, band_start, band_width, mixing):
    row_count, col_count, chan_count = fields.shape
    basis_count = lon_taps.shape[1]
    taps_count = lon_taps.shape[2]
    reach_cells = (taps_count - 1) // 2
    band_len = lat_taps.shape[2]
    polar_rows = row_count // 2
    lat_count = lax.axis_size("lat")
    lon_count = lax.axis_size("lon")
    assert lon_count == 2 and reach_cells == HALO
    cycle_len = lon_count * col_count
    lat_pos = lax.axis_index("lat")
    ext_rows = row_count + 2 * HALO
    total_rows = lat_count * row_count

    mix_flat = mixing.reshape(basis_count * chan_count, chan_count)
    lon_t = jnp.transpose(lon_taps, (2, 1, 0))
    lat_t = jnp.transpose(lat_taps, (2, 1, 0))

    hbm = pl.BlockSpec(memory_space=pl.ANY)
    kernel = functools.partial(
        conv_kernel, basis_count, row_count, band_len, polar_rows, total_rows
    )
    halo_block = pltpu.VMEM((HALO, col_count, chan_count), fields.dtype)
    return copy_out(pl.pallas_call(
        kernel,
        out_shape=jax.ShapeDtypeStruct(fields.shape, fields.dtype),
        in_specs=[hbm] * 6 + [pl.BlockSpec(memory_space=pltpu.HBM)],
        out_specs=pl.BlockSpec(memory_space=pltpu.VMEM),
        scratch_shapes=[
            pltpu.SMEM(band_start.shape, band_start.dtype),
            pltpu.SMEM(band_width.shape, band_width.dtype),
            pltpu.VMEM(lat_t.shape, lat_t.dtype),
            pltpu.VMEM(lon_t.shape, lon_t.dtype),
            pltpu.VMEM((basis_count, ext_rows, LANES), jnp.float32),
            pltpu.VMEM(cycle_taps.shape, cycle_taps.dtype),
            pltpu.VMEM(fields.shape, fields.dtype),
            pltpu.VMEM(mix_flat.shape, mix_flat.dtype),
            halo_block,
            halo_block,
            halo_block,
            halo_block,
            pltpu.VMEM(fields.shape, fields.dtype),
            pltpu.VMEM((polar_rows, col_count, chan_count), fields.dtype),
            pltpu.VMEM((basis_count, ext_rows, col_count, chan_count), jnp.float32),
            pltpu.VMEM((row_count, basis_count, col_count, chan_count), jnp.float32),
            pltpu.VMEM((row_count, col_count, basis_count * chan_count), jnp.bfloat16),
            pltpu.VMEM((2 * HALO, basis_count * col_count, 2 * col_count), jnp.bfloat16),
            pltpu.VMEM((2 * HALO, basis_count * 16, 2 * col_count), jnp.bfloat16),
            pltpu.SemaphoreType.DMA((9,)),
            pltpu.SemaphoreType.DMA((9,)),
            pltpu.SemaphoreType.DMA((7,)),
        ],
        compiler_params=pltpu.CompilerParams(
            vmem_limit_bytes=67043328, collective_id=0, has_side_effects=True
        ),
    )(band_start, band_width, lat_t, lon_t, cycle_taps, fields, mix_flat))


def copy_out(block):
    pieces = 4
    step = block.shape[0] // pieces

    def body(src, dst, stage, sem_in, sem_out):
        ins = [
            pltpu.make_async_copy(src.at[pl.ds(n * step, step)], stage.at[pl.ds(n * step, step)], sem_in.at[n])
            for n in range(pieces)
        ]
        outs = [
            pltpu.make_async_copy(stage.at[pl.ds(n * step, step)], dst.at[pl.ds(n * step, step)], sem_out.at[n])
            for n in range(pieces)
        ]
        for c in ins:
            c.start()
        for c_in, c_out in zip(ins, outs):
            c_in.wait()
            c_out.start()
        for c in outs:
            c.wait()

    hbm = pl.BlockSpec(memory_space=pl.ANY)
    return pl.pallas_call(
        body,
        out_shape=jax.ShapeDtypeStruct(block.shape, block.dtype),
        in_specs=[hbm],
        out_specs=hbm,
        scratch_shapes=[
            pltpu.VMEM(block.shape, block.dtype),
            pltpu.SemaphoreType.DMA((pieces,)),
            pltpu.SemaphoreType.DMA((pieces,)),
        ],
    )(block)


def solution(mesh):
    in_specs = (
        P(("ens", "lat"), "lon", None),
        P(),
        P("lat", None, None),
        P(),
        P("lat"),
        P("lat"),
        P(),
    )
    out_specs = P(("ens", "lat"), "lon", None)
    return jax.shard_map(shards, mesh=mesh, in_specs=in_specs, out_specs=out_specs, check_vma=False)
```

```python
import functools

import jax
import jax.numpy as jnp
from jax import lax
from jax.experimental import pallas as pl
from jax.experimental.pallas import tpu as pltpu
from jax.sharding import PartitionSpec as P

HALO = 4
LANES = 128
EDGE = 16
X_CHIPS = 4
MESH = pl.DeviceIdType.MESH


def rolled(vec, rows):
    return pltpu.roll(jnp.broadcast_to(vec, (rows, LANES)), 0, 1, stride=1, stride_axis=0)


def conv_kernel(basis, out_rows, band_len, polar_count, total_rows,
                start_hbm, width_hbm, lat_hbm, lon_hbm, cyc_hbm, fields_hbm, mix_hbm, out_ref,
                start_s, width_s, lat_v, tap_v, tap_u, cyc_v, fields_ref, mix_ref,
                top_c, bot_c, top_h, bot_h, own_h, polar_o, f_ref, acc_ref, h_ref, tm_ref, tc_ref,
                send_sem, recv_sem, load_sem):
    cols = out_ref.shape[1]
    chans = out_ref.shape[2]
    ext_rows = out_rows + 2 * HALO
    lat = lax.axis_index("lat")
    loads = [
        pltpu.make_async_copy(fields_hbm, fields_ref, load_sem.at[0]),
        pltpu.make_async_copy(lon_hbm, tap_v, load_sem.at[1]),
        pltpu.make_async_copy(start_hbm, start_s, load_sem.at[2]),
        pltpu.make_async_copy(width_hbm, width_s, load_sem.at[3]),
        pltpu.make_async_copy(lat_hbm, lat_v, load_sem.at[4]),
        pltpu.make_async_copy(cyc_hbm, cyc_v, load_sem.at[5]),
        pltpu.make_async_copy(mix_hbm, mix_ref, load_sem.at[6]),
    ]
    for c in loads:
        c.start()
    lon = lax.axis_index("lon")
    last = lax.axis_size("lat") - 1
    has_up = lat < last
    has_down = lat > 0
    is_polar = (lat == 0) | (lat == last)
    slot = jnp.minimum(lat, 1) * (out_rows - polar_count)
    up = jnp.minimum(lat + 1, last)
    down = jnp.maximum(lat - 1, 0)
    side = 1 - lon

    middle = pl.ds(EDGE, cols - 2 * EDGE)
    for buf in (top_h, bot_h, own_h):
        buf[:, middle] = jnp.zeros((buf.shape[0], cols - 2 * EDGE, chans), buf.dtype)

    barrier = pltpu.get_barrier_semaphore()

    def greet(where):
        pl.semaphore_signal(barrier, 1, device_id=where, device_id_type=MESH)

    greet({"lat": lat, "lon": side})

    @pl.when(has_up)
    def _():
        greet({"lat": up, "lon": lon})
        greet({"lat": up, "lon": side})

    @pl.when(has_down)
    def _():
        greet({"lat": down, "lon": lon})
        greet({"lat": down, "lon": side})

    pl.semaphore_wait(barrier, 1 + 2 * (has_up.astype(jnp.int32) + has_down.astype(jnp.int32)))

    def copy(n, src, dst, where):
        return pltpu.make_async_remote_copy(
            src_ref=src, dst_ref=dst, send_sem=send_sem.at[n], recv_sem=recv_sem.at[n],
            device_id=where, device_id_type=MESH)

    lo_rows = pl.ds(0, HALO)
    hi_rows = pl.ds(out_rows - HALO, HALO)
    first_cols = pl.ds(0, EDGE)
    last_cols = pl.ds(cols - EDGE, EDGE)
    c_up = copy(0, fields_hbm.at[hi_rows], top_c, {"lat": up, "lon": lon})
    c_dn = copy(1, fields_hbm.at[lo_rows], bot_c, {"lat": down, "lon": lon})
    h_up = [
        copy(2, fields_hbm.at[hi_rows, first_cols], top_h.at[:, first_cols], {"lat": up, "lon": side}),
        copy(3, fields_hbm.at[hi_rows, last_cols], top_h.at[:, last_cols], {"lat": up, "lon": side}),
    ]
    h_dn = [
        copy(4, fields_hbm.at[lo_rows, first_cols], bot_h.at[:, first_cols], {"lat": down, "lon": side}),
        copy(5, fields_hbm.at[lo_rows, last_cols], bot_h.at[:, last_cols], {"lat": down, "lon": side}),
    ]
    h_side = [
        copy(6, fields_hbm.at[:, first_cols], own_h.at[:, first_cols], {"lat": lat, "lon": side}),
        copy(7, fields_hbm.at[:, last_cols], own_h.at[:, last_cols], {"lat": lat, "lon": side}),
    ]
    pol = copy(8, fields_hbm.at[pl.ds(slot, polar_count)], polar_o, {"lat": lat, "lon": side})

    for c in h_side:
        c.start()

    @pl.when(has_up)
    def _():
        c_up.start()
        for c in h_up:
            c.start()

    @pl.when(has_down)
    def _():
        c_dn.start()
        for c in h_dn:
            c.start()

    @pl.when(is_polar)
    def _():
        pol.start()

    row_id = lax.broadcasted_iota(jnp.int32, (cols, LANES), 0)
    col_id = lax.broadcasted_iota(jnp.int32, (cols, LANES), 1)
    near = jnp.abs(col_id - row_id) <= HALO

    near_edge = jnp.concatenate([near[:8], near[cols - 8 :]], axis=0)

    def build(e):
        centred = tap_u[:, e]
        main, corr = [], []
        for k in range(basis):
            u = centred[k : k + 1]
            u_hi = u.astype(jnp.bfloat16).astype(jnp.float32)
            w_hi = rolled(u_hi, cols)
            w_lo = rolled(u - u_hi, cols)
            main.append(
                jnp.concatenate(
                    [jnp.where(near, w_hi, 0.0), jnp.where(near, w_lo, 0.0)], axis=1
                ).astype(jnp.bfloat16)
            )
            e_hi = jnp.concatenate([w_hi[:8], w_hi[cols - 8 :]], axis=0)
            e_lo = jnp.concatenate([w_lo[:8], w_lo[cols - 8 :]], axis=0)
            corr.append(
                jnp.concatenate(
                    [jnp.where(near_edge, 0.0, e_hi), jnp.where(near_edge, 0.0, e_lo)], axis=1
                ).astype(jnp.bfloat16)
            )
        return jnp.concatenate(main, axis=0), jnp.concatenate(corr, axis=0)

    def apply(xc, xe, tall, tall_e, e):
        rhs_c = jnp.concatenate([xc, xc], axis=0)
        rhs_e = jnp.concatenate([xe, xe], axis=0)
        y = jnp.dot(tall, rhs_c, preferred_element_type=jnp.float32)
        yc = jnp.dot(tall_e, rhs_e, preferred_element_type=jnp.float32)
        for k in range(basis):
            v = y[k * cols : (k + 1) * cols]
            c = yc[k * 16 : (k + 1) * 16]
            v = jnp.concatenate([v[:8] + c[:8], v[8 : cols - 8], v[cols - 8 :] + c[8:]], axis=0)
            f_ref[k, e] = v.astype(jnp.bfloat16).astype(jnp.float32)

    def filter_rows(c_ref, e_ref, count, first):
        def filter_row(r, carry):
            tall, tall_e = build(first + r)
            apply(c_ref[r], e_ref[r], tall, tall_e, first + r)
            return carry

        lax.fori_loop(0, count, filter_row, 0)

    def build_halo(slot, first):
        def one(r, carry):
            tall, tall_e = build(first + r)
            tm_ref[slot + r] = tall
            tc_ref[slot + r] = tall_e
            return carry

        lax.fori_loop(0, HALO, one, 0)

    def filter_halo(c_ref, e_ref, slot, first):
        def one(r, carry):
            apply(c_ref[r], e_ref[r], tm_ref[slot + r], tc_ref[slot + r], first + r)
            return carry

        lax.fori_loop(0, HALO, one, 0)

    def zero_rows(first):
        f_ref[:, pl.ds(first, HALO)] = jnp.zeros((basis, HALO, cols, chans), jnp.float32)

    for n in (0, 1):
        loads[n].wait()
    taps_count = tap_v.shape[0]
    shift = lax.rem(total_rows - (lat * out_rows - HALO) + total_rows, total_rows)
    for k in range(basis):
        a = tap_v[:, k, :]
        a = jnp.concatenate([a, jnp.zeros((2 * 8 - taps_count, total_rows), jnp.float32)], axis=0)
        a = pltpu.roll(a, shift, 1)[:, :LANES]
        a = jnp.transpose(a)
        a = jnp.concatenate([a, jnp.zeros((LANES, LANES - 2 * 8), jnp.float32)], axis=1)
        tap_u[k] = pltpu.roll(a, LANES - HALO, 1)[:ext_rows]
    for c in h_side:
        c.wait_recv()
    filter_rows(fields_ref, own_h, out_rows, HALO)

    build_halo(0, 0)
    build_halo(HALO, HALO + out_rows)
    loads[5].wait()

    def polar_rows(pole):
        pol.wait_recv()
        upper = col_id >= row_id
        for k in range(basis):
            for p in range(polar_count):
                a = cyc_v[k, pl.ds(pole * polar_count + p, 1), :].astype(jnp.float32)
                ra = rolled(a[:, :LANES], cols)
                rb = rolled(a[:, LANES:], cols)
                circ_t = jnp.concatenate(
                    [jnp.where(upper, ra, rb), jnp.where(upper, rb, ra)], axis=0
                )
                circ = jnp.transpose(circ_t).astype(jnp.bfloat16)
                g = jnp.concatenate([fields_ref[slot + p], polar_o[p]], axis=0)
                y = jnp.dot(circ, g, preferred_element_type=jnp.float32)
                f_ref[k, HALO + slot + p] = y.astype(jnp.bfloat16).astype(jnp.float32)

    @pl.when(lat == 0)
    def _():
        polar_rows(0)

    @pl.when(lat == last)
    def _():
        polar_rows(1)

    for n in (2, 3, 4, 6):
        loads[n].wait()
    base_row = lat * out_rows
    lw_all = lat_v[...].astype(jnp.float32)
    terms = []
    for i in range(out_rows):
        begin = start_s[i]
        width = width_s[i]
        row_terms = []
        for t in range(band_len):
            source = begin + t
            ok = (t < width) & (source >= 0) & (source < total_rows)
            r = jnp.clip(source - base_row + HALO, 0, ext_rows - 1)
            row_terms.append((ok, r))
        terms.append(row_terms)

    def weight(i, k, t, keep):
        ok, r = terms[i][t]
        return jnp.where(ok & keep(r), lw_all[t, k : k + 1, i : i + 1], 0.0)

    def own(r):
        return (r >= HALO) & (r < HALO + out_rows)

    def own_steps(i):
        shifts = [0] if i == 0 else [HALO - 1] if i == out_rows - 1 else range(HALO)
        return [
            t for t in range(band_len)
            if any(HALO <= i + s + t < HALO + out_rows for s in shifts)
        ]

    for i in range(out_rows):
        for k in range(basis):
            acc = jnp.zeros((cols, chans), jnp.float32)
            for t in own_steps(i):
                r = jnp.clip(terms[i][t][1], HALO, HALO + out_rows - 1)
                acc = acc + weight(i, k, t, own) * f_ref[k, r]
            acc_ref[i, k] = acc

    def finish(rows, steps, keep):
        for i in rows:
            for k in range(basis):
                acc = acc_ref[i, k]
                for t in steps(i):
                    acc = acc + weight(i, k, t, keep) * f_ref[k, terms[i][t][1]]
                h_ref[i, :, k * chans : (k + 1) * chans] = acc.astype(jnp.bfloat16)
        first, count = rows[0], len(rows)
        flat = (count * cols, chans)
        mixed = jnp.dot(
            h_ref[pl.ds(first, count)].reshape(count * cols, basis * chans), mix_ref[...],
            preferred_element_type=jnp.float32,
        )
        own_rows = fields_ref[pl.ds(first, count)].astype(jnp.float32).reshape(flat)
        out_ref[pl.ds(first, count)] = (own_rows + mixed).astype(out_ref.dtype).reshape(
            (count, cols, chans)
        )

    half = out_rows // 2

    def top_half():
        @pl.when(has_down)
        def _():
            c_up.wait_recv()
            for c in h_up:
                c.wait_recv()
            filter_halo(top_c, top_h, 0, 0)

        @pl.when(lat == 0)
        def _():
            zero_rows(0)

        finish(list(range(half)), lambda i: range(0, HALO - i), lambda r: r < HALO)

    def bottom_half():
        @pl.when(has_up)
        def _():
            c_dn.wait_recv()
            for c in h_dn:
                c.wait_recv()
            filter_halo(bot_c, bot_h, HALO, HALO + out_rows)

        @pl.when(lat == last)
        def _():
            zero_rows(HALO + out_rows)

        finish(
            list(range(half, out_rows)),
            lambda i: range(out_rows + 1 - i, band_len),
            lambda r: r >= HALO + out_rows,
        )

    far_above = lax.rem(lat, X_CHIPS) == 0

    @pl.when(jnp.logical_not(far_above))
    def _():
        top_half()
        bottom_half()

    @pl.when(far_above)
    def _():
        bottom_half()
        top_half()

    for c in h_side:
        c.wait_send()

    @pl.when(has_up)
    def _():
        c_up.wait_send()
        for c in h_up:
            c.wait_send()

    @pl.when(has_down)
    def _():
        c_dn.wait_send()
        for c in h_dn:
            c.wait_send()

    @pl.when(is_polar)
    def _():
        pol.wait_send()


def shards(fields, lon_taps, lat_taps, cycle_taps, band_start, band_width, mixing):
    row_count, col_count, chan_count = fields.shape
    basis_count = lon_taps.shape[1]
    taps_count = lon_taps.shape[2]
    reach_cells = (taps_count - 1) // 2
    band_len = lat_taps.shape[2]
    polar_rows = row_count // 2
    lat_count = lax.axis_size("lat")
    lon_count = lax.axis_size("lon")
    assert lon_count == 2 and reach_cells == HALO
    cycle_len = lon_count * col_count
    lat_pos = lax.axis_index("lat")
    ext_rows = row_count + 2 * HALO
    total_rows = lat_count * row_count

    mix_flat = mixing.reshape(basis_count * chan_count, chan_count)
    lon_t = jnp.transpose(lon_taps, (2, 1, 0))
    lat_t = jnp.transpose(lat_taps, (2, 1, 0))

    hbm = pl.BlockSpec(memory_space=pl.ANY)
    kernel = functools.partial(
        conv_kernel, basis_count, row_count, band_len, polar_rows, total_rows
    )
    halo_block = pltpu.VMEM((HALO, col_count, chan_count), fields.dtype)
    return copy_out(pl.pallas_call(
        kernel,
        out_shape=jax.ShapeDtypeStruct(fields.shape, fields.dtype),
        in_specs=[hbm] * 6 + [pl.BlockSpec(memory_space=pltpu.HBM)],
        out_specs=pl.BlockSpec(memory_space=pltpu.VMEM),
        scratch_shapes=[
            pltpu.SMEM(band_start.shape, band_start.dtype),
            pltpu.SMEM(band_width.shape, band_width.dtype),
            pltpu.VMEM(lat_t.shape, lat_t.dtype),
            pltpu.VMEM(lon_t.shape, lon_t.dtype),
            pltpu.VMEM((basis_count, ext_rows, LANES), jnp.float32),
            pltpu.VMEM(cycle_taps.shape, cycle_taps.dtype),
            pltpu.VMEM(fields.shape, fields.dtype),
            pltpu.VMEM(mix_flat.shape, mix_flat.dtype),
            halo_block,
            halo_block,
            halo_block,
            halo_block,
            pltpu.VMEM(fields.shape, fields.dtype),
            pltpu.VMEM((polar_rows, col_count, chan_count), fields.dtype),
            pltpu.VMEM((basis_count, ext_rows, col_count, chan_count), jnp.float32),
            pltpu.VMEM((row_count, basis_count, col_count, chan_count), jnp.float32),
            pltpu.VMEM((row_count, col_count, basis_count * chan_count), jnp.bfloat16),
            pltpu.VMEM((2 * HALO, basis_count * col_count, 2 * col_count), jnp.bfloat16),
            pltpu.VMEM((2 * HALO, basis_count * 16, 2 * col_count), jnp.bfloat16),
            pltpu.SemaphoreType.DMA((9,)),
            pltpu.SemaphoreType.DMA((9,)),
            pltpu.SemaphoreType.DMA((7,)),
        ],
        compiler_params=pltpu.CompilerParams(
            vmem_limit_bytes=67043328, collective_id=0, has_side_effects=True
        ),
    )(band_start, band_width, lat_t, lon_t, cycle_taps, fields, mix_flat))


def copy_out(block):
    pieces = 4
    step = block.shape[0] // pieces

    def body(src, dst, stage, sem_in, sem_out):
        ins = [
            pltpu.make_async_copy(src.at[pl.ds(n * step, step)], stage.at[pl.ds(n * step, step)], sem_in.at[n])
            for n in range(pieces)
        ]
        outs = [
            pltpu.make_async_copy(stage.at[pl.ds(n * step, step)], dst.at[pl.ds(n * step, step)], sem_out.at[n])
            for n in range(pieces)
        ]
        for c in ins:
            c.start()
        for c_in, c_out in zip(ins, outs):
            c_in.wait()
            c_out.start()
        for c in outs:
            c.wait()

    hbm = pl.BlockSpec(memory_space=pl.ANY)
    return pl.pallas_call(
        body,
        out_shape=jax.ShapeDtypeStruct(block.shape, block.dtype),
        in_specs=[hbm],
        out_specs=hbm,
        scratch_shapes=[
            pltpu.VMEM(block.shape, block.dtype),
            pltpu.SemaphoreType.DMA((pieces,)),
            pltpu.SemaphoreType.DMA((pieces,)),
        ],
    )(block)


def solution(mesh):
    in_specs = (
        P(("ens", "lat"), "lon", None),
        P(),
        P("lat", None, None),
        P(),
        P("lat"),
        P("lat"),
        P(),
    )
    out_specs = P(("ens", "lat"), "lon", None)
    return jax.shard_map(shards, mesh=mesh, in_specs=in_specs, out_specs=out_specs, check_vma=False)
```

```python
import functools

import jax
import jax.numpy as jnp
from jax import lax
from jax.experimental import pallas as pl
from jax.experimental.pallas import tpu as pltpu
from jax.sharding import PartitionSpec as P

HALO = 4
LANES = 128
EDGE = 16
X_CHIPS = 4
MESH = pl.DeviceIdType.MESH


def rolled(vec, rows):
    return pltpu.roll(jnp.broadcast_to(vec, (rows, LANES)), 0, 1, stride=1, stride_axis=0)


def conv_kernel(basis, out_rows, band_len, polar_count, total_rows,
                start_hbm, width_hbm, lat_hbm, lon_hbm, cyc_hbm, fields_hbm, mix_hbm, out_ref,
                start_s, width_s, lat_v, tap_v, tap_u, cyc_v, fields_ref, mix_ref,
                top_c, bot_c, top_h, bot_h, own_h, polar_o, f_ref, acc_ref, h_ref, tm_ref, tc_ref,
                out_v, send_sem, recv_sem, load_sem, out_sem):
    cols = out_ref.shape[1]
    chans = out_ref.shape[2]
    ext_rows = out_rows + 2 * HALO
    lat = lax.axis_index("lat")
    loads = [
        pltpu.make_async_copy(fields_hbm, fields_ref, load_sem.at[0]),
        pltpu.make_async_copy(lon_hbm, tap_v, load_sem.at[1]),
        pltpu.make_async_copy(start_hbm, start_s, load_sem.at[2]),
        pltpu.make_async_copy(width_hbm, width_s, load_sem.at[3]),
        pltpu.make_async_copy(lat_hbm, lat_v, load_sem.at[4]),
        pltpu.make_async_copy(cyc_hbm, cyc_v, load_sem.at[5]),
        pltpu.make_async_copy(mix_hbm, mix_ref, load_sem.at[6]),
    ]
    for c in loads:
        c.start()
    lon = lax.axis_index("lon")
    last = lax.axis_size("lat") - 1
    has_up = lat < last
    has_down = lat > 0
    is_polar = (lat == 0) | (lat == last)
    slot = jnp.minimum(lat, 1) * (out_rows - polar_count)
    up = jnp.minimum(lat + 1, last)
    down = jnp.maximum(lat - 1, 0)
    side = 1 - lon

    middle = pl.ds(EDGE, cols - 2 * EDGE)
    for buf in (top_h, bot_h, own_h):
        buf[:, middle] = jnp.zeros((buf.shape[0], cols - 2 * EDGE, chans), buf.dtype)

    barrier = pltpu.get_barrier_semaphore()

    def greet(where):
        pl.semaphore_signal(barrier, 1, device_id=where, device_id_type=MESH)

    greet({"lat": lat, "lon": side})

    @pl.when(has_up)
    def _():
        greet({"lat": up, "lon": lon})
        greet({"lat": up, "lon": side})

    @pl.when(has_down)
    def _():
        greet({"lat": down, "lon": lon})
        greet({"lat": down, "lon": side})

    pl.semaphore_wait(barrier, 1 + 2 * (has_up.astype(jnp.int32) + has_down.astype(jnp.int32)))

    def copy(n, src, dst, where):
        return pltpu.make_async_remote_copy(
            src_ref=src, dst_ref=dst, send_sem=send_sem.at[n], recv_sem=recv_sem.at[n],
            device_id=where, device_id_type=MESH)

    lo_rows = pl.ds(0, HALO)
    hi_rows = pl.ds(out_rows - HALO, HALO)
    first_cols = pl.ds(0, EDGE)
    last_cols = pl.ds(cols - EDGE, EDGE)
    c_up = copy(0, fields_hbm.at[hi_rows], top_c, {"lat": up, "lon": lon})
    c_dn = copy(1, fields_hbm.at[lo_rows], bot_c, {"lat": down, "lon": lon})
    h_up = [
        copy(2, fields_hbm.at[hi_rows, first_cols], top_h.at[:, first_cols], {"lat": up, "lon": side}),
        copy(3, fields_hbm.at[hi_rows, last_cols], top_h.at[:, last_cols], {"lat": up, "lon": side}),
    ]
    h_dn = [
        copy(4, fields_hbm.at[lo_rows, first_cols], bot_h.at[:, first_cols], {"lat": down, "lon": side}),
        copy(5, fields_hbm.at[lo_rows, last_cols], bot_h.at[:, last_cols], {"lat": down, "lon": side}),
    ]
    h_side = [
        copy(6, fields_hbm.at[:, first_cols], own_h.at[:, first_cols], {"lat": lat, "lon": side}),
        copy(7, fields_hbm.at[:, last_cols], own_h.at[:, last_cols], {"lat": lat, "lon": side}),
    ]
    pol = copy(8, fields_hbm.at[pl.ds(slot, polar_count)], polar_o, {"lat": lat, "lon": side})

    for c in h_side:
        c.start()

    @pl.when(has_up)
    def _():
        c_up.start()
        for c in h_up:
            c.start()

    @pl.when(has_down)
    def _():
        c_dn.start()
        for c in h_dn:
            c.start()

    @pl.when(is_polar)
    def _():
        pol.start()

    row_id = lax.broadcasted_iota(jnp.int32, (cols, LANES), 0)
    col_id = lax.broadcasted_iota(jnp.int32, (cols, LANES), 1)
    near = jnp.abs(col_id - row_id) <= HALO

    near_edge = jnp.concatenate([near[:8], near[cols - 8 :]], axis=0)

    def build(e):
        centred = tap_u[:, e]
        main, corr = [], []
        for k in range(basis):
            u = centred[k : k + 1]
            u_hi = u.astype(jnp.bfloat16).astype(jnp.float32)
            w_hi = rolled(u_hi, cols)
            w_lo = rolled(u - u_hi, cols)
            main.append(
                jnp.concatenate(
                    [jnp.where(near, w_hi, 0.0), jnp.where(near, w_lo, 0.0)], axis=1
                ).astype(jnp.bfloat16)
            )
            e_hi = jnp.concatenate([w_hi[:8], w_hi[cols - 8 :]], axis=0)
            e_lo = jnp.concatenate([w_lo[:8], w_lo[cols - 8 :]], axis=0)
            corr.append(
                jnp.concatenate(
                    [jnp.where(near_edge, 0.0, e_hi), jnp.where(near_edge, 0.0, e_lo)], axis=1
                ).astype(jnp.bfloat16)
            )
        return jnp.concatenate(main, axis=0), jnp.concatenate(corr, axis=0)

    def apply(xc, xe, tall, tall_e, e):
        rhs_c = jnp.concatenate([xc, xc], axis=0)
        rhs_e = jnp.concatenate([xe, xe], axis=0)
        y = jnp.dot(tall, rhs_c, preferred_element_type=jnp.float32)
        yc = jnp.dot(tall_e, rhs_e, preferred_element_type=jnp.float32)
        for k in range(basis):
            v = y[k * cols : (k + 1) * cols]
            c = yc[k * 16 : (k + 1) * 16]
            v = jnp.concatenate([v[:8] + c[:8], v[8 : cols - 8], v[cols - 8 :] + c[8:]], axis=0)
            f_ref[k, e] = v.astype(jnp.bfloat16).astype(jnp.float32)

    def filter_rows(c_ref, e_ref, count, first):
        def filter_row(r, carry):
            tall, tall_e = build(first + r)
            apply(c_ref[r], e_ref[r], tall, tall_e, first + r)
            return carry

        lax.fori_loop(0, count, filter_row, 0)

    def build_halo(slot, first):
        def one(r, carry):
            tall, tall_e = build(first + r)
            tm_ref[slot + r] = tall
            tc_ref[slot + r] = tall_e
            return carry

        lax.fori_loop(0, HALO, one, 0)

    def filter_halo(c_ref, e_ref, slot, first):
        def one(r, carry):
            apply(c_ref[r], e_ref[r], tm_ref[slot + r], tc_ref[slot + r], first + r)
            return carry

        lax.fori_loop(0, HALO, one, 0)

    def zero_rows(first):
        f_ref[:, pl.ds(first, HALO)] = jnp.zeros((basis, HALO, cols, chans), jnp.float32)

    for n in (0, 1):
        loads[n].wait()
    taps_count = tap_v.shape[0]
    shift = lax.rem(total_rows - (lat * out_rows - HALO) + total_rows, total_rows)
    for k in range(basis):
        a = tap_v[:, k, :]
        a = jnp.concatenate([a, jnp.zeros((2 * 8 - taps_count, total_rows), jnp.float32)], axis=0)
        a = pltpu.roll(a, shift, 1)[:, :LANES]
        a = jnp.transpose(a)
        a = jnp.concatenate([a, jnp.zeros((LANES, LANES - 2 * 8), jnp.float32)], axis=1)
        tap_u[k] = pltpu.roll(a, LANES - HALO, 1)[:ext_rows]
    for c in h_side:
        c.wait_recv()
    filter_rows(fields_ref, own_h, out_rows, HALO)

    build_halo(0, 0)
    build_halo(HALO, HALO + out_rows)
    loads[5].wait()

    def polar_rows(pole):
        pol.wait_recv()
        upper = col_id >= row_id
        for k in range(basis):
            for p in range(polar_count):
                a = cyc_v[k, pl.ds(pole * polar_count + p, 1), :].astype(jnp.float32)
                ra = rolled(a[:, :LANES], cols)
                rb = rolled(a[:, LANES:], cols)
                circ_t = jnp.concatenate(
                    [jnp.where(upper, ra, rb), jnp.where(upper, rb, ra)], axis=0
                )
                circ = jnp.transpose(circ_t).astype(jnp.bfloat16)
                g = jnp.concatenate([fields_ref[slot + p], polar_o[p]], axis=0)
                y = jnp.dot(circ, g, preferred_element_type=jnp.float32)
                f_ref[k, HALO + slot + p] = y.astype(jnp.bfloat16).astype(jnp.float32)

    @pl.when(lat == 0)
    def _():
        polar_rows(0)

    @pl.when(lat == last)
    def _():
        polar_rows(1)

    for n in (2, 3, 4, 6):
        loads[n].wait()
    base_row = lat * out_rows
    lw_all = lat_v[...].astype(jnp.float32)
    terms = []
    for i in range(out_rows):
        begin = start_s[i]
        width = width_s[i]
        row_terms = []
        for t in range(band_len):
            source = begin + t
            ok = (t < width) & (source >= 0) & (source < total_rows)
            r = jnp.clip(source - base_row + HALO, 0, ext_rows - 1)
            row_terms.append((ok, r))
        terms.append(row_terms)

    def weight(i, k, t, keep):
        ok, r = terms[i][t]
        return jnp.where(ok & keep(r), lw_all[t, k : k + 1, i : i + 1], 0.0)

    def own(r):
        return (r >= HALO) & (r < HALO + out_rows)

    for i in range(out_rows):
        for k in range(basis):
            acc = jnp.zeros((cols, chans), jnp.float32)
            for t in range(band_len):
                r = jnp.clip(terms[i][t][1], HALO, HALO + out_rows - 1)
                acc = acc + weight(i, k, t, own) * f_ref[k, r]
            acc_ref[i, k] = acc

    def finish(rows, steps, keep):
        for i in rows:
            for k in range(basis):
                acc = acc_ref[i, k]
                for t in steps(i):
                    acc = acc + weight(i, k, t, keep) * f_ref[k, terms[i][t][1]]
                h_ref[i, :, k * chans : (k + 1) * chans] = acc.astype(jnp.bfloat16)
        first, count = rows[0], len(rows)
        flat = (count * cols, chans)
        mixed = jnp.dot(
            h_ref[pl.ds(first, count)].reshape(count * cols, basis * chans), mix_ref[...],
            preferred_element_type=jnp.float32,
        )
        own_rows = fields_ref[pl.ds(first, count)].astype(jnp.float32).reshape(flat)
        out_v[pl.ds(first, count)] = (own_rows + mixed).astype(out_v.dtype).reshape(
            (count, cols, chans)
        )
        stores[first // half].start()

    half = out_rows // 2
    stores = [
        pltpu.make_async_copy(
            out_v.at[pl.ds(n * half, half)], out_ref.at[pl.ds(n * half, half)], out_sem.at[n]
        )
        for n in range(2)
    ]

    def top_half():
        @pl.when(has_down)
        def _():
            c_up.wait_recv()
            for c in h_up:
                c.wait_recv()
            filter_halo(top_c, top_h, 0, 0)

        @pl.when(lat == 0)
        def _():
            zero_rows(0)

        finish(list(range(half)), lambda i: range(0, HALO - i), lambda r: r < HALO)

    def bottom_half():
        @pl.when(has_up)
        def _():
            c_dn.wait_recv()
            for c in h_dn:
                c.wait_recv()
            filter_halo(bot_c, bot_h, HALO, HALO + out_rows)

        @pl.when(lat == last)
        def _():
            zero_rows(HALO + out_rows)

        finish(
            list(range(half, out_rows)),
            lambda i: range(out_rows + 1 - i, band_len),
            lambda r: r >= HALO + out_rows,
        )

    far_above = lax.rem(lat, X_CHIPS) == 0

    @pl.when(jnp.logical_not(far_above))
    def _():
        top_half()
        bottom_half()

    @pl.when(far_above)
    def _():
        bottom_half()
        top_half()

    for c in stores:
        c.wait()

    for c in h_side:
        c.wait_send()

    @pl.when(has_up)
    def _():
        c_up.wait_send()
        for c in h_up:
            c.wait_send()

    @pl.when(has_down)
    def _():
        c_dn.wait_send()
        for c in h_dn:
            c.wait_send()

    @pl.when(is_polar)
    def _():
        pol.wait_send()


def shards(fields, lon_taps, lat_taps, cycle_taps, band_start, band_width, mixing):
    row_count, col_count, chan_count = fields.shape
    basis_count = lon_taps.shape[1]
    taps_count = lon_taps.shape[2]
    reach_cells = (taps_count - 1) // 2
    band_len = lat_taps.shape[2]
    polar_rows = row_count // 2
    lat_count = lax.axis_size("lat")
    lon_count = lax.axis_size("lon")
    assert lon_count == 2 and reach_cells == HALO
    cycle_len = lon_count * col_count
    lat_pos = lax.axis_index("lat")
    ext_rows = row_count + 2 * HALO
    total_rows = lat_count * row_count

    mix_flat = mixing.reshape(basis_count * chan_count, chan_count)
    lon_t = jnp.transpose(lon_taps, (2, 1, 0))
    lat_t = jnp.transpose(lat_taps, (2, 1, 0))

    hbm = pl.BlockSpec(memory_space=pl.ANY)
    kernel = functools.partial(
        conv_kernel, basis_count, row_count, band_len, polar_rows, total_rows
    )
    halo_block = pltpu.VMEM((HALO, col_count, chan_count), fields.dtype)
    return copy_out(pl.pallas_call(
        kernel,
        out_shape=jax.ShapeDtypeStruct(fields.shape, fields.dtype),
        in_specs=[hbm] * 6 + [pl.BlockSpec(memory_space=pltpu.HBM)],
        out_specs=pl.BlockSpec(memory_space=pl.ANY),
        scratch_shapes=[
            pltpu.SMEM(band_start.shape, band_start.dtype),
            pltpu.SMEM(band_width.shape, band_width.dtype),
            pltpu.VMEM(lat_t.shape, lat_t.dtype),
            pltpu.VMEM(lon_t.shape, lon_t.dtype),
            pltpu.VMEM((basis_count, ext_rows, LANES), jnp.float32),
            pltpu.VMEM(cycle_taps.shape, cycle_taps.dtype),
            pltpu.VMEM(fields.shape, fields.dtype),
            pltpu.VMEM(mix_flat.shape, mix_flat.dtype),
            halo_block,
            halo_block,
            halo_block,
            halo_block,
            pltpu.VMEM(fields.shape, fields.dtype),
            pltpu.VMEM((polar_rows, col_count, chan_count), fields.dtype),
            pltpu.VMEM((basis_count, ext_rows, col_count, chan_count), jnp.float32),
            pltpu.VMEM((row_count, basis_count, col_count, chan_count), jnp.float32),
            pltpu.VMEM((row_count, col_count, basis_count * chan_count), jnp.bfloat16),
            pltpu.VMEM((2 * HALO, basis_count * col_count, 2 * col_count), jnp.bfloat16),
            pltpu.VMEM((2 * HALO, basis_count * 16, 2 * col_count), jnp.bfloat16),
            pltpu.VMEM(fields.shape, fields.dtype),
            pltpu.SemaphoreType.DMA((9,)),
            pltpu.SemaphoreType.DMA((9,)),
            pltpu.SemaphoreType.DMA((7,)),
            pltpu.SemaphoreType.DMA((2,)),
        ],
        compiler_params=pltpu.CompilerParams(
            vmem_limit_bytes=67043328, collective_id=0, has_side_effects=True
        ),
    )(band_start, band_width, lat_t, lon_t, cycle_taps, fields, mix_flat))


def copy_out(block):
    pieces = 4
    step = block.shape[0] // pieces

    def body(src, dst, stage, sem_in, sem_out):
        ins = [
            pltpu.make_async_copy(src.at[pl.ds(n * step, step)], stage.at[pl.ds(n * step, step)], sem_in.at[n])
            for n in range(pieces)
        ]
        outs = [
            pltpu.make_async_copy(stage.at[pl.ds(n * step, step)], dst.at[pl.ds(n * step, step)], sem_out.at[n])
            for n in range(pieces)
        ]
        for c in ins:
            c.start()
        for c_in, c_out in zip(ins, outs):
            c_in.wait()
            c_out.start()
        for c in outs:
            c.wait()

    hbm = pl.BlockSpec(memory_space=pl.ANY)
    return pl.pallas_call(
        body,
        out_shape=jax.ShapeDtypeStruct(block.shape, block.dtype),
        in_specs=[hbm],
        out_specs=hbm,
        scratch_shapes=[
            pltpu.VMEM(block.shape, block.dtype),
            pltpu.SemaphoreType.DMA((pieces,)),
            pltpu.SemaphoreType.DMA((pieces,)),
        ],
    )(block)


def solution(mesh):
    in_specs = (
        P(("ens", "lat"), "lon", None),
        P(),
        P("lat", None, None),
        P(),
        P("lat"),
        P("lat"),
        P(),
    )
    out_specs = P(("ens", "lat"), "lon", None)
    return jax.shard_map(shards, mesh=mesh, in_specs=in_specs, out_specs=out_specs, check_vma=False)
```

```python
import functools

import jax
import jax.numpy as jnp
from jax import lax
from jax.experimental import pallas as pl
from jax.experimental.pallas import tpu as pltpu
from jax.sharding import PartitionSpec as P

HALO = 4
LANES = 128
EDGE = 16
X_CHIPS = 4
MESH = pl.DeviceIdType.MESH


def rolled(vec, rows):
    return pltpu.roll(jnp.broadcast_to(vec, (rows, LANES)), 0, 1, stride=1, stride_axis=0)


def conv_kernel(basis, out_rows, band_len, polar_count, total_rows,
                start_hbm, width_hbm, lat_hbm, lon_hbm, cyc_hbm, fields_hbm, mix_hbm, out_ref,
                start_s, width_s, lat_v, tap_v, tap_u, cyc_v, fields_ref, mix_ref,
                top_c, bot_c, top_h, bot_h, own_h, polar_o, f_ref, acc_ref, h_ref, tm_ref,
                send_sem, recv_sem, load_sem):
    cols = out_ref.shape[1]
    chans = out_ref.shape[2]
    ext_rows = out_rows + 2 * HALO
    lat = lax.axis_index("lat")
    loads = [
        pltpu.make_async_copy(fields_hbm, fields_ref, load_sem.at[0]),
        pltpu.make_async_copy(lon_hbm, tap_v, load_sem.at[1]),
        pltpu.make_async_copy(start_hbm, start_s, load_sem.at[2]),
        pltpu.make_async_copy(width_hbm, width_s, load_sem.at[3]),
        pltpu.make_async_copy(lat_hbm, lat_v, load_sem.at[4]),
        pltpu.make_async_copy(cyc_hbm, cyc_v, load_sem.at[5]),
        pltpu.make_async_copy(mix_hbm, mix_ref, load_sem.at[6]),
    ]
    for c in loads:
        c.start()
    lon = lax.axis_index("lon")
    last = lax.axis_size("lat") - 1
    has_up = lat < last
    has_down = lat > 0
    is_polar = (lat == 0) | (lat == last)
    slot = jnp.minimum(lat, 1) * (out_rows - polar_count)
    up = jnp.minimum(lat + 1, last)
    down = jnp.maximum(lat - 1, 0)
    side = 1 - lon


    barrier = pltpu.get_barrier_semaphore()

    def greet(where):
        pl.semaphore_signal(barrier, 1, device_id=where, device_id_type=MESH)

    greet({"lat": lat, "lon": side})

    @pl.when(has_up)
    def _():
        greet({"lat": up, "lon": lon})
        greet({"lat": up, "lon": side})

    @pl.when(has_down)
    def _():
        greet({"lat": down, "lon": lon})
        greet({"lat": down, "lon": side})

    pl.semaphore_wait(barrier, 1 + 2 * (has_up.astype(jnp.int32) + has_down.astype(jnp.int32)))

    def copy(n, src, dst, where):
        return pltpu.make_async_remote_copy(
            src_ref=src, dst_ref=dst, send_sem=send_sem.at[n], recv_sem=recv_sem.at[n],
            device_id=where, device_id_type=MESH)

    lo_rows = pl.ds(0, HALO)
    hi_rows = pl.ds(out_rows - HALO, HALO)
    first_cols = pl.ds(0, EDGE)
    last_cols = pl.ds(cols - EDGE, EDGE)
    c_up = copy(0, fields_hbm.at[hi_rows], top_c, {"lat": up, "lon": lon})
    c_dn = copy(1, fields_hbm.at[lo_rows], bot_c, {"lat": down, "lon": lon})
    h_up = [
        copy(2, fields_hbm.at[hi_rows, first_cols], top_h.at[:, first_cols], {"lat": up, "lon": side}),
        copy(3, fields_hbm.at[hi_rows, last_cols], top_h.at[:, last_cols], {"lat": up, "lon": side}),
    ]
    h_dn = [
        copy(4, fields_hbm.at[lo_rows, first_cols], bot_h.at[:, first_cols], {"lat": down, "lon": side}),
        copy(5, fields_hbm.at[lo_rows, last_cols], bot_h.at[:, last_cols], {"lat": down, "lon": side}),
    ]
    h_side = [
        copy(6, fields_hbm.at[:, first_cols], own_h.at[:, first_cols], {"lat": lat, "lon": side}),
        copy(7, fields_hbm.at[:, last_cols], own_h.at[:, last_cols], {"lat": lat, "lon": side}),
    ]
    pol = copy(8, fields_hbm.at[pl.ds(slot, polar_count)], polar_o, {"lat": lat, "lon": side})

    for c in h_side:
        c.start()

    @pl.when(has_up)
    def _():
        c_up.start()
        for c in h_up:
            c.start()

    @pl.when(has_down)
    def _():
        c_dn.start()
        for c in h_dn:
            c.start()

    @pl.when(is_polar)
    def _():
        pol.start()

    row_id = lax.broadcasted_iota(jnp.int32, (cols, LANES), 0)
    col_id = lax.broadcasted_iota(jnp.int32, (cols, LANES), 1)
    near = jnp.abs(col_id - row_id) <= HALO

    row8 = lax.broadcasted_iota(jnp.int32, (8, chans), 0)

    def build(e):
        centred = tap_u[:, e]
        main = []
        for k in range(basis):
            u = centred[k : k + 1]
            u_hi = u.astype(jnp.bfloat16).astype(jnp.float32)
            w_hi = rolled(u_hi, cols)
            w_lo = rolled(u - u_hi, cols)
            main.append(
                jnp.concatenate(
                    [jnp.where(near, w_hi, 0.0), jnp.where(near, w_lo, 0.0)], axis=1
                ).astype(jnp.bfloat16)
            )
        return jnp.concatenate(main, axis=0)

    def apply(xc, e_row, tall, e):
        rhs_c = jnp.concatenate([xc, xc], axis=0)
        y = jnp.dot(tall, rhs_c, preferred_element_type=jnp.float32)
        lt = e_row[pl.ds(cols - EDGE, EDGE)].astype(jnp.float32)[EDGE - 8 :]
        rt = e_row[pl.ds(0, EDGE)].astype(jnp.float32)[:8]
        left = [
            jnp.where(row8 < HALO - d, pltpu.roll(lt, HALO - d, 0), 0.0) for d in range(HALO)
        ]
        right = [
            jnp.where(row8 >= HALO + q, pltpu.roll(rt, (HALO + q) % 8, 0), 0.0)
            for q in range(HALO)
        ]
        centred = tap_u[:, e]
        for k in range(basis):
            u = centred[k : k + 1]

            def tap(d):
                lane = (d - HALO) % LANES
                return jnp.broadcast_to(u[:, lane : lane + 1], (8, chans))

            top = sum(tap(d) * left[d] for d in range(HALO))
            bottom = sum(tap(2 * HALO - q) * right[q] for q in range(HALO))
            v = y[k * cols : (k + 1) * cols]
            v = jnp.concatenate([v[:8] + top, v[8 : cols - 8], v[cols - 8 :] + bottom], axis=0)
            f_ref[k, e] = v.astype(jnp.bfloat16).astype(jnp.float32)

    def filter_rows(c_ref, e_ref, count, first):
        def filter_row(r, carry):
            apply(c_ref[r], e_ref.at[r], build(first + r), first + r)
            return carry

        lax.fori_loop(0, count, filter_row, 0)

    def build_halo(slot, first):
        def one(r, carry):
            tm_ref[slot + r] = build(first + r)
            return carry

        lax.fori_loop(0, HALO, one, 0)

    def filter_halo(c_ref, e_ref, slot, first):
        def one(r, carry):
            apply(c_ref[r], e_ref.at[r], tm_ref[slot + r], first + r)
            return carry

        lax.fori_loop(0, HALO, one, 0)

    def zero_rows(first):
        f_ref[:, pl.ds(first, HALO)] = jnp.zeros((basis, HALO, cols, chans), jnp.float32)

    for n in (0, 1):
        loads[n].wait()
    taps_count = tap_v.shape[0]
    shift = lax.rem(total_rows - (lat * out_rows - HALO) + total_rows, total_rows)
    for k in range(basis):
        a = tap_v[:, k, :]
        a = jnp.concatenate([a, jnp.zeros((2 * 8 - taps_count, total_rows), jnp.float32)], axis=0)
        a = pltpu.roll(a, shift, 1)[:, :LANES]
        a = jnp.transpose(a)
        a = jnp.concatenate([a, jnp.zeros((LANES, LANES - 2 * 8), jnp.float32)], axis=1)
        tap_u[k] = pltpu.roll(a, LANES - HALO, 1)[:ext_rows]
    for c in h_side:
        c.wait_recv()
    filter_rows(fields_ref, own_h, out_rows, HALO)

    build_halo(0, 0)
    build_halo(HALO, HALO + out_rows)
    loads[5].wait()

    def polar_rows(pole):
        pol.wait_recv()
        upper = col_id >= row_id
        for k in range(basis):
            for p in range(polar_count):
                a = cyc_v[k, pl.ds(pole * polar_count + p, 1), :].astype(jnp.float32)
                ra = rolled(a[:, :LANES], cols)
                rb = rolled(a[:, LANES:], cols)
                circ_t = jnp.concatenate(
                    [jnp.where(upper, ra, rb), jnp.where(upper, rb, ra)], axis=0
                )
                circ = jnp.transpose(circ_t).astype(jnp.bfloat16)
                g = jnp.concatenate([fields_ref[slot + p], polar_o[p]], axis=0)
                y = jnp.dot(circ, g, preferred_element_type=jnp.float32)
                f_ref[k, HALO + slot + p] = y.astype(jnp.bfloat16).astype(jnp.float32)

    @pl.when(lat == 0)
    def _():
        polar_rows(0)

    @pl.when(lat == last)
    def _():
        polar_rows(1)

    for n in (2, 3, 4, 6):
        loads[n].wait()
    base_row = lat * out_rows
    lw_all = lat_v[...].astype(jnp.float32)
    terms = []
    for i in range(out_rows):
        begin = start_s[i]
        width = width_s[i]
        row_terms = []
        for t in range(band_len):
            source = begin + t
            ok = (t < width) & (source >= 0) & (source < total_rows)
            r = jnp.clip(source - base_row + HALO, 0, ext_rows - 1)
            row_terms.append((ok, r))
        terms.append(row_terms)

    def weight(i, k, t, keep):
        ok, r = terms[i][t]
        return jnp.where(ok & keep(r), lw_all[t, k : k + 1, i : i + 1], 0.0)

    def own(r):
        return (r >= HALO) & (r < HALO + out_rows)

    for i in range(out_rows):
        for k in range(basis):
            acc = jnp.zeros((cols, chans), jnp.float32)
            for t in range(band_len):
                r = jnp.clip(terms[i][t][1], HALO, HALO + out_rows - 1)
                acc = acc + weight(i, k, t, own) * f_ref[k, r]
            acc_ref[i, k] = acc

    def finish(rows, steps, keep):
        for i in rows:
            for k in range(basis):
                acc = acc_ref[i, k]
                for t in steps(i):
                    acc = acc + weight(i, k, t, keep) * f_ref[k, terms[i][t][1]]
                h_ref[i, :, k * chans : (k + 1) * chans] = acc.astype(jnp.bfloat16)
        first, count = rows[0], len(rows)
        flat = (count * cols, chans)
        mixed = jnp.dot(
            h_ref[pl.ds(first, count)].reshape(count * cols, basis * chans), mix_ref[...],
            preferred_element_type=jnp.float32,
        )
        own_rows = fields_ref[pl.ds(first, count)].astype(jnp.float32).reshape(flat)
        out_ref[pl.ds(first, count)] = (own_rows + mixed).astype(out_ref.dtype).reshape(
            (count, cols, chans)
        )

    half = out_rows // 2

    def top_half():
        @pl.when(has_down)
        def _():
            c_up.wait_recv()
            for c in h_up:
                c.wait_recv()
            filter_halo(top_c, top_h, 0, 0)

        @pl.when(lat == 0)
        def _():
            zero_rows(0)

        finish(list(range(half)), lambda i: range(0, HALO - i), lambda r: r < HALO)

    def bottom_half():
        @pl.when(has_up)
        def _():
            c_dn.wait_recv()
            for c in h_dn:
                c.wait_recv()
            filter_halo(bot_c, bot_h, HALO, HALO + out_rows)

        @pl.when(lat == last)
        def _():
            zero_rows(HALO + out_rows)

        finish(
            list(range(half, out_rows)),
            lambda i: range(out_rows + 1 - i, band_len),
            lambda r: r >= HALO + out_rows,
        )

    far_above = lax.rem(lat, X_CHIPS) == 0

    @pl.when(jnp.logical_not(far_above))
    def _():
        top_half()
        bottom_half()

    @pl.when(far_above)
    def _():
        bottom_half()
        top_half()

    for c in h_side:
        c.wait_send()

    @pl.when(has_up)
    def _():
        c_up.wait_send()
        for c in h_up:
            c.wait_send()

    @pl.when(has_down)
    def _():
        c_dn.wait_send()
        for c in h_dn:
            c.wait_send()

    @pl.when(is_polar)
    def _():
        pol.wait_send()


def shards(fields, lon_taps, lat_taps, cycle_taps, band_start, band_width, mixing):
    row_count, col_count, chan_count = fields.shape
    basis_count = lon_taps.shape[1]
    taps_count = lon_taps.shape[2]
    reach_cells = (taps_count - 1) // 2
    band_len = lat_taps.shape[2]
    polar_rows = row_count // 2
    lat_count = lax.axis_size("lat")
    lon_count = lax.axis_size("lon")
    assert lon_count == 2 and reach_cells == HALO
    cycle_len = lon_count * col_count
    lat_pos = lax.axis_index("lat")
    ext_rows = row_count + 2 * HALO
    total_rows = lat_count * row_count

    mix_flat = mixing.reshape(basis_count * chan_count, chan_count)
    lon_t = jnp.transpose(lon_taps, (2, 1, 0))
    lat_t = jnp.transpose(lat_taps, (2, 1, 0))

    hbm = pl.BlockSpec(memory_space=pl.ANY)
    kernel = functools.partial(
        conv_kernel, basis_count, row_count, band_len, polar_rows, total_rows
    )
    halo_block = pltpu.VMEM((HALO, col_count, chan_count), fields.dtype)
    return copy_out(pl.pallas_call(
        kernel,
        out_shape=jax.ShapeDtypeStruct(fields.shape, fields.dtype),
        in_specs=[hbm] * 6 + [pl.BlockSpec(memory_space=pltpu.HBM)],
        out_specs=pl.BlockSpec(memory_space=pltpu.VMEM),
        scratch_shapes=[
            pltpu.SMEM(band_start.shape, band_start.dtype),
            pltpu.SMEM(band_width.shape, band_width.dtype),
            pltpu.VMEM(lat_t.shape, lat_t.dtype),
            pltpu.VMEM(lon_t.shape, lon_t.dtype),
            pltpu.VMEM((basis_count, ext_rows, LANES), jnp.float32),
            pltpu.VMEM(cycle_taps.shape, cycle_taps.dtype),
            pltpu.VMEM(fields.shape, fields.dtype),
            pltpu.VMEM(mix_flat.shape, mix_flat.dtype),
            halo_block,
            halo_block,
            halo_block,
            halo_block,
            pltpu.VMEM(fields.shape, fields.dtype),
            pltpu.VMEM((polar_rows, col_count, chan_count), fields.dtype),
            pltpu.VMEM((basis_count, ext_rows, col_count, chan_count), jnp.float32),
            pltpu.VMEM((row_count, basis_count, col_count, chan_count), jnp.float32),
            pltpu.VMEM((row_count, col_count, basis_count * chan_count), jnp.bfloat16),
            pltpu.VMEM((2 * HALO, basis_count * col_count, 2 * col_count), jnp.bfloat16),
            pltpu.SemaphoreType.DMA((9,)),
            pltpu.SemaphoreType.DMA((9,)),
            pltpu.SemaphoreType.DMA((7,)),
        ],
        compiler_params=pltpu.CompilerParams(
            vmem_limit_bytes=67043328, collective_id=0, has_side_effects=True
        ),
    )(band_start, band_width, lat_t, lon_t, cycle_taps, fields, mix_flat))


def copy_out(block):
    pieces = 4
    step = block.shape[0] // pieces

    def body(src, dst, stage, sem_in, sem_out):
        ins = [
            pltpu.make_async_copy(src.at[pl.ds(n * step, step)], stage.at[pl.ds(n * step, step)], sem_in.at[n])
            for n in range(pieces)
        ]
        outs = [
            pltpu.make_async_copy(stage.at[pl.ds(n * step, step)], dst.at[pl.ds(n * step, step)], sem_out.at[n])
            for n in range(pieces)
        ]
        for c in ins:
            c.start()
        for c_in, c_out in zip(ins, outs):
            c_in.wait()
            c_out.start()
        for c in outs:
            c.wait()

    hbm = pl.BlockSpec(memory_space=pl.ANY)
    return pl.pallas_call(
        body,
        out_shape=jax.ShapeDtypeStruct(block.shape, block.dtype),
        in_specs=[hbm],
        out_specs=hbm,
        scratch_shapes=[
            pltpu.VMEM(block.shape, block.dtype),
            pltpu.SemaphoreType.DMA((pieces,)),
            pltpu.SemaphoreType.DMA((pieces,)),
        ],
    )(block)


def solution(mesh):
    in_specs = (
        P(("ens", "lat"), "lon", None),
        P(),
        P("lat", None, None),
        P(),
        P("lat"),
        P("lat"),
        P(),
    )
    out_specs = P(("ens", "lat"), "lon", None)
    return jax.shard_map(shards, mesh=mesh, in_specs=in_specs, out_specs=out_specs, check_vma=False)
```

```python
import functools

import jax
import jax.numpy as jnp
from jax import lax
from jax.experimental import pallas as pl
from jax.experimental.pallas import tpu as pltpu
from jax.sharding import PartitionSpec as P

HALO = 4
LANES = 128
EDGE = 16
X_CHIPS = 4
MESH = pl.DeviceIdType.MESH


def rolled(vec, rows):
    return pltpu.roll(jnp.broadcast_to(vec, (rows, LANES)), 0, 1, stride=1, stride_axis=0)


def conv_kernel(basis, out_rows, band_len, polar_count, total_rows,
                start_hbm, width_hbm, lat_hbm, lon_hbm, cyc_hbm, fields_hbm, mix_hbm, out_ref,
                start_s, width_s, lat_v, tap_v, tap_u, cyc_v, fields_ref, mix_ref,
                top_c, bot_c, top_h, bot_h, own_h, polar_o, f_ref, acc_ref, h_ref, tm_ref, tc_ref,
                send_sem, recv_sem, load_sem):
    cols = out_ref.shape[1]
    chans = out_ref.shape[2]
    ext_rows = out_rows + 2 * HALO
    lat = lax.axis_index("lat")
    loads = [
        pltpu.make_async_copy(fields_hbm, fields_ref, load_sem.at[0]),
        pltpu.make_async_copy(lon_hbm, tap_v, load_sem.at[1]),
        pltpu.make_async_copy(start_hbm, start_s, load_sem.at[2]),
        pltpu.make_async_copy(width_hbm, width_s, load_sem.at[3]),
        pltpu.make_async_copy(lat_hbm, lat_v, load_sem.at[4]),
        pltpu.make_async_copy(cyc_hbm, cyc_v, load_sem.at[5]),
        pltpu.make_async_copy(mix_hbm, mix_ref, load_sem.at[6]),
    ]
    for c in loads:
        c.start()
    lon = lax.axis_index("lon")
    last = lax.axis_size("lat") - 1
    has_up = lat < last
    has_down = lat > 0
    is_polar = (lat == 0) | (lat == last)
    slot = jnp.minimum(lat, 1) * (out_rows - polar_count)
    up = jnp.minimum(lat + 1, last)
    down = jnp.maximum(lat - 1, 0)
    side = 1 - lon

    middle = pl.ds(EDGE, cols - 2 * EDGE)
    for buf in (top_h, bot_h, own_h):
        buf[:, middle] = jnp.zeros((buf.shape[0], cols - 2 * EDGE, chans), buf.dtype)

    barrier = pltpu.get_barrier_semaphore()

    def greet(where):
        pl.semaphore_signal(barrier, 1, device_id=where, device_id_type=MESH)

    greet({"lat": lat, "lon": side})

    @pl.when(has_up)
    def _():
        greet({"lat": up, "lon": lon})
        greet({"lat": up, "lon": side})

    @pl.when(has_down)
    def _():
        greet({"lat": down, "lon": lon})
        greet({"lat": down, "lon": side})

    pl.semaphore_wait(barrier, 1 + 2 * (has_up.astype(jnp.int32) + has_down.astype(jnp.int32)))

    def copy(n, src, dst, where):
        return pltpu.make_async_remote_copy(
            src_ref=src, dst_ref=dst, send_sem=send_sem.at[n], recv_sem=recv_sem.at[n],
            device_id=where, device_id_type=MESH)

    lo_rows = pl.ds(0, HALO)
    hi_rows = pl.ds(out_rows - HALO, HALO)
    first_cols = pl.ds(0, EDGE)
    last_cols = pl.ds(cols - EDGE, EDGE)
    c_up = copy(0, fields_hbm.at[hi_rows], top_c, {"lat": up, "lon": lon})
    c_dn = copy(1, fields_hbm.at[lo_rows], bot_c, {"lat": down, "lon": lon})
    h_up = [
        copy(2, fields_hbm.at[hi_rows, first_cols], top_h.at[:, first_cols], {"lat": up, "lon": side}),
        copy(3, fields_hbm.at[hi_rows, last_cols], top_h.at[:, last_cols], {"lat": up, "lon": side}),
    ]
    h_dn = [
        copy(4, fields_hbm.at[lo_rows, first_cols], bot_h.at[:, first_cols], {"lat": down, "lon": side}),
        copy(5, fields_hbm.at[lo_rows, last_cols], bot_h.at[:, last_cols], {"lat": down, "lon": side}),
    ]
    h_side = [
        copy(6, fields_hbm.at[:, first_cols], own_h.at[:, first_cols], {"lat": lat, "lon": side}),
        copy(7, fields_hbm.at[:, last_cols], own_h.at[:, last_cols], {"lat": lat, "lon": side}),
    ]
    pol = copy(8, fields_hbm.at[pl.ds(slot, polar_count)], polar_o, {"lat": lat, "lon": side})

    @pl.when(has_up)
    def _():
        c_up.start()

    @pl.when(has_down)
    def _():
        c_dn.start()

    @pl.when(has_up)
    def _():
        for c in h_up:
            c.start()

    @pl.when(has_down)
    def _():
        for c in h_dn:
            c.start()

    for c in h_side:
        c.start()

    @pl.when(is_polar)
    def _():
        pol.start()

    row_id = lax.broadcasted_iota(jnp.int32, (cols, LANES), 0)
    col_id = lax.broadcasted_iota(jnp.int32, (cols, LANES), 1)
    near = jnp.abs(col_id - row_id) <= HALO

    near_edge = jnp.concatenate([near[:8], near[cols - 8 :]], axis=0)

    def build(e):
        centred = tap_u[:, e]
        main, corr = [], []
        for k in range(basis):
            u = centred[k : k + 1]
            u_hi = u.astype(jnp.bfloat16).astype(jnp.float32)
            w_hi = rolled(u_hi, cols)
            w_lo = rolled(u - u_hi, cols)
            main.append(
                jnp.concatenate(
                    [jnp.where(near, w_hi, 0.0), jnp.where(near, w_lo, 0.0)], axis=1
                ).astype(jnp.bfloat16)
            )
            e_hi = jnp.concatenate([w_hi[:8], w_hi[cols - 8 :]], axis=0)
            e_lo = jnp.concatenate([w_lo[:8], w_lo[cols - 8 :]], axis=0)
            corr.append(
                jnp.concatenate(
                    [jnp.where(near_edge, 0.0, e_hi), jnp.where(near_edge, 0.0, e_lo)], axis=1
                ).astype(jnp.bfloat16)
            )
        return jnp.concatenate(main, axis=0), jnp.concatenate(corr, axis=0)

    def apply(xc, xe, tall, tall_e, e):
        rhs_c = jnp.concatenate([xc, xc], axis=0)
        rhs_e = jnp.concatenate([xe, xe], axis=0)
        y = jnp.dot(tall, rhs_c, preferred_element_type=jnp.float32)
        yc = jnp.dot(tall_e, rhs_e, preferred_element_type=jnp.float32)
        for k in range(basis):
            v = y[k * cols : (k + 1) * cols]
            c = yc[k * 16 : (k + 1) * 16]
            v = jnp.concatenate([v[:8] + c[:8], v[8 : cols - 8], v[cols - 8 :] + c[8:]], axis=0)
            f_ref[k, e] = v.astype(jnp.bfloat16).astype(jnp.float32)

    def filter_rows(c_ref, e_ref, count, first):
        def filter_row(r, carry):
            tall, tall_e = build(first + r)
            apply(c_ref[r], e_ref[r], tall, tall_e, first + r)
            return carry

        lax.fori_loop(0, count, filter_row, 0)

    def build_halo(slot, first):
        def one(r, carry):
            tall, tall_e = build(first + r)
            tm_ref[slot + r] = tall
            tc_ref[slot + r] = tall_e
            return carry

        lax.fori_loop(0, HALO, one, 0)

    def filter_halo(c_ref, e_ref, slot, first):
        def one(r, carry):
            apply(c_ref[r], e_ref[r], tm_ref[slot + r], tc_ref[slot + r], first + r)
            return carry

        lax.fori_loop(0, HALO, one, 0)

    def zero_rows(first):
        f_ref[:, pl.ds(first, HALO)] = jnp.zeros((basis, HALO, cols, chans), jnp.float32)

    for n in (0, 1):
        loads[n].wait()
    taps_count = tap_v.shape[0]
    shift = lax.rem(total_rows - (lat * out_rows - HALO) + total_rows, total_rows)
    for k in range(basis):
        a = tap_v[:, k, :]
        a = jnp.concatenate([a, jnp.zeros((2 * 8 - taps_count, total_rows), jnp.float32)], axis=0)
        a = pltpu.roll(a, shift, 1)[:, :LANES]
        a = jnp.transpose(a)
        a = jnp.concatenate([a, jnp.zeros((LANES, LANES - 2 * 8), jnp.float32)], axis=1)
        tap_u[k] = pltpu.roll(a, LANES - HALO, 1)[:ext_rows]
    for c in h_side:
        c.wait_recv()
    filter_rows(fields_ref, own_h, out_rows, HALO)

    build_halo(0, 0)
    build_halo(HALO, HALO + out_rows)
    loads[5].wait()

    def polar_rows(pole):
        pol.wait_recv()
        upper = col_id >= row_id
        for k in range(basis):
            for p in range(polar_count):
                a = cyc_v[k, pl.ds(pole * polar_count + p, 1), :].astype(jnp.float32)
                ra = rolled(a[:, :LANES], cols)
                rb = rolled(a[:, LANES:], cols)
                circ_t = jnp.concatenate(
                    [jnp.where(upper, ra, rb), jnp.where(upper, rb, ra)], axis=0
                )
                circ = jnp.transpose(circ_t).astype(jnp.bfloat16)
                g = jnp.concatenate([fields_ref[slot + p], polar_o[p]], axis=0)
                y = jnp.dot(circ, g, preferred_element_type=jnp.float32)
                f_ref[k, HALO + slot + p] = y.astype(jnp.bfloat16).astype(jnp.float32)

    @pl.when(lat == 0)
    def _():
        polar_rows(0)

    @pl.when(lat == last)
    def _():
        polar_rows(1)

    for n in (2, 3, 4, 6):
        loads[n].wait()
    base_row = lat * out_rows
    lw_all = lat_v[...].astype(jnp.float32)
    terms = []
    for i in range(out_rows):
        begin = start_s[i]
        width = width_s[i]
        row_terms = []
        for t in range(band_len):
            source = begin + t
            ok = (t < width) & (source >= 0) & (source < total_rows)
            r = jnp.clip(source - base_row + HALO, 0, ext_rows - 1)
            row_terms.append((ok, r))
        terms.append(row_terms)

    def weight(i, k, t, keep):
        ok, r = terms[i][t]
        return jnp.where(ok & keep(r), lw_all[t, k : k + 1, i : i + 1], 0.0)

    def own(r):
        return (r >= HALO) & (r < HALO + out_rows)

    for i in range(out_rows):
        for k in range(basis):
            acc = jnp.zeros((cols, chans), jnp.float32)
            for t in range(band_len):
                r = jnp.clip(terms[i][t][1], HALO, HALO + out_rows - 1)
                acc = acc + weight(i, k, t, own) * f_ref[k, r]
            acc_ref[i, k] = acc

    def finish(rows, steps, keep):
        for i in rows:
            for k in range(basis):
                acc = acc_ref[i, k]
                for t in steps(i):
                    acc = acc + weight(i, k, t, keep) * f_ref[k, terms[i][t][1]]
                h_ref[i, :, k * chans : (k + 1) * chans] = acc.astype(jnp.bfloat16)
        first, count = rows[0], len(rows)
        flat = (count * cols, chans)
        mixed = jnp.dot(
            h_ref[pl.ds(first, count)].reshape(count * cols, basis * chans), mix_ref[...],
            preferred_element_type=jnp.float32,
        )
        own_rows = fields_ref[pl.ds(first, count)].astype(jnp.float32).reshape(flat)
        out_ref[pl.ds(first, count)] = (own_rows + mixed).astype(out_ref.dtype).reshape(
            (count, cols, chans)
        )

    half = out_rows // 2

    def top_half():
        @pl.when(has_down)
        def _():
            c_up.wait_recv()
            for c in h_up:
                c.wait_recv()
            filter_halo(top_c, top_h, 0, 0)

        @pl.when(lat == 0)
        def _():
            zero_rows(0)

        finish(list(range(half)), lambda i: range(0, HALO - i), lambda r: r < HALO)

    def bottom_half():
        @pl.when(has_up)
        def _():
            c_dn.wait_recv()
            for c in h_dn:
                c.wait_recv()
            filter_halo(bot_c, bot_h, HALO, HALO + out_rows)

        @pl.when(lat == last)
        def _():
            zero_rows(HALO + out_rows)

        finish(
            list(range(half, out_rows)),
            lambda i: range(out_rows + 1 - i, band_len),
            lambda r: r >= HALO + out_rows,
        )

    far_above = lax.rem(lat, X_CHIPS) == 0

    @pl.when(jnp.logical_not(far_above))
    def _():
        top_half()
        bottom_half()

    @pl.when(far_above)
    def _():
        bottom_half()
        top_half()

    for c in h_side:
        c.wait_send()

    @pl.when(has_up)
    def _():
        c_up.wait_send()
        for c in h_up:
            c.wait_send()

    @pl.when(has_down)
    def _():
        c_dn.wait_send()
        for c in h_dn:
            c.wait_send()

    @pl.when(is_polar)
    def _():
        pol.wait_send()


def shards(fields, lon_taps, lat_taps, cycle_taps, band_start, band_width, mixing):
    row_count, col_count, chan_count = fields.shape
    basis_count = lon_taps.shape[1]
    taps_count = lon_taps.shape[2]
    reach_cells = (taps_count - 1) // 2
    band_len = lat_taps.shape[2]
    polar_rows = row_count // 2
    lat_count = lax.axis_size("lat")
    lon_count = lax.axis_size("lon")
    assert lon_count == 2 and reach_cells == HALO
    cycle_len = lon_count * col_count
    lat_pos = lax.axis_index("lat")
    ext_rows = row_count + 2 * HALO
    total_rows = lat_count * row_count

    mix_flat = mixing.reshape(basis_count * chan_count, chan_count)
    lon_t = jnp.transpose(lon_taps, (2, 1, 0))
    lat_t = jnp.transpose(lat_taps, (2, 1, 0))

    hbm = pl.BlockSpec(memory_space=pl.ANY)
    kernel = functools.partial(
        conv_kernel, basis_count, row_count, band_len, polar_rows, total_rows
    )
    halo_block = pltpu.VMEM((HALO, col_count, chan_count), fields.dtype)
    return copy_out(pl.pallas_call(
        kernel,
        out_shape=jax.ShapeDtypeStruct(fields.shape, fields.dtype),
        in_specs=[hbm] * 6 + [pl.BlockSpec(memory_space=pltpu.HBM)],
        out_specs=pl.BlockSpec(memory_space=pltpu.VMEM),
        scratch_shapes=[
            pltpu.SMEM(band_start.shape, band_start.dtype),
            pltpu.SMEM(band_width.shape, band_width.dtype),
            pltpu.VMEM(lat_t.shape, lat_t.dtype),
            pltpu.VMEM(lon_t.shape, lon_t.dtype),
            pltpu.VMEM((basis_count, ext_rows, LANES), jnp.float32),
            pltpu.VMEM(cycle_taps.shape, cycle_taps.dtype),
            pltpu.VMEM(fields.shape, fields.dtype),
            pltpu.VMEM(mix_flat.shape, mix_flat.dtype),
            halo_block,
            halo_block,
            halo_block,
            halo_block,
            pltpu.VMEM(fields.shape, fields.dtype),
            pltpu.VMEM((polar_rows, col_count, chan_count), fields.dtype),
            pltpu.VMEM((basis_count, ext_rows, col_count, chan_count), jnp.float32),
            pltpu.VMEM((row_count, basis_count, col_count, chan_count), jnp.float32),
            pltpu.VMEM((row_count, col_count, basis_count * chan_count), jnp.bfloat16),
            pltpu.VMEM((2 * HALO, basis_count * col_count, 2 * col_count), jnp.bfloat16),
            pltpu.VMEM((2 * HALO, basis_count * 16, 2 * col_count), jnp.bfloat16),
            pltpu.SemaphoreType.DMA((9,)),
            pltpu.SemaphoreType.DMA((9,)),
            pltpu.SemaphoreType.DMA((7,)),
        ],
        compiler_params=pltpu.CompilerParams(
            vmem_limit_bytes=67043328, collective_id=0, has_side_effects=True
        ),
    )(band_start, band_width, lat_t, lon_t, cycle_taps, fields, mix_flat))


def copy_out(block):
    pieces = 4
    step = block.shape[0] // pieces

    def body(src, dst, stage, sem_in, sem_out):
        ins = [
            pltpu.make_async_copy(src.at[pl.ds(n * step, step)], stage.at[pl.ds(n * step, step)], sem_in.at[n])
            for n in range(pieces)
        ]
        outs = [
            pltpu.make_async_copy(stage.at[pl.ds(n * step, step)], dst.at[pl.ds(n * step, step)], sem_out.at[n])
            for n in range(pieces)
        ]
        for c in ins:
            c.start()
        for c_in, c_out in zip(ins, outs):
            c_in.wait()
            c_out.start()
        for c in outs:
            c.wait()

    hbm = pl.BlockSpec(memory_space=pl.ANY)
    return pl.pallas_call(
        body,
        out_shape=jax.ShapeDtypeStruct(block.shape, block.dtype),
        in_specs=[hbm],
        out_specs=hbm,
        scratch_shapes=[
            pltpu.VMEM(block.shape, block.dtype),
            pltpu.SemaphoreType.DMA((pieces,)),
            pltpu.SemaphoreType.DMA((pieces,)),
        ],
    )(block)


def solution(mesh):
    in_specs = (
        P(("ens", "lat"), "lon", None),
        P(),
        P("lat", None, None),
        P(),
        P("lat"),
        P("lat"),
        P(),
    )
    out_specs = P(("ens", "lat"), "lon", None)
    return jax.shard_map(shards, mesh=mesh, in_specs=in_specs, out_specs=out_specs, check_vma=False)
```

```python
import functools

import jax
import jax.numpy as jnp
from jax import lax
from jax.experimental import pallas as pl
from jax.experimental.pallas import tpu as pltpu
from jax.sharding import PartitionSpec as P

HALO = 4
LANES = 128
EDGE = 16
X_CHIPS = 4
MESH = pl.DeviceIdType.MESH


def rolled(vec, rows):
    return pltpu.roll(jnp.broadcast_to(vec, (rows, LANES)), 0, 1, stride=1, stride_axis=0)


def conv_kernel(basis, out_rows, band_len, polar_count, total_rows,
                start_hbm, width_hbm, lat_hbm, lon_hbm, cyc_hbm, fields_hbm, mix_hbm, out_ref,
                start_s, width_s, lat_v, tap_v, tap_u, cyc_v, fields_ref, mix_ref,
                top_c, bot_c, top_h, bot_h, own_h, polar_o, f_ref, acc_ref, h_ref, tm_ref, tc_ref,
                send_sem, recv_sem, load_sem):
    cols = out_ref.shape[1]
    chans = out_ref.shape[2]
    ext_rows = out_rows + 2 * HALO
    lat = lax.axis_index("lat")
    loads = [
        pltpu.make_async_copy(fields_hbm, fields_ref, load_sem.at[0]),
        pltpu.make_async_copy(lon_hbm, tap_v, load_sem.at[1]),
        pltpu.make_async_copy(start_hbm, start_s, load_sem.at[2]),
        pltpu.make_async_copy(width_hbm, width_s, load_sem.at[3]),
        pltpu.make_async_copy(lat_hbm, lat_v, load_sem.at[4]),
        pltpu.make_async_copy(cyc_hbm, cyc_v, load_sem.at[5]),
        pltpu.make_async_copy(mix_hbm, mix_ref, load_sem.at[6]),
    ]
    for c in loads:
        c.start()
    lon = lax.axis_index("lon")
    last = lax.axis_size("lat") - 1
    has_up = lat < last
    has_down = lat > 0
    is_polar = (lat == 0) | (lat == last)
    slot = jnp.minimum(lat, 1) * (out_rows - polar_count)
    up = jnp.minimum(lat + 1, last)
    down = jnp.maximum(lat - 1, 0)
    side = 1 - lon

    middle = pl.ds(EDGE, cols - 2 * EDGE)
    for buf in (top_h, bot_h, own_h):
        buf[:, middle] = jnp.zeros((buf.shape[0], cols - 2 * EDGE, chans), buf.dtype)

    barrier = pltpu.get_barrier_semaphore()

    def greet(where):
        pl.semaphore_signal(barrier, 1, device_id=where, device_id_type=MESH)

    greet({"lat": lat, "lon": side})

    @pl.when(has_up)
    def _():
        greet({"lat": up, "lon": lon})
        greet({"lat": up, "lon": side})

    @pl.when(has_down)
    def _():
        greet({"lat": down, "lon": lon})
        greet({"lat": down, "lon": side})

    pl.semaphore_wait(barrier, 1 + 2 * (has_up.astype(jnp.int32) + has_down.astype(jnp.int32)))

    def copy(n, src, dst, where):
        return pltpu.make_async_remote_copy(
            src_ref=src, dst_ref=dst, send_sem=send_sem.at[n], recv_sem=recv_sem.at[n],
            device_id=where, device_id_type=MESH)

    lo_rows = pl.ds(0, HALO)
    hi_rows = pl.ds(out_rows - HALO, HALO)
    first_cols = pl.ds(0, EDGE)
    last_cols = pl.ds(cols - EDGE, EDGE)
    c_up = copy(0, fields_hbm.at[hi_rows], top_c, {"lat": up, "lon": lon})
    c_dn = copy(1, fields_hbm.at[lo_rows], bot_c, {"lat": down, "lon": lon})
    h_up = [
        copy(2, fields_hbm.at[hi_rows, first_cols], top_h.at[:, first_cols], {"lat": up, "lon": side}),
        copy(3, fields_hbm.at[hi_rows, last_cols], top_h.at[:, last_cols], {"lat": up, "lon": side}),
    ]
    h_dn = [
        copy(4, fields_hbm.at[lo_rows, first_cols], bot_h.at[:, first_cols], {"lat": down, "lon": side}),
        copy(5, fields_hbm.at[lo_rows, last_cols], bot_h.at[:, last_cols], {"lat": down, "lon": side}),
    ]
    h_side = [
        copy(6, fields_hbm.at[:, first_cols], own_h.at[:, first_cols], {"lat": lat, "lon": side}),
        copy(7, fields_hbm.at[:, last_cols], own_h.at[:, last_cols], {"lat": lat, "lon": side}),
    ]
    pol = copy(8, fields_hbm.at[pl.ds(slot, polar_count)], polar_o, {"lat": lat, "lon": side})

    for c in h_side:
        c.start()

    @pl.when(has_up)
    def _():
        c_up.start()
        for c in h_up:
            c.start()

    @pl.when(has_down)
    def _():
        c_dn.start()
        for c in h_dn:
            c.start()

    @pl.when(is_polar)
    def _():
        pol.start()

    row_id = lax.broadcasted_iota(jnp.int32, (cols, LANES), 0)
    col_id = lax.broadcasted_iota(jnp.int32, (cols, LANES), 1)
    near = jnp.abs(col_id - row_id) <= HALO

    near_edge = jnp.concatenate([near[:8], near[cols - 8 :]], axis=0)

    def build(e):
        centred = tap_u[:, e]
        main, corr = [], []
        for k in range(basis):
            u = centred[k : k + 1]
            u_hi = u.astype(jnp.bfloat16).astype(jnp.float32)
            w_hi = rolled(u_hi, cols)
            w_lo = rolled(u - u_hi, cols)
            main.append(
                jnp.concatenate(
                    [jnp.where(near, w_hi, 0.0), jnp.where(near, w_lo, 0.0)], axis=1
                ).astype(jnp.bfloat16)
            )
            e_hi = jnp.concatenate([w_hi[:8], w_hi[cols - 8 :]], axis=0)
            e_lo = jnp.concatenate([w_lo[:8], w_lo[cols - 8 :]], axis=0)
            corr.append(
                jnp.concatenate(
                    [jnp.where(near_edge, 0.0, e_hi), jnp.where(near_edge, 0.0, e_lo)], axis=1
                ).astype(jnp.bfloat16)
            )
        return jnp.concatenate(main, axis=0), jnp.concatenate(corr, axis=0)

    def apply(xc, xe, tall, tall_e, e):
        rhs_c = jnp.concatenate([xc, xc], axis=0)
        rhs_e = jnp.concatenate([xe, xe], axis=0)
        y = jnp.dot(tall, rhs_c, preferred_element_type=jnp.float32)
        yc = jnp.dot(tall_e, rhs_e, preferred_element_type=jnp.float32)
        for k in range(basis):
            v = y[k * cols : (k + 1) * cols]
            c = yc[k * 16 : (k + 1) * 16]
            v = jnp.concatenate([v[:8] + c[:8], v[8 : cols - 8], v[cols - 8 :] + c[8:]], axis=0)
            f_ref[k, e] = v.astype(jnp.bfloat16).astype(jnp.float32)

    def filter_rows(c_ref, e_ref, count, first):
        def filter_row(r, carry):
            tall, tall_e = build(first + r)
            apply(c_ref[r], e_ref[r], tall, tall_e, first + r)
            return carry

        lax.fori_loop(0, count, filter_row, 0)

    def build_halo(slot, first):
        def one(r, carry):
            tall, tall_e = build(first + r)
            tm_ref[slot + r] = tall
            tc_ref[slot + r] = tall_e
            return carry

        lax.fori_loop(0, HALO, one, 0)

    def filter_halo(c_ref, e_ref, slot, first):
        for r in range(HALO):
            apply(c_ref[r], e_ref[r], tm_ref[slot + r], tc_ref[slot + r], first + r)

    def zero_rows(first):
        f_ref[:, pl.ds(first, HALO)] = jnp.zeros((basis, HALO, cols, chans), jnp.float32)

    for n in (0, 1):
        loads[n].wait()
    taps_count = tap_v.shape[0]
    shift = lax.rem(total_rows - (lat * out_rows - HALO) + total_rows, total_rows)
    for k in range(basis):
        a = tap_v[:, k, :]
        a = jnp.concatenate([a, jnp.zeros((2 * 8 - taps_count, total_rows), jnp.float32)], axis=0)
        a = pltpu.roll(a, shift, 1)[:, :LANES]
        a = jnp.transpose(a)
        a = jnp.concatenate([a, jnp.zeros((LANES, LANES - 2 * 8), jnp.float32)], axis=1)
        tap_u[k] = pltpu.roll(a, LANES - HALO, 1)[:ext_rows]
    for c in h_side:
        c.wait_recv()
    filter_rows(fields_ref, own_h, out_rows, HALO)

    build_halo(0, 0)
    build_halo(HALO, HALO + out_rows)
    loads[5].wait()

    def polar_rows(pole):
        pol.wait_recv()
        upper = col_id >= row_id
        for k in range(basis):
            for p in range(polar_count):
                a = cyc_v[k, pl.ds(pole * polar_count + p, 1), :].astype(jnp.float32)
                ra = rolled(a[:, :LANES], cols)
                rb = rolled(a[:, LANES:], cols)
                circ_t = jnp.concatenate(
                    [jnp.where(upper, ra, rb), jnp.where(upper, rb, ra)], axis=0
                )
                circ = jnp.transpose(circ_t).astype(jnp.bfloat16)
                g = jnp.concatenate([fields_ref[slot + p], polar_o[p]], axis=0)
                y = jnp.dot(circ, g, preferred_element_type=jnp.float32)
                f_ref[k, HALO + slot + p] = y.astype(jnp.bfloat16).astype(jnp.float32)

    @pl.when(lat == 0)
    def _():
        polar_rows(0)

    @pl.when(lat == last)
    def _():
        polar_rows(1)

    for n in (2, 3, 4, 6):
        loads[n].wait()
    base_row = lat * out_rows
    lw_all = lat_v[...].astype(jnp.float32)
    terms = []
    for i in range(out_rows):
        begin = start_s[i]
        width = width_s[i]
        row_terms = []
        for t in range(band_len):
            source = begin + t
            ok = (t < width) & (source >= 0) & (source < total_rows)
            r = jnp.clip(source - base_row + HALO, 0, ext_rows - 1)
            row_terms.append((ok, r))
        terms.append(row_terms)

    def weight(i, k, t, keep):
        ok, r = terms[i][t]
        return jnp.where(ok & keep(r), lw_all[t, k : k + 1, i : i + 1], 0.0)

    def own(r):
        return (r >= HALO) & (r < HALO + out_rows)

    for i in range(out_rows):
        for k in range(basis):
            acc = jnp.zeros((cols, chans), jnp.float32)
            for t in range(band_len):
                r = jnp.clip(terms[i][t][1], HALO, HALO + out_rows - 1)
                acc = acc + weight(i, k, t, own) * f_ref[k, r]
            acc_ref[i, k] = acc

    def finish(rows, steps, keep):
        for i in rows:
            for k in range(basis):
                acc = acc_ref[i, k]
                for t in steps(i):
                    acc = acc + weight(i, k, t, keep) * f_ref[k, terms[i][t][1]]
                h_ref[i, :, k * chans : (k + 1) * chans] = acc.astype(jnp.bfloat16)
        first, count = rows[0], len(rows)
        flat = (count * cols, chans)
        mixed = jnp.dot(
            h_ref[pl.ds(first, count)].reshape(count * cols, basis * chans), mix_ref[...],
            preferred_element_type=jnp.float32,
        )
        own_rows = fields_ref[pl.ds(first, count)].astype(jnp.float32).reshape(flat)
        out_ref[pl.ds(first, count)] = (own_rows + mixed).astype(out_ref.dtype).reshape(
            (count, cols, chans)
        )

    half = out_rows // 2

    def top_half():
        @pl.when(has_down)
        def _():
            c_up.wait_recv()
            for c in h_up:
                c.wait_recv()
            filter_halo(top_c, top_h, 0, 0)

        @pl.when(lat == 0)
        def _():
            zero_rows(0)

        finish(list(range(half)), lambda i: range(0, HALO - i), lambda r: r < HALO)

    def bottom_half():
        @pl.when(has_up)
        def _():
            c_dn.wait_recv()
            for c in h_dn:
                c.wait_recv()
            filter_halo(bot_c, bot_h, HALO, HALO + out_rows)

        @pl.when(lat == last)
        def _():
            zero_rows(HALO + out_rows)

        finish(
            list(range(half, out_rows)),
            lambda i: range(out_rows + 1 - i, band_len),
            lambda r: r >= HALO + out_rows,
        )

    far_above = lax.rem(lat, X_CHIPS) == 0

    @pl.when(jnp.logical_not(far_above))
    def _():
        top_half()
        bottom_half()

    @pl.when(far_above)
    def _():
        bottom_half()
        top_half()

    for c in h_side:
        c.wait_send()

    @pl.when(has_up)
    def _():
        c_up.wait_send()
        for c in h_up:
            c.wait_send()

    @pl.when(has_down)
    def _():
        c_dn.wait_send()
        for c in h_dn:
            c.wait_send()

    @pl.when(is_polar)
    def _():
        pol.wait_send()


def shards(fields, lon_taps, lat_taps, cycle_taps, band_start, band_width, mixing):
    row_count, col_count, chan_count = fields.shape
    basis_count = lon_taps.shape[1]
    taps_count = lon_taps.shape[2]
    reach_cells = (taps_count - 1) // 2
    band_len = lat_taps.shape[2]
    polar_rows = row_count // 2
    lat_count = lax.axis_size("lat")
    lon_count = lax.axis_size("lon")
    assert lon_count == 2 and reach_cells == HALO
    cycle_len = lon_count * col_count
    lat_pos = lax.axis_index("lat")
    ext_rows = row_count + 2 * HALO
    total_rows = lat_count * row_count

    mix_flat = mixing.reshape(basis_count * chan_count, chan_count)
    lon_t = jnp.transpose(lon_taps, (2, 1, 0))
    lat_t = jnp.transpose(lat_taps, (2, 1, 0))

    hbm = pl.BlockSpec(memory_space=pl.ANY)
    kernel = functools.partial(
        conv_kernel, basis_count, row_count, band_len, polar_rows, total_rows
    )
    halo_block = pltpu.VMEM((HALO, col_count, chan_count), fields.dtype)
    return copy_out(pl.pallas_call(
        kernel,
        out_shape=jax.ShapeDtypeStruct(fields.shape, fields.dtype),
        in_specs=[hbm] * 6 + [pl.BlockSpec(memory_space=pltpu.HBM)],
        out_specs=pl.BlockSpec(memory_space=pltpu.VMEM),
        scratch_shapes=[
            pltpu.SMEM(band_start.shape, band_start.dtype),
            pltpu.SMEM(band_width.shape, band_width.dtype),
            pltpu.VMEM(lat_t.shape, lat_t.dtype),
            pltpu.VMEM(lon_t.shape, lon_t.dtype),
            pltpu.VMEM((basis_count, ext_rows, LANES), jnp.float32),
            pltpu.VMEM(cycle_taps.shape, cycle_taps.dtype),
            pltpu.VMEM(fields.shape, fields.dtype),
            pltpu.VMEM(mix_flat.shape, mix_flat.dtype),
            halo_block,
            halo_block,
            halo_block,
            halo_block,
            pltpu.VMEM(fields.shape, fields.dtype),
            pltpu.VMEM((polar_rows, col_count, chan_count), fields.dtype),
            pltpu.VMEM((basis_count, ext_rows, col_count, chan_count), jnp.float32),
            pltpu.VMEM((row_count, basis_count, col_count, chan_count), jnp.float32),
            pltpu.VMEM((row_count, col_count, basis_count * chan_count), jnp.bfloat16),
            pltpu.VMEM((2 * HALO, basis_count * col_count, 2 * col_count), jnp.bfloat16),
            pltpu.VMEM((2 * HALO, basis_count * 16, 2 * col_count), jnp.bfloat16),
            pltpu.SemaphoreType.DMA((9,)),
            pltpu.SemaphoreType.DMA((9,)),
            pltpu.SemaphoreType.DMA((7,)),
        ],
        compiler_params=pltpu.CompilerParams(
            vmem_limit_bytes=67043328, collective_id=0, has_side_effects=True
        ),
    )(band_start, band_width, lat_t, lon_t, cycle_taps, fields, mix_flat))


def copy_out(block):
    pieces = 4
    step = block.shape[0] // pieces

    def body(src, dst, stage, sem_in, sem_out):
        ins = [
            pltpu.make_async_copy(src.at[pl.ds(n * step, step)], stage.at[pl.ds(n * step, step)], sem_in.at[n])
            for n in range(pieces)
        ]
        outs = [
            pltpu.make_async_copy(stage.at[pl.ds(n * step, step)], dst.at[pl.ds(n * step, step)], sem_out.at[n])
            for n in range(pieces)
        ]
        for c in ins:
            c.start()
        for c_in, c_out in zip(ins, outs):
            c_in.wait()
            c_out.start()
        for c in outs:
            c.wait()

    hbm = pl.BlockSpec(memory_space=pl.ANY)
    return pl.pallas_call(
        body,
        out_shape=jax.ShapeDtypeStruct(block.shape, block.dtype),
        in_specs=[hbm],
        out_specs=hbm,
        scratch_shapes=[
            pltpu.VMEM(block.shape, block.dtype),
            pltpu.SemaphoreType.DMA((pieces,)),
            pltpu.SemaphoreType.DMA((pieces,)),
        ],
    )(block)


def solution(mesh):
    in_specs = (
        P(("ens", "lat"), "lon", None),
        P(),
        P("lat", None, None),
        P(),
        P("lat"),
        P("lat"),
        P(),
    )
    out_specs = P(("ens", "lat"), "lon", None)
    return jax.shard_map(shards, mesh=mesh, in_specs=in_specs, out_specs=out_specs, check_vma=False)
```

```python
import functools

import jax
import jax.numpy as jnp
from jax import lax
from jax.experimental import pallas as pl
from jax.experimental.pallas import tpu as pltpu
from jax.sharding import PartitionSpec as P

HALO = 4
LANES = 128
EDGE = 16
X_CHIPS = 4
MESH = pl.DeviceIdType.MESH


def rolled(vec, rows):
    return pltpu.roll(jnp.broadcast_to(vec, (rows, LANES)), 0, 1, stride=1, stride_axis=0)


def conv_kernel(basis, out_rows, band_len, polar_count, total_rows,
                start_hbm, width_hbm, lat_hbm, lon_hbm, cyc_hbm, fields_hbm, mix_hbm, out_ref,
                start_s, width_s, lat_v, tap_v, tap_u, cyc_v, fields_ref, mix_ref,
                top_c, bot_c, top_h, bot_h, own_h, polar_o, f_ref, acc_ref, h_ref, tm_ref, tc_ref,
                send_sem, recv_sem, load_sem):
    cols = out_ref.shape[1]
    chans = out_ref.shape[2]
    ext_rows = out_rows + 2 * HALO
    lat = lax.axis_index("lat")
    loads = [
        pltpu.make_async_copy(fields_hbm, fields_ref, load_sem.at[0]),
        pltpu.make_async_copy(lon_hbm, tap_v, load_sem.at[1]),
        pltpu.make_async_copy(start_hbm, start_s, load_sem.at[2]),
        pltpu.make_async_copy(width_hbm, width_s, load_sem.at[3]),
        pltpu.make_async_copy(lat_hbm, lat_v, load_sem.at[4]),
        pltpu.make_async_copy(cyc_hbm, cyc_v, load_sem.at[5]),
        pltpu.make_async_copy(mix_hbm, mix_ref, load_sem.at[6]),
    ]
    for c in loads:
        c.start()
    lon = lax.axis_index("lon")
    last = lax.axis_size("lat") - 1
    has_up = lat < last
    has_down = lat > 0
    is_polar = (lat == 0) | (lat == last)
    slot = jnp.minimum(lat, 1) * (out_rows - polar_count)
    up = jnp.minimum(lat + 1, last)
    down = jnp.maximum(lat - 1, 0)
    side = 1 - lon

    middle = pl.ds(EDGE, cols - 2 * EDGE)
    for buf in (top_h, bot_h, own_h):
        buf[:, middle] = jnp.zeros((buf.shape[0], cols - 2 * EDGE, chans), buf.dtype)

    barrier = pltpu.get_barrier_semaphore()

    def greet(where):
        pl.semaphore_signal(barrier, 1, device_id=where, device_id_type=MESH)

    greet({"lat": lat, "lon": side})

    @pl.when(has_up)
    def _():
        greet({"lat": up, "lon": lon})
        greet({"lat": up, "lon": side})

    @pl.when(has_down)
    def _():
        greet({"lat": down, "lon": lon})
        greet({"lat": down, "lon": side})

    pl.semaphore_wait(barrier, 1 + 2 * (has_up.astype(jnp.int32) + has_down.astype(jnp.int32)))

    def copy(n, src, dst, where):
        return pltpu.make_async_remote_copy(
            src_ref=src, dst_ref=dst, send_sem=send_sem.at[n], recv_sem=recv_sem.at[n],
            device_id=where, device_id_type=MESH)

    lo_rows = pl.ds(0, HALO)
    hi_rows = pl.ds(out_rows - HALO, HALO)
    first_cols = pl.ds(0, EDGE)
    last_cols = pl.ds(cols - EDGE, EDGE)
    c_up = copy(0, fields_hbm.at[hi_rows], top_c, {"lat": up, "lon": lon})
    c_dn = copy(1, fields_hbm.at[lo_rows], bot_c, {"lat": down, "lon": lon})
    h_up = [
        copy(2, fields_hbm.at[hi_rows, first_cols], top_h.at[:, first_cols], {"lat": up, "lon": side}),
        copy(3, fields_hbm.at[hi_rows, last_cols], top_h.at[:, last_cols], {"lat": up, "lon": side}),
    ]
    h_dn = [
        copy(4, fields_hbm.at[lo_rows, first_cols], bot_h.at[:, first_cols], {"lat": down, "lon": side}),
        copy(5, fields_hbm.at[lo_rows, last_cols], bot_h.at[:, last_cols], {"lat": down, "lon": side}),
    ]
    h_side = [
        copy(6, fields_hbm.at[:, first_cols], own_h.at[:, first_cols], {"lat": lat, "lon": side}),
        copy(7, fields_hbm.at[:, last_cols], own_h.at[:, last_cols], {"lat": lat, "lon": side}),
    ]
    pol = copy(8, fields_hbm.at[pl.ds(slot, polar_count)], polar_o, {"lat": lat, "lon": side})

    for c in h_side:
        c.start()

    @pl.when(has_up)
    def _():
        c_up.start()
        for c in h_up:
            c.start()

    @pl.when(has_down)
    def _():
        c_dn.start()
        for c in h_dn:
            c.start()

    @pl.when(is_polar)
    def _():
        pol.start()

    row_id = lax.broadcasted_iota(jnp.int32, (cols, LANES), 0)
    col_id = lax.broadcasted_iota(jnp.int32, (cols, LANES), 1)
    near = jnp.abs(col_id - row_id) <= HALO

    near_edge = jnp.concatenate([near[:8], near[cols - 8 :]], axis=0)

    def build(e):
        centred = tap_u[:, e]
        main, corr = [], []
        for k in range(basis):
            u = centred[k : k + 1]
            u_hi = u.astype(jnp.bfloat16).astype(jnp.float32)
            w_hi = rolled(u_hi, cols)
            w_lo = rolled(u - u_hi, cols)
            main.append(
                jnp.concatenate(
                    [jnp.where(near, w_hi, 0.0), jnp.where(near, w_lo, 0.0)], axis=1
                ).astype(jnp.bfloat16)
            )
            e_hi = jnp.concatenate([w_hi[:8], w_hi[cols - 8 :]], axis=0)
            e_lo = jnp.concatenate([w_lo[:8], w_lo[cols - 8 :]], axis=0)
            corr.append(
                jnp.concatenate(
                    [jnp.where(near_edge, 0.0, e_hi), jnp.where(near_edge, 0.0, e_lo)], axis=1
                ).astype(jnp.bfloat16)
            )
        return jnp.concatenate(main, axis=0), jnp.concatenate(corr, axis=0)

    def apply(xc, xe, tall, tall_e, e):
        rhs_c = jnp.concatenate([xc, xc], axis=0)
        rhs_e = jnp.concatenate([xe, xe], axis=0)
        y = jnp.dot(tall, rhs_c, preferred_element_type=jnp.float32)
        yc = jnp.dot(tall_e, rhs_e, preferred_element_type=jnp.float32)
        for k in range(basis):
            v = y[k * cols : (k + 1) * cols]
            c = yc[k * 16 : (k + 1) * 16]
            v = jnp.concatenate([v[:8] + c[:8], v[8 : cols - 8], v[cols - 8 :] + c[8:]], axis=0)
            f_ref[k, e] = v.astype(jnp.bfloat16).astype(jnp.float32)

    def filter_rows(c_ref, e_ref, count, first):
        def filter_row(r, carry):
            tall, tall_e = build(first + r)
            apply(c_ref[r], e_ref[r], tall, tall_e, first + r)
            return carry

        for r in range(count):
            filter_row(r, 0)

    def build_halo(slot, first):
        def one(r, carry):
            tall, tall_e = build(first + r)
            tm_ref[slot + r] = tall
            tc_ref[slot + r] = tall_e
            return carry

        lax.fori_loop(0, HALO, one, 0)

    def filter_halo(c_ref, e_ref, slot, first):
        for r in range(HALO):
            apply(c_ref[r], e_ref[r], tm_ref[slot + r], tc_ref[slot + r], first + r)

    def zero_rows(first):
        f_ref[:, pl.ds(first, HALO)] = jnp.zeros((basis, HALO, cols, chans), jnp.float32)

    for n in (0, 1):
        loads[n].wait()
    taps_count = tap_v.shape[0]
    shift = lax.rem(total_rows - (lat * out_rows - HALO) + total_rows, total_rows)
    for k in range(basis):
        a = tap_v[:, k, :]
        a = jnp.concatenate([a, jnp.zeros((2 * 8 - taps_count, total_rows), jnp.float32)], axis=0)
        a = pltpu.roll(a, shift, 1)[:, :LANES]
        a = jnp.transpose(a)
        a = jnp.concatenate([a, jnp.zeros((LANES, LANES - 2 * 8), jnp.float32)], axis=1)
        tap_u[k] = pltpu.roll(a, LANES - HALO, 1)[:ext_rows]
    for c in h_side:
        c.wait_recv()
    filter_rows(fields_ref, own_h, out_rows, HALO)

    build_halo(0, 0)
    build_halo(HALO, HALO + out_rows)
    loads[5].wait()

    def polar_rows(pole):
        pol.wait_recv()
        upper = col_id >= row_id
        for k in range(basis):
            for p in range(polar_count):
                a = cyc_v[k, pl.ds(pole * polar_count + p, 1), :].astype(jnp.float32)
                ra = rolled(a[:, :LANES], cols)
                rb = rolled(a[:, LANES:], cols)
                circ_t = jnp.concatenate(
                    [jnp.where(upper, ra, rb), jnp.where(upper, rb, ra)], axis=0
                )
                circ = jnp.transpose(circ_t).astype(jnp.bfloat16)
                g = jnp.concatenate([fields_ref[slot + p], polar_o[p]], axis=0)
                y = jnp.dot(circ, g, preferred_element_type=jnp.float32)
                f_ref[k, HALO + slot + p] = y.astype(jnp.bfloat16).astype(jnp.float32)

    @pl.when(lat == 0)
    def _():
        polar_rows(0)

    @pl.when(lat == last)
    def _():
        polar_rows(1)

    for n in (2, 3, 4, 6):
        loads[n].wait()
    base_row = lat * out_rows
    lw_all = lat_v[...].astype(jnp.float32)
    terms = []
    for i in range(out_rows):
        begin = start_s[i]
        width = width_s[i]
        row_terms = []
        for t in range(band_len):
            source = begin + t
            ok = (t < width) & (source >= 0) & (source < total_rows)
            r = jnp.clip(source - base_row + HALO, 0, ext_rows - 1)
            row_terms.append((ok, r))
        terms.append(row_terms)

    def weight(i, k, t, keep):
        ok, r = terms[i][t]
        return jnp.where(ok & keep(r), lw_all[t, k : k + 1, i : i + 1], 0.0)

    def own(r):
        return (r >= HALO) & (r < HALO + out_rows)

    for i in range(out_rows):
        for k in range(basis):
            acc = jnp.zeros((cols, chans), jnp.float32)
            for t in range(band_len):
                r = jnp.clip(terms[i][t][1], HALO, HALO + out_rows - 1)
                acc = acc + weight(i, k, t, own) * f_ref[k, r]
            acc_ref[i, k] = acc

    def finish(rows, steps, keep):
        for i in rows:
            for k in range(basis):
                acc = acc_ref[i, k]
                for t in steps(i):
                    acc = acc + weight(i, k, t, keep) * f_ref[k, terms[i][t][1]]
                h_ref[i, :, k * chans : (k + 1) * chans] = acc.astype(jnp.bfloat16)
        first, count = rows[0], len(rows)
        flat = (count * cols, chans)
        mixed = jnp.dot(
            h_ref[pl.ds(first, count)].reshape(count * cols, basis * chans), mix_ref[...],
            preferred_element_type=jnp.float32,
        )
        own_rows = fields_ref[pl.ds(first, count)].astype(jnp.float32).reshape(flat)
        out_ref[pl.ds(first, count)] = (own_rows + mixed).astype(out_ref.dtype).reshape(
            (count, cols, chans)
        )

    half = out_rows // 2

    def top_half():
        @pl.when(has_down)
        def _():
            c_up.wait_recv()
            for c in h_up:
                c.wait_recv()
            filter_halo(top_c, top_h, 0, 0)

        @pl.when(lat == 0)
        def _():
            zero_rows(0)

        finish(list(range(half)), lambda i: range(0, HALO - i), lambda r: r < HALO)

    def bottom_half():
        @pl.when(has_up)
        def _():
            c_dn.wait_recv()
            for c in h_dn:
                c.wait_recv()
            filter_halo(bot_c, bot_h, HALO, HALO + out_rows)

        @pl.when(lat == last)
        def _():
            zero_rows(HALO + out_rows)

        finish(
            list(range(half, out_rows)),
            lambda i: range(out_rows + 1 - i, band_len),
            lambda r: r >= HALO + out_rows,
        )

    far_above = lax.rem(lat, X_CHIPS) == 0

    @pl.when(jnp.logical_not(far_above))
    def _():
        top_half()
        bottom_half()

    @pl.when(far_above)
    def _():
        bottom_half()
        top_half()

    for c in h_side:
        c.wait_send()

    @pl.when(has_up)
    def _():
        c_up.wait_send()
        for c in h_up:
            c.wait_send()

    @pl.when(has_down)
    def _():
        c_dn.wait_send()
        for c in h_dn:
            c.wait_send()

    @pl.when(is_polar)
    def _():
        pol.wait_send()


def shards(fields, lon_taps, lat_taps, cycle_taps, band_start, band_width, mixing):
    row_count, col_count, chan_count = fields.shape
    basis_count = lon_taps.shape[1]
    taps_count = lon_taps.shape[2]
    reach_cells = (taps_count - 1) // 2
    band_len = lat_taps.shape[2]
    polar_rows = row_count // 2
    lat_count = lax.axis_size("lat")
    lon_count = lax.axis_size("lon")
    assert lon_count == 2 and reach_cells == HALO
    cycle_len = lon_count * col_count
    lat_pos = lax.axis_index("lat")
    ext_rows = row_count + 2 * HALO
    total_rows = lat_count * row_count

    mix_flat = mixing.reshape(basis_count * chan_count, chan_count)
    lon_t = jnp.transpose(lon_taps, (2, 1, 0))
    lat_t = jnp.transpose(lat_taps, (2, 1, 0))

    hbm = pl.BlockSpec(memory_space=pl.ANY)
    kernel = functools.partial(
        conv_kernel, basis_count, row_count, band_len, polar_rows, total_rows
    )
    halo_block = pltpu.VMEM((HALO, col_count, chan_count), fields.dtype)
    return copy_out(pl.pallas_call(
        kernel,
        out_shape=jax.ShapeDtypeStruct(fields.shape, fields.dtype),
        in_specs=[hbm] * 6 + [pl.BlockSpec(memory_space=pltpu.HBM)],
        out_specs=pl.BlockSpec(memory_space=pltpu.VMEM),
        scratch_shapes=[
            pltpu.SMEM(band_start.shape, band_start.dtype),
            pltpu.SMEM(band_width.shape, band_width.dtype),
            pltpu.VMEM(lat_t.shape, lat_t.dtype),
            pltpu.VMEM(lon_t.shape, lon_t.dtype),
            pltpu.VMEM((basis_count, ext_rows, LANES), jnp.float32),
            pltpu.VMEM(cycle_taps.shape, cycle_taps.dtype),
            pltpu.VMEM(fields.shape, fields.dtype),
            pltpu.VMEM(mix_flat.shape, mix_flat.dtype),
            halo_block,
            halo_block,
            halo_block,
            halo_block,
            pltpu.VMEM(fields.shape, fields.dtype),
            pltpu.VMEM((polar_rows, col_count, chan_count), fields.dtype),
            pltpu.VMEM((basis_count, ext_rows, col_count, chan_count), jnp.float32),
            pltpu.VMEM((row_count, basis_count, col_count, chan_count), jnp.float32),
            pltpu.VMEM((row_count, col_count, basis_count * chan_count), jnp.bfloat16),
            pltpu.VMEM((2 * HALO, basis_count * col_count, 2 * col_count), jnp.bfloat16),
            pltpu.VMEM((2 * HALO, basis_count * 16, 2 * col_count), jnp.bfloat16),
            pltpu.SemaphoreType.DMA((9,)),
            pltpu.SemaphoreType.DMA((9,)),
            pltpu.SemaphoreType.DMA((7,)),
        ],
        compiler_params=pltpu.CompilerParams(
            vmem_limit_bytes=67043328, collective_id=0, has_side_effects=True
        ),
    )(band_start, band_width, lat_t, lon_t, cycle_taps, fields, mix_flat))


def copy_out(block):
    pieces = 4
    step = block.shape[0] // pieces

    def body(src, dst, stage, sem_in, sem_out):
        ins = [
            pltpu.make_async_copy(src.at[pl.ds(n * step, step)], stage.at[pl.ds(n * step, step)], sem_in.at[n])
            for n in range(pieces)
        ]
        outs = [
            pltpu.make_async_copy(stage.at[pl.ds(n * step, step)], dst.at[pl.ds(n * step, step)], sem_out.at[n])
            for n in range(pieces)
        ]
        for c in ins:
            c.start()
        for c_in, c_out in zip(ins, outs):
            c_in.wait()
            c_out.start()
        for c in outs:
            c.wait()

    hbm = pl.BlockSpec(memory_space=pl.ANY)
    return pl.pallas_call(
        body,
        out_shape=jax.ShapeDtypeStruct(block.shape, block.dtype),
        in_specs=[hbm],
        out_specs=hbm,
        scratch_shapes=[
            pltpu.VMEM(block.shape, block.dtype),
            pltpu.SemaphoreType.DMA((pieces,)),
            pltpu.SemaphoreType.DMA((pieces,)),
        ],
    )(block)


def solution(mesh):
    in_specs = (
        P(("ens", "lat"), "lon", None),
        P(),
        P("lat", None, None),
        P(),
        P("lat"),
        P("lat"),
        P(),
    )
    out_specs = P(("ens", "lat"), "lon", None)
    return jax.shard_map(shards, mesh=mesh, in_specs=in_specs, out_specs=out_specs, check_vma=False)
```
